32 devices in a mesh: tp: 4 (over y, core), dp: 8 (over z, x).
Axes of the slice: x: 2, y: 2, z: 4, core: 2. Of those that a mesh axis runs over, the one named last changes fastest.
Arguments:
- tokens: bfloat16 [24, 1024, 768], P('dp', 'tp'), may hold values from -6 to 6
- lengths: int32 [24], P('dp'), may hold values from 196 to 1024, as said below
- ln_gain: float32 [768], replicated, may hold values from 0.1 to 1.9
- w_qkv: bfloat16 [768, 2304], P(None, 'tp'), may hold values from -0.21875 to 0.21875
- q_gain: float32 [12, 64], P('tp'), may hold values from 0.1 to 1.9
- k_gain: float32 [12, 64], P('tp'), may hold values from 0.1 to 1.9
- w_proj: bfloat16 [768, 768], P('tp'), may hold values from -1.75 to 1.75
- w_fc1: bfloat16 [768, 3072], P(None, 'tp'), may hold values from -0.21875 to 0.21875
- b_fc1: float32 [3072], P('tp'), may hold values from -3 to 3
- w_fc2: bfloat16 [3072, 768], P('tp'), may hold values from -0.109375 to 0.109375
- b_fc2: float32 [768], replicated, may hold values from -2 to 2
- d_out: bfloat16 [24, 1024, 768], P('dp', 'tp'), may hold values from -6 to 6
Outputs:
- output: bfloat16 [24, 1024, 768], P('dp', 'tp')
- d_tokens: float32 [24, 1024, 768], P('dp', 'tp')
- d_ln_gain: float32 [768], replicated
- d_qkv: float32 [768, 2304], P(None, 'tp')
- d_q_gain: float32 [12, 64], P('tp')
- d_k_gain: float32 [12, 64], P('tp')
- d_proj: float32 [768, 768], P('tp')
- d_fc1: float32 [768, 3072], P(None, 'tp')
- d_bias_one: float32 [3072], P('tp')
- d_fc2: float32 [3072, 768], P('tp')
- d_bias_two: float32 [768], replicated
The draws below stay inside these ranges and needn't reach their ends.
Inputs may be any that keep to these rules, and one draw needn't show every extreme that they name: `lengths`: each image's length is one of 196, 576 and 1024; every draw holds all three.
All inputs are finite; a program needn't handle non-finite values.
Results may differ from the reference program's by a relative error of at most 0.014.
Values may be sent and summed in bfloat16 or wider, within the bound.
No kernel may reach another device: no remote copies, remote signals or barrier semaphores. Data moves between devices by JAX's collectives and lax.ppermute only.
A program may use at most 192 MiB of HBM per device.

```python
import jax
import jax.numpy as jnp
from jax import lax

D = 768
HEADS = 12
HD = 64
FF = 3072
SEQ = 1024
IMAGES = 24


def draw_lengths(key, part):
    chosen = jax.random.randint(key, (IMAGES,), 0, 3)
    position = lax.broadcasted_iota(jnp.int32, (IMAGES,), 0)
    chosen = jnp.where(position < 3, position, chosen)
    levels = jnp.array([SEQ * 196 // 1024, SEQ * 576 // 1024, SEQ], jnp.int32)
    return jnp.take(levels, chosen).astype(jnp.int32)


def block_levels(stream_key, extent, cuts, least, high):
    def one(axis_at, parts):
        heights = jax.random.uniform(jax.random.fold_in(jax.random.fold_in(stream_key, 6), axis_at), (parts,), jnp.float32, least / len(cuts), high / len(cuts))
        return jnp.repeat(jnp.exp(heights), extent[axis_at] // parts).reshape((-1,) + (1,) * (len(extent) - axis_at - 1))

    factor_of = one(*cuts[0])
    for cut in cuts[1:]:
        factor_of = factor_of * one(*cut)
    return factor_of


def scatter_about(key, extent, width, reach, shards=(), held_as=jnp.bfloat16):
    entries = jax.random.normal(key, extent, jnp.float32) * width
    if len(shards) > 0:
        entries = block_levels(key, extent, shards, -0.22, 0.18) * entries
    return jnp.clip(entries, min=-reach, max=reach).astype(held_as)


def setup_inputs(seed: int = 0) -> dict:
    streams_of = jax.random.split(jax.random.key(seed), 13)
    return {
        "tokens": scatter_about(streams_of[0], (IMAGES, SEQ, D), 1.0, 6.0, ((0, 8), (1, 4))),
        "lengths": draw_lengths(jax.random.fold_in(streams_of[12], 71), 0),
        "ln_gain": jnp.clip(1.0 + 0.18 * jax.random.normal(streams_of[2], (D,), jnp.float32), 0.1, 1.9),
        "w_qkv": scatter_about(streams_of[3], (D, 3 * D), D ** -0.5, 0.21875, ((1, 4),)),
        "q_gain": jnp.clip(1.0 + 0.18 * jax.random.normal(streams_of[4], (HEADS, HD), jnp.float32), 0.1, 1.9),
        "k_gain": jnp.clip(1.0 + 0.18 * jax.random.normal(streams_of[5], (HEADS, HD), jnp.float32), 0.1, 1.9),
        "w_proj": scatter_about(streams_of[6], (D, D), (D // 64) ** -0.5, 1.75, ((0, 4),)),
        "w_fc1": scatter_about(streams_of[7], (D, FF), D ** -0.5, 0.21875, ((1, 4),)),
        "b_fc1": scatter_about(streams_of[8], (FF,), 0.5, 3.0, ((0, 4),), jnp.float32),
        "w_fc2": scatter_about(streams_of[9], (FF, D), FF ** -0.5, 0.109375, ((0, 4),)),
        "b_fc2": scatter_about(streams_of[10], (D,), 0.3, 2.0, (), jnp.float32),
        "d_out": scatter_about(streams_of[11], (IMAGES, SEQ, D), 1.0, 6.0, ((0, 8), (1, 4))),
    }


@jax.custom_vjp
def low(v):
    return lax.optimization_barrier(v.astype(jnp.bfloat16)).astype(jnp.float32)

@jax.custom_vjp
def low_back(v):
    return v

def low_keep(v):
    return (low(v), None)

def low_pass(kept, grad):
    return (grad,)

def back_keep(v):
    return (v, None)

def back_low(kept, grad):
    return (low(grad),)
low.defvjp(low_keep, low_pass)
low_back.defvjp(back_keep, back_low)
epsilon = 1e-06
highest = lax.Precision.HIGHEST

def layer_norm(values, scale_gain):
    average = lax.optimization_barrier(jnp.mean(values, axis=-1, keepdims=True))
    centred = values - average
    variance = lax.optimization_barrier(jnp.mean(centred * centred, axis=-1, keepdims=True))
    return centred * lax.rsqrt(variance + epsilon) * scale_gain

def image_block(inputs, weights):
    image_rows, length = inputs
    ln_gain, w_qkv, q_gain, k_gain, w_proj, w_fc1, b_fc1, w_fc2, b_fc2 = weights
    normed = low(layer_norm(image_rows, ln_gain))
    joined = low_back(jnp.dot(normed, w_qkv, precision=highest, preferred_element_type=jnp.float32))
    joined = joined.reshape(SEQ, HEADS, 3, HD)
    queries = low(layer_norm(joined[:, :, 0], q_gain))
    keys_normed = low(layer_norm(joined[:, :, 1], k_gain))
    value_rows = low(joined[:, :, 2])
    factor = HD ** (-0.5)
    scores = low_back(jnp.einsum('qhd,khd->hqk', queries, keys_normed, precision=highest) * factor)
    visible = lax.broadcasted_iota(jnp.int32, (1, 1, SEQ), 2) < length
    masked = jnp.where(visible, scores, -1e+30)
    row_peak = lax.optimization_barrier(jnp.max(masked, axis=-1, keepdims=True))
    exponent = jnp.exp(masked - row_peak)
    probability = low(exponent / lax.optimization_barrier(jnp.sum(exponent, axis=-1, keepdims=True)))
    attended = jnp.einsum('hqk,khd->qhd', probability, value_rows, precision=highest)
    attended = low(low_back(attended.reshape(SEQ, D)))
    hidden = low_back(jnp.dot(normed, w_fc1, precision=highest, preferred_element_type=jnp.float32) + b_fc1)
    active = low(jax.nn.gelu(hidden, approximate=False))
    branch = jnp.dot(attended, w_proj, precision=highest, preferred_element_type=jnp.float32)
    branch = branch + jnp.dot(active, w_fc2, precision=highest, preferred_element_type=jnp.float32)
    return image_rows + branch + b_fc2

def forward(images, lengths, weights):

    def advance(carried, inputs):
        return (carried, jax.checkpoint(image_block)(inputs, weights))
    _, outputs = lax.scan(advance, jnp.zeros((), jnp.float32), (images, lengths))
    return outputs

def reference(tokens, lengths, ln_gain, w_qkv, q_gain, k_gain, w_proj, w_fc1, b_fc1, w_fc2, b_fc2, d_out):
    floats = tuple((array.astype(jnp.float32) for array in (tokens, ln_gain, w_qkv, q_gain, k_gain, w_proj, w_fc1, b_fc1, w_fc2, b_fc2)))

    def wrapped(images, *weights):
        return forward(images, lengths, weights)
    outputs, pullback = jax.vjp(wrapped, *floats)
    gradients = pullback(d_out.astype(jnp.float32))
    return (outputs.astype(jnp.bfloat16), gradients[0], gradients[1], gradients[2], gradients[3], gradients[4], gradients[5], gradients[6], gradients[7], gradients[8], gradients[9])
```

```python
import functools
import math

import jax
import jax.numpy as jnp
from jax import lax
from jax.experimental import pallas as pl
from jax.experimental.pallas import tpu as pltpu
from jax.sharding import PartitionSpec as P


EPS = 1e-06
F32 = jnp.float32
BF16 = jnp.bfloat16
NN = (((1,), (0,)), ((), ()))
NT = (((1,), (1,)), ((), ()))
TN = (((0,), (0,)), ((), ()))
VMEM_SPEC = pl.BlockSpec(memory_space=pltpu.VMEM)
SMEM_SPEC = pl.BlockSpec(memory_space=pltpu.SMEM)


def mm(a, b, dims=NN):
    return lax.dot_general(a, b, dims, preferred_element_type=F32)


def call(kernel, outs, n_smem, *args, scratch=(), flops=0, aliases=None, name=None):
    in_specs = [SMEM_SPEC] * n_smem + [VMEM_SPEC] * (len(args) - n_smem)
    moved = sum(a.size * a.dtype.itemsize for a in args)
    moved += sum(math.prod(s) * jnp.dtype(d).itemsize for s, d in outs)
    return pl.pallas_call(
        kernel,
        out_shape=[jax.ShapeDtypeStruct(s, d) for s, d in outs],
        in_specs=in_specs,
        out_specs=[VMEM_SPEC] * len(outs),
        scratch_shapes=list(scratch),
        input_output_aliases=aliases or {},
        compiler_params=pltpu.CompilerParams(vmem_limit_bytes=60 * 1024 * 1024),
        cost_estimate=pl.CostEstimate(flops=flops, transcendentals=0, bytes_accessed=moved),
        name=name,
    )(*args)


def norm_kernel(tokens_ref, gain_ref, *out_refs):
    for i, out in enumerate(out_refs):
        v = tokens_ref[i].astype(F32)
        c = v - jnp.mean(v, axis=-1, keepdims=True)
        r = lax.rsqrt(jnp.mean(c * c, axis=-1, keepdims=True) + EPS)
        out[...] = (c * r * gain_ref[...]).astype(BF16)


def ff_kernel(first, last, blocks, *refs):
    refs = list(refs)
    take = lambda n: [refs.pop(0) for _ in range(n)]
    (pos,) = take(1)
    xs, gs = take(blocks), take(blocks)
    w1, w2, b1 = take(3)
    prior = [] if first else take(3)
    o_ff, n_ff = take(2)
    if last:
        keep1, send1, keep2, send2, small, ln_col = take(6)
    else:
        acc1, acc2, accb = take(3)
    act_s, dh_s = take(2)
    if last:
        acc1, acc2 = take(2)
    rows = xs[0].shape[0]
    bias = None
    bias_two = None
    inv_sqrt2 = 2.0**-0.5
    for k in range(blocks):
        sl = slice(k * rows, (k + 1) * rows)
        h = mm(xs[k][...], w1[...]) + b1[...]
        da = mm(gs[k][...], w2[...], NT)
        cdf = 0.5 * (1.0 + lax.erf(h * inv_sqrt2))
        pdf = jnp.exp(-0.5 * h * h) * (1.0 / math.sqrt(2.0 * math.pi))
        act = (h * cdf).astype(BF16)
        dhf = da * (cdf + h * pdf)
        dh = dhf.astype(BF16)
        act_s[sl] = act
        dh_s[sl] = dh
        part = jnp.sum(dh.astype(F32), axis=0, keepdims=True)
        bias = part if bias is None else bias + part
        o_ff[sl] = mm(act, w2[...]).astype(BF16)
        n_ff[sl] = mm(dh, w1[...], NT).astype(BF16)
    bias_two = jnp.sum(gs[0][...].astype(F32), axis=0, keepdims=True)
    t1 = t2 = None
    for k in range(blocks):
        sl = slice(k * rows, (k + 1) * rows)
        p1 = mm(xs[k][...], dh_s[sl], TN)
        p2 = mm(act_s[sl], gs[k][...], TN)
        t1 = p1 if t1 is None else t1 + p1
        t2 = p2 if t2 is None else t2 + p2
    if prior:
        t1 = t1 + prior[0][...]
        t2 = t2 + prior[1][...]
        bias = bias + prior[2][0:1]
        bias_two = bias_two + prior[2][1:2]
    both = jnp.concatenate([bias, bias_two], axis=0)
    acc1[...] = t1
    acc2[...] = t2
    if not last:
        accb[...] = both
    else:
        small[...] = both
        ln_col[...] = jnp.sum(w1[...].astype(F32) * acc1[...], axis=1, keepdims=True)
        half = acc1.shape[0] // 2
        mine = pl.multiple_of(pos[0] * half, half)
        other = pl.multiple_of((1 - pos[0]) * half, half)
        keep1[...] = acc1[pl.ds(mine, half), :]
        send1[...] = acc1[pl.ds(other, half), :].astype(BF16)
        keep2[...] = acc2[pl.ds(mine, half), :]
        send2[...] = acc2[pl.ds(other, half), :].astype(BF16)


def att_kernel(first, last, blocks, heads, size, *refs):
    refs = list(refs)
    take = lambda n: [refs.pop(0) for _ in range(n)]
    length, pos = take(2)
    xs, gs = take(blocks), take(blocks)
    wqkv, wproj, qg, kg, o_ff, n_ff = take(6)
    prior = [] if first else take(3)
    o_keep, o_send, n_keep, n_send = take(4)
    if last:
        keepq, sendq, keepp, sendp, accg, ln_row = take(6)
    else:
        accq, accp, accg = take(3)
    jt, dot_s, qs_t, q_s, k_s, kt_s, v_s, vt_s, es, dqt, dk, dv, ot, djt = take(14)
    if last:
        accq, accp = take(2)
    rows = xs[0].shape[0]
    total = rows * blocks
    scale = size**-0.5
    up = scale * math.log2(math.e)
    for k in range(blocks):
        cols = slice(k * rows, (k + 1) * rows)
        jt[:, cols] = mm(wqkv[...], xs[k][...], NT)
        dot_s[:, cols] = mm(wproj[...], gs[k][...], NT)

    def normed(u):
        c = u - jnp.mean(u, axis=0, keepdims=True)
        r = lax.rsqrt(jnp.mean(c * c, axis=0, keepdims=True) + EPS)
        return c * r, r

    ones = jnp.concatenate(
        [jnp.ones((1, rows), F32), jnp.zeros((15, rows), F32)], axis=0
    ).astype(BF16)
    for h in range(heads):
        base = h * 3 * size
        gh = slice(h * size, (h + 1) * size)
        qt = normed(jt[base : base + size])[0] * qg[gh]
        kt = normed(jt[base + size : base + 2 * size])[0] * kg[gh]
        vt = jt[base + 2 * size : base + 3 * size]
        qs_t[h] = (qt * up).astype(BF16)
        q_s[h] = qt.T.astype(BF16)
        k_s[h] = kt.T.astype(BF16)
        v_s[h] = vt.T.astype(BF16)
        for k in range(blocks):
            cols = slice(k * rows, (k + 1) * rows)
            kt_s[h, k] = kt[:, cols].astype(BF16)
            vt_s[h, k, 0:size] = vt[:, cols].astype(BF16)
            vt_s[h, k, size : size + 16] = ones

    live = length[0]
    count = (live + rows - 1) // rows

    dk[...] = jnp.zeros(dk.shape, F32)
    dv[...] = jnp.zeros(dv.shape, F32)

    def head(h, carry):
        def forward(j, acc):
            b = j ^ pos[0]
            start = pl.multiple_of(b * rows, rows)
            s = mm(k_s[h, pl.ds(start, rows), :], qs_t[h])
            slot = lax.broadcasted_iota(jnp.int32, (rows, 1), 0) + j * rows
            e = jnp.where(slot < live, jnp.exp2(s), 0.0).astype(BF16)
            es[b] = e
            return acc + mm(vt_s[h, b], e)

        acc = lax.fori_loop(0, count, forward, jnp.zeros((size + 16, total), F32))
        inv = 1.0 / acc[size : size + 1]
        o = acc[0:size] * inv
        hs = pl.ds(pl.multiple_of(h * size, size), size)
        ot[hs, :] = o.astype(BF16)
        dof = dot_s[hs, :] * inv
        dot_b = dof.astype(BF16)
        do_b = dof.T.astype(BF16)
        r = jnp.sum(dot_b.astype(F32) * o, axis=0, keepdims=True)
        q_h = q_s[h]

        def backward(j, acc):
            b = j ^ pos[0]
            start = pl.multiple_of(b * rows, rows)
            dp = mm(v_s[h, pl.ds(start, rows), :], dot_b)
            e = es[b]
            ds = (e.astype(F32) * (dp - r)).astype(BF16)
            dv[h, pl.ds(start, rows), :] = mm(e, do_b)
            dk[h, pl.ds(start, rows), :] = mm(ds, q_h)
            return acc + mm(kt_s[h, b], ds)

        dqt[h] = lax.fori_loop(0, count, backward, jnp.zeros((size, total), F32))
        return carry

    lax.fori_loop(0, heads, head, 0)

    gains = []
    for h in range(heads):
        base = h * 3 * size
        gh = slice(h * size, (h + 1) * size)
        for c, gain, grad in ((0, qg, dqt[h]), (1, kg, dk[h].T)):
            n, r = normed(jt[base + c * size : base + (c + 1) * size])
            grad = grad * scale
            y = grad * gain[gh]
            back = r * (
                y
                - jnp.mean(y, axis=0, keepdims=True)
                - n * jnp.mean(y * n, axis=0, keepdims=True)
            )
            djt[base + c * size : base + (c + 1) * size] = back.astype(BF16)
            gains.append(jnp.sum(grad * n, axis=1, keepdims=True))
        djt[base + 2 * size : base + 3 * size] = dv[h].T.astype(BF16)
    gain_col = jnp.concatenate(gains[0::2] + gains[1::2], axis=0)

    tq = tp = None
    for k in range(blocks):
        cols = slice(k * rows, (k + 1) * rows)
        p = mm(djt[:, cols], xs[k][...])
        tq = p if tq is None else tq + p
        p = mm(ot[:, cols], gs[k][...])
        tp = p if tp is None else tp + p
        n = n_ff[cols].astype(F32) + mm(djt[:, cols], wqkv[...], TN)
        o = o_ff[cols].astype(F32) + mm(ot[:, cols], wproj[...], TN)
        to_n, to_o = (n_keep, o_keep) if k % 2 == 0 else (n_send, o_send)
        at = slice(k // 2 * rows, (k // 2 + 1) * rows)
        to_n[at] = n.astype(BF16)
        to_o[at] = o.astype(BF16)
    if prior:
        tq = tq + prior[0][...]
        tp = tp + prior[1][...]
        gain_col = gain_col + prior[2][...]
    accg[...] = gain_col
    if not last:
        accq[...] = tq
        accp[...] = tp
    else:
        ln_row[...] = jnp.sum(wqkv[...].astype(F32) * tq, axis=0, keepdims=True)
        accq[...] = tq.T
        accp[...] = tp
        for acc, keep, send in ((accq, keepq, sendq), (accp, keepp, sendp)):
            half = acc.shape[0] // 2
            mine = pl.multiple_of(pos[1] * half, half)
            other = pl.multiple_of((1 - pos[1]) * half, half)
            keep[...] = acc[pl.ds(mine, half), :]
            send[...] = acc[pl.ds(other, half), :].astype(BF16)


def final_kernel(images, *refs):
    tokens, d_out, gain, bias = refs[:4]
    ins = refs[4 : 4 + 4 * images]
    out, d_tokens = refs[4 + 4 * images :]
    for i in range(images):
        oa, ob, na, nb = ins[4 * i : 4 * i + 4]
        v = tokens[i].astype(F32)
        c = v - jnp.mean(v, axis=-1, keepdims=True)
        r = lax.rsqrt(jnp.mean(c * c, axis=-1, keepdims=True) + EPS)
        xhat = c * r
        branch = oa[...].astype(F32) + ob[...].astype(F32)
        out[i] = (v + branch + bias[...]).astype(BF16)
        z = (na[...].astype(F32) + nb[...].astype(F32)) * gain[...]
        back = r * (
            z
            - jnp.mean(z, axis=-1, keepdims=True)
            - xhat * jnp.mean(z * xhat, axis=-1, keepdims=True)
        )
        d_tokens[i] = d_out[i].astype(F32) + back


def join_kernel(parts, cols, *refs):
    pos, refs = refs[0], refs[1:]
    outs = refs[-len(cols) :]
    n = parts // 2
    for a, out in enumerate(outs):
        for s in range(2):
            for k in range(n):
                at = (pos[0] ^ s) * n + (pos[1] ^ k)
                out[at] = refs[(a * 2 + s) * n + k][...].astype(F32)


def shards(dp_size, tp_size, *args):
    (tokens, lengths, ln_gain, w_qkv, q_gain, k_gain, w_proj, w_fc1, b_fc1, w_fc2, b_fc2, d_out) = args
    images, rows, width = tokens.shape
    heads, size = q_gain.shape
    hidden = w_fc1.shape[1]
    total = rows * tp_size
    blocks = tp_size
    t = lax.axis_index("tp").astype(jnp.int32)
    d = lax.axis_index("dp").astype(jnp.int32)

    def swap(v, axis, mask):
        n = tp_size if axis == "tp" else dp_size
        return lax.ppermute(v, axis, [(i, i ^ mask) for i in range(n)])

    normed = call(norm_kernel, [((rows, width), BF16)] * images, 0, tokens, ln_gain[None, :], name="norm")

    def gather(v):
        far = swap(v, "tp", 2)
        return [v, swap(v, "tp", 1), far, swap(far, "tp", 1)]

    gs, xs = [], []
    for i in range(images):
        gs.append(gather(d_out[i]))
        xs.append(gather(normed[i]))

    x_bit = (d & 1)[None]
    ff_pos = x_bit
    b1 = b_fc1[None, :]
    wide = (total, width)
    o_ff, n_ff = [], []
    state = []
    for i in range(images):
        first, last = i == 0, i == images - 1
        outs = [(wide, BF16), (wide, BF16)]
        scratch = [pltpu.VMEM((total, hidden), BF16)] * 2
        if last:
            outs += [((width // 2, hidden), F32), ((width // 2, hidden), BF16)]
            outs += [((hidden // 2, width), F32), ((hidden // 2, width), BF16)]
            outs += [((2, width), F32), ((width, 1), F32)]
            scratch += [pltpu.VMEM((width, hidden), F32), pltpu.VMEM((hidden, width), F32)]
        else:
            outs += [((width, hidden), F32), ((hidden, width), F32), ((2, width), F32)]
        res = call(
            functools.partial(ff_kernel, first, last, blocks), outs, 1,
            ff_pos, *xs[i], *gs[i], w_fc1, w_fc2, b1, *state,
            scratch=scratch, flops=12 * total * width * hidden, name=f"ff{i}",
        )
        o_ff.append(res[0])
        n_ff.append(res[1])
        state = res[2:]
    keep1, send1, keep2, send2, small, ln_ff = state

    def reduce_weight(keep, send):
        half = keep + swap(send, "dp", 1).astype(F32)
        n = dp_size // 2
        z = d >> 1
        step = half.shape[0] // n
        piece = lambda k: lax.dynamic_slice_in_dim(half, (z ^ k) * step, step, 0)
        done = piece(0)
        for k in range(1, n):
            done = done + swap(piece(k).astype(BF16), "dp", 2 * k).astype(F32)
        done = done.astype(BF16)
        near = [done] + [swap(done, "dp", 2 * k) for k in range(1, n)]
        return near + [swap(v, "dp", 1) for v in near]

    def join(parts_list):
        outs, flat = [], []
        for parts in parts_list:
            outs.append(((dp_size,) + parts[0].shape, F32))
            flat += parts
        where = jnp.stack([d & 1, d >> 1])
        got = call(
            functools.partial(join_kernel, dp_size, [o[0] for o in outs]), outs, 1, where, *flat, name="join"
        )
        return [g.reshape(-1, g.shape[-1]) for g in got]

    def small_sum(v, axis):
        n = tp_size if axis == "tp" else dp_size
        mask = 1
        while mask < n:
            v = v + swap(v, axis, mask)
            mask *= 2
        return v

    red1 = reduce_weight(keep1, send1)
    red2 = reduce_weight(keep2, send2)
    small = small_sum(small, "dp")
    d_bias_one = small[0]
    d_bias_two = small_sum(small[1:2], "tp")[0]

    qg = q_gain.reshape(-1, 1)
    kg = k_gain.reshape(-1, 1)
    w_t = w_qkv.T
    joined = heads * 3 * size
    inner = heads * size
    att_pos = jnp.stack([t, d & 1])
    state = []
    fin = []
    for i in range(images):
        first, last = i == 0, i == images - 1
        outs = [((total // 2, width), BF16)] * 4
        scratch = [
            pltpu.VMEM((joined, total), F32),
            pltpu.VMEM((inner, total), F32),
            pltpu.VMEM((heads, size, total), BF16),
            pltpu.VMEM((heads, total, size), BF16),
            pltpu.VMEM((heads, total, size), BF16),
            pltpu.VMEM((heads, blocks, size, rows), BF16),
            pltpu.VMEM((heads, total, size), BF16),
            pltpu.VMEM((heads, blocks, size + 16, rows), BF16),
            pltpu.VMEM((blocks, rows, total), BF16),
            pltpu.VMEM((heads, size, total), F32),
            pltpu.VMEM((heads, total, size), F32),
            pltpu.VMEM((heads, total, size), F32),
            pltpu.VMEM((inner, total), BF16),
            pltpu.VMEM((joined, total), BF16),
        ]
        if last:
            outs += [((width // 2, joined), F32), ((width // 2, joined), BF16)]
            outs += [((inner // 2, width), F32), ((inner // 2, width), BF16)]
            outs += [((2 * inner, 1), F32), ((1, width), F32)]
            scratch += [pltpu.VMEM((width, joined), F32), pltpu.VMEM((inner, width), F32)]
        else:
            outs += [((joined, width), F32), ((inner, width), F32), ((2 * inner, 1), F32)]
        res = call(
            functools.partial(att_kernel, first, last, blocks, heads, size), outs, 2,
            lengths[i : i + 1], att_pos, *xs[i], *gs[i], w_t, w_proj, qg, kg, o_ff[i], n_ff[i], *state,
            scratch=scratch,
            flops=6 * 8 * heads * total * total * size + 8 * total * width * (joined + inner),
            name=f"att{i}",
        )
        o_keep, o_send, n_keep, n_send = res[:4]
        state = res[4:]
        for keep, send in ((o_keep, o_send), (n_keep, n_send)):
            both = (keep.astype(F32) + swap(send, "tp", 1).astype(F32)).astype(BF16)
            fin += [both[:rows], swap(both[rows:], "tp", 2)]
    keepq, sendq, keepp, sendp, gain_col, ln_att = state
    redq = reduce_weight(keepq, sendq)
    redp = reduce_weight(keepp, sendp)
    pad = jnp.zeros((1, width - 2 * inner), F32)
    late = jnp.concatenate(
        [jnp.concatenate([gain_col.reshape(1, -1), pad], axis=1), ln_att + ln_ff.reshape(1, -1)], axis=0
    )
    late = small_sum(late, "dp")
    d_q_gain = late[0, :inner].reshape(heads, size)
    d_k_gain = late[0, inner : 2 * inner].reshape(heads, size)
    d_ln_gain = small_sum(late[1:2], "tp")[0] / ln_gain

    d_fc1, d_fc2 = join([red1, red2])
    d_qkv, d_proj = join([redq, redp])
    output, d_tokens = call(
        functools.partial(final_kernel, images),
        [((images, rows, width), BF16), ((images, rows, width), F32)], 0,
        tokens, d_out, ln_gain[None, :], b_fc2[None, :], *fin, name="final",
    )
    return (output, d_tokens, d_ln_gain, d_qkv, d_q_gain, d_k_gain, d_proj, d_fc1, d_bias_one, d_fc2, d_bias_two)


def solution(mesh):
    rows = P("dp", "tp", None)
    wide = P(None, "tp")
    tall = P("tp", None)
    return jax.shard_map(
        functools.partial(shards, mesh.shape["dp"], mesh.shape["tp"]),
        mesh=mesh,
        in_specs=(rows, P("dp"), P(), wide, tall, tall, tall, wide, P("tp"), tall, P(), rows),
        out_specs=(rows, rows, P(), wide, tall, tall, tall, wide, P("tp"), tall, P()),
        check_vma=False,
    )
```

```python
import functools
import math

import jax
import jax.numpy as jnp
from jax import lax
from jax.experimental import pallas as pl
from jax.experimental.pallas import tpu as pltpu
from jax.sharding import PartitionSpec as P


EPS = 1e-06
F32 = jnp.float32
BF16 = jnp.bfloat16
NN = (((1,), (0,)), ((), ()))
NT = (((1,), (1,)), ((), ()))
TN = (((0,), (0,)), ((), ()))
VMEM_SPEC = pl.BlockSpec(memory_space=pltpu.VMEM)
SMEM_SPEC = pl.BlockSpec(memory_space=pltpu.SMEM)


def mm(a, b, dims=NN):
    return lax.dot_general(a, b, dims, preferred_element_type=F32)


def call(kernel, outs, n_smem, *args, scratch=(), flops=0, aliases=None):
    in_specs = [SMEM_SPEC] * n_smem + [VMEM_SPEC] * (len(args) - n_smem)
    moved = sum(a.size * a.dtype.itemsize for a in args)
    moved += sum(math.prod(s) * jnp.dtype(d).itemsize for s, d in outs)
    return pl.pallas_call(
        kernel,
        out_shape=[jax.ShapeDtypeStruct(s, d) for s, d in outs],
        in_specs=in_specs,
        out_specs=[VMEM_SPEC] * len(outs),
        scratch_shapes=list(scratch),
        input_output_aliases=aliases or {},
        compiler_params=pltpu.CompilerParams(vmem_limit_bytes=60 * 1024 * 1024),
        cost_estimate=pl.CostEstimate(flops=flops, transcendentals=0, bytes_accessed=moved),
    )(*args)


def norm_kernel(tokens_ref, d_out_ref, gain_ref, *out_refs):
    rows = tokens_ref.shape[1]
    for i, out in enumerate(out_refs):
        v = tokens_ref[i].astype(F32)
        c = v - jnp.mean(v, axis=-1, keepdims=True)
        r = lax.rsqrt(jnp.mean(c * c, axis=-1, keepdims=True) + EPS)
        out[0:rows] = (c * r * gain_ref[...]).astype(BF16)
        out[rows : 2 * rows] = d_out_ref[i]


def emit_pieces(acc, pos, keep_a, send_a, keep_b, *send_b):
    third = acc.shape[0] // 3
    half, step = third, keep_b.shape[0]
    keep_a[...] = acc[pl.ds(pl.multiple_of(pos[0] * half, half), half), :]
    send_a[...] = acc[pl.ds(pl.multiple_of((1 - pos[0]) * half, half), half), :].astype(BF16)
    for k, out in enumerate((keep_b,) + send_b):
        at = pl.multiple_of(2 * third + (pos[1] ^ k) * step, step)
        out[...] = acc[pl.ds(at, step), :].astype(out.dtype)


def ff_kernel(first, last, blocks, owned, *refs):
    refs = list(refs)
    take = lambda n: [refs.pop(0) for _ in range(n)]
    (pos,) = take(1)
    packs = take(blocks)
    w1, w2, b1 = take(3)
    prior = [] if first else take(2)
    o_ff, n_ff = take(blocks // 2), take(blocks // 2)
    if last:
        n_pieces = len(refs) - 5
        pieces = take(n_pieces)
        small, ln_col = take(2)
    else:
        acc, accb = take(2)
    act_s, dh_s = take(2)
    if last:
        (acc,) = take(1)
    rows = packs[0].shape[0] // 2
    width = w1.shape[0]
    xs = [p.at[0:rows] for p in packs]
    gs = [p.at[rows : 2 * rows] for p in packs]
    bias = None
    inv_sqrt2 = 2.0**-0.5
    for k in range(blocks):
        sl = slice(k * rows, (k + 1) * rows)
        at = slice((k % 2) * rows, (k % 2 + 1) * rows)
        h = mm(xs[k][...], w1[...]) + b1[...]
        da = mm(gs[k][...], w2[...], NT)
        cdf = 0.5 * (1.0 + lax.erf(h * inv_sqrt2))
        pdf = jnp.exp(-0.5 * h * h) * (1.0 / math.sqrt(2.0 * math.pi))
        act = (h * cdf).astype(BF16)
        dh = (da * (cdf + h * pdf)).astype(BF16)
        act_s[sl] = act
        dh_s[sl] = dh
        part = jnp.sum(dh.astype(F32), axis=0, keepdims=True)
        bias = part if bias is None else bias + part
        o_ff[k // 2][at] = mm(act, w2[...]).astype(BF16)
        n_ff[k // 2][at] = mm(dh, w1[...], NT).astype(BF16)
    bias_two = jnp.zeros_like(bias)
    for k in owned:
        bias_two = bias_two + jnp.sum(gs[k][...].astype(F32), axis=0, keepdims=True)
    t1 = t2 = None
    for k in range(blocks):
        sl = slice(k * rows, (k + 1) * rows)
        p1 = mm(xs[k][...], dh_s[sl], TN)
        p2 = mm(act_s[sl], gs[k][...], TN)
        t1 = p1 if t1 is None else t1 + p1
        t2 = p2 if t2 is None else t2 + p2
    if prior:
        t1 = t1 + prior[0][0:width]
        t2 = t2 + prior[0][width:]
        bias = bias + prior[1][0:1]
        bias_two = bias_two + prior[1][1:2]
    both = jnp.concatenate([bias, bias_two], axis=0)
    acc[0:width] = t1
    acc[width:] = t2
    if not last:
        accb[...] = both
    else:
        small[...] = both
        ln_col[...] = jnp.sum(w1[...].astype(F32) * acc[0:width], axis=1, keepdims=True)
        emit_pieces(acc, pos, *pieces)


def att_kernel(first, last, blocks, heads, size, *refs):
    refs = list(refs)
    take = lambda n: [refs.pop(0) for _ in range(n)]
    length, pos = take(2)
    packs = take(blocks)
    wqkv, wproj, qg, kg = take(4)
    o_ff, n_ff = take(2), take(2)
    prior = [] if first else take(2)
    keep_near, keep_far, send = take(3)
    if last:
        pieces = take(len(refs) - 17)
        accg, ln_row = take(2)
    else:
        acc, accg = take(2)
    jt, dot_s, qs_t, q_s, k_s, kt_s, v_s, vt_s, es, dqt, dk, dv, ot, djt = take(14)
    if last:
        (acc,) = take(1)
    rows = packs[0].shape[0] // 2
    xs = [p.at[0:rows] for p in packs]
    gs = [p.at[rows : 2 * rows] for p in packs]
    joined = wqkv.shape[0]
    total = rows * blocks
    scale = size**-0.5
    up = scale * math.log2(math.e)
    for k in range(blocks):
        cols = slice(k * rows, (k + 1) * rows)
        jt[:, cols] = mm(wqkv[...], xs[k][...], NT)
        dot_s[:, cols] = mm(wproj[...], gs[k][...], NT)

    def normed(u):
        c = u - jnp.mean(u, axis=0, keepdims=True)
        r = lax.rsqrt(jnp.mean(c * c, axis=0, keepdims=True) + EPS)
        return c * r, r

    ones = jnp.concatenate(
        [jnp.ones((1, rows), F32), jnp.zeros((15, rows), F32)], axis=0
    ).astype(BF16)
    for h in range(heads):
        base = h * 3 * size
        gh = slice(h * size, (h + 1) * size)
        qt = normed(jt[base : base + size])[0] * qg[gh]
        kt = normed(jt[base + size : base + 2 * size])[0] * kg[gh]
        vt = jt[base + 2 * size : base + 3 * size]
        qs_t[h] = (qt * up).astype(BF16)
        q_s[h] = qt.T.astype(BF16)
        k_s[h] = kt.T.astype(BF16)
        v_s[h] = vt.T.astype(BF16)
        for k in range(blocks):
            cols = slice(k * rows, (k + 1) * rows)
            kt_s[h, k] = kt[:, cols].astype(BF16)
            vt_s[h, k, 0:size] = vt[:, cols].astype(BF16)
            vt_s[h, k, size : size + 16] = ones

    live = length[0]
    count = (live + rows - 1) // rows

    dk[...] = jnp.zeros(dk.shape, F32)
    dv[...] = jnp.zeros(dv.shape, F32)

    def head(h, carry):
        def forward(j, acc):
            b = j ^ pos[0]
            start = pl.multiple_of(b * rows, rows)
            s = mm(k_s[h, pl.ds(start, rows), :], qs_t[h])
            slot = lax.broadcasted_iota(jnp.int32, (rows, 1), 0) + j * rows
            e = jnp.where(slot < live, jnp.exp2(s), 0.0).astype(BF16)
            es[b] = e
            return acc + mm(vt_s[h, b], e)

        acc = lax.fori_loop(0, count, forward, jnp.zeros((size + 16, total), F32))
        inv = 1.0 / acc[size : size + 1]
        o = acc[0:size] * inv
        hs = pl.ds(pl.multiple_of(h * size, size), size)
        ot[hs, :] = o.astype(BF16)
        dof = dot_s[hs, :] * inv
        dot_b = dof.astype(BF16)
        do_b = dof.T.astype(BF16)
        r = jnp.sum(dot_b.astype(F32) * o, axis=0, keepdims=True)
        q_h = q_s[h]

        def backward(j, acc):
            b = j ^ pos[0]
            start = pl.multiple_of(b * rows, rows)
            dp = mm(v_s[h, pl.ds(start, rows), :], dot_b)
            e = es[b]
            ds = (e.astype(F32) * (dp - r)).astype(BF16)
            dv[h, pl.ds(start, rows), :] = mm(e, do_b)
            dk[h, pl.ds(start, rows), :] = mm(ds, q_h)
            return acc + mm(kt_s[h, b], ds)

        dqt[h] = lax.fori_loop(0, count, backward, jnp.zeros((size, total), F32))
        return carry

    lax.fori_loop(0, heads, head, 0)

    gains = []
    for h in range(heads):
        base = h * 3 * size
        gh = slice(h * size, (h + 1) * size)
        for c, gain, grad in ((0, qg, dqt[h]), (1, kg, dk[h].T)):
            n, r = normed(jt[base + c * size : base + (c + 1) * size])
            grad = grad * scale
            y = grad * gain[gh]
            back = r * (
                y
                - jnp.mean(y, axis=0, keepdims=True)
                - n * jnp.mean(y * n, axis=0, keepdims=True)
            )
            djt[base + c * size : base + (c + 1) * size] = back.astype(BF16)
            gains.append(jnp.sum(grad * n, axis=1, keepdims=True))
        djt[base + 2 * size : base + 3 * size] = dv[h].T.astype(BF16)
    gain_col = jnp.concatenate(gains[0::2] + gains[1::2], axis=0)

    tq = tp = None
    for k in range(blocks):
        cols = slice(k * rows, (k + 1) * rows)
        p = mm(djt[:, cols], xs[k][...])
        tq = p if tq is None else tq + p
        p = mm(ot[:, cols], gs[k][...])
        tp = p if tp is None else tp + p
        part = slice((k % 2) * rows, (k % 2 + 1) * rows)
        n = n_ff[k // 2][part].astype(F32) + mm(djt[:, cols], wqkv[...], TN)
        o = o_ff[k // 2][part].astype(F32) + mm(ot[:, cols], wproj[...], TN)
        if k % 2 == 0:
            out, base = (keep_near, keep_far)[k // 2], 0
        else:
            out, base = send, (k // 2) * 2 * rows
        out[base : base + rows] = o.astype(BF16)
        out[base + rows : base + 2 * rows] = n.astype(BF16)
    if prior:
        tq = tq + prior[0][0:joined]
        tp = tp + prior[0][joined:]
        gain_col = gain_col + prior[1][...]
    accg[...] = gain_col
    acc[0:joined] = tq
    acc[joined:] = tp
    if last:
        ln_row[...] = jnp.sum(wqkv[...].astype(F32) * tq, axis=0, keepdims=True)
        emit_pieces(acc, pos.at[1:3], *pieces)


def final_kernel(images, *refs):
    tokens, d_out, gain, bias = refs[:4]
    ins = refs[4 : 4 + 3 * images]
    out, d_tokens = refs[4 + 3 * images :]
    rows = tokens.shape[1]
    for i in range(images):
        keep, near, far = ins[3 * i : 3 * i + 3]
        both = [
            keep[at].astype(F32) + near[at].astype(F32) + far[at].astype(F32)
            for at in (slice(0, rows), slice(rows, 2 * rows))
        ]
        v = tokens[i].astype(F32)
        c = v - jnp.mean(v, axis=-1, keepdims=True)
        r = lax.rsqrt(jnp.mean(c * c, axis=-1, keepdims=True) + EPS)
        xhat = c * r
        out[i] = (v + both[0] + bias[...]).astype(BF16)
        z = both[1] * gain[...]
        back = r * (
            z
            - jnp.mean(z, axis=-1, keepdims=True)
            - xhat * jnp.mean(z * xhat, axis=-1, keepdims=True)
        )
        d_tokens[i] = d_out[i].astype(F32) + back


def join_kernel(n, flip, *refs):
    pos, own, far, pairs = refs[0], refs[1 : 1 + n], refs[1 + n], refs[2 + n : 2 + 2 * n]
    one, two, whole = refs[2 + 2 * n :]
    step = own[0].shape[0]
    third = step * n
    for k in range(n):
        z = pos[1] ^ k
        at = pl.multiple_of(pos[0] * third + z * step, step)
        whole[pl.ds(at, step), :] = own[k][...].astype(F32)
        at = pl.multiple_of((1 - pos[0]) * third + z * step, step)
        whole[pl.ds(at, step), :] = far[k * step : (k + 1) * step].astype(F32)
        half = step // 2
        for s in range(2):
            at = pl.multiple_of(2 * third + z * step + (pos[0] ^ s) * half, half)
            whole[pl.ds(at, half), :] = pairs[k][s * half : (s + 1) * half].astype(F32)
    cut = one.shape[1] if flip else one.shape[0]
    one[...] = whole[0:cut].T if flip else whole[0:cut]
    two[...] = whole[cut:]


def block(dp_size, tp_size, *args):
    (tokens, lengths, ln_gain, w_qkv, q_gain, k_gain, w_proj, w_fc1, b_fc1, w_fc2, b_fc2, d_out) = args
    images, rows, width = tokens.shape
    heads, size = q_gain.shape
    hidden = w_fc1.shape[1]
    total = rows * tp_size
    blocks = tp_size
    joined = heads * 3 * size
    inner = heads * size
    n = dp_size // 2
    t = lax.axis_index("tp").astype(jnp.int32)
    d = lax.axis_index("dp").astype(jnp.int32)
    x, z = d & 1, d >> 1

    def swap(v, axis, mask):
        count = tp_size if axis == "tp" else dp_size
        return lax.ppermute(v, axis, [(i, i ^ mask) for i in range(count)])

    def after(v, dep):
        return lax.optimization_barrier((v, dep))[0]

    own = call(norm_kernel, [((2 * rows, width), BF16)] * images, 0, tokens, d_out, ln_gain[None, :])
    far = [swap(v, "tp", 2) for v in own]
    near = [swap(v, "tp", 1) for v in own]
    cross = [None] * images

    def forward(i, dep):
        cross[i] = swap(after(far[i], dep), "tp", 1)

    b1 = b_fc1[None, :]
    pos = jnp.stack([x, z])

    def pieces_of(third, columns):
        step = third // n
        return [((third, columns), F32), ((third, columns), BF16), ((step, columns), F32)] + [
            ((step, columns), BF16)
        ] * (n - 1)

    ff_pieces = pieces_of((width + hidden) // 3, width)
    qp_pieces = pieces_of((joined + inner) // 3, width)

    def ff(first, last, packs, owned, state):
        count = len(packs)
        outs = [((2 * rows, width), BF16)] * count
        scratch = [pltpu.VMEM((count * rows, hidden), BF16)] * 2
        if last:
            outs += ff_pieces + [((2, width), F32), ((width, 1), F32)]
            scratch += [pltpu.VMEM((width + hidden, width), F32)]
        else:
            outs += [((width + hidden, width), F32), ((2, width), F32)]
        res = call(
            functools.partial(ff_kernel, first, last, count, owned), outs, 1,
            pos, *packs, w_fc1, w_fc2, b1, *state,
            scratch=scratch, flops=12 * count * rows * width * hidden,
        )
        half = count // 2
        return res[:half], res[half:count], res[count:]

    qg = q_gain.reshape(-1, 1)
    kg = k_gain.reshape(-1, 1)
    w_t = w_qkv.T
    att_pos = jnp.stack([t, x, z])
    keeps = []

    def att(i, o_ff, n_ff, state):
        first, last = i == 0, i == images - 1
        outs = [((2 * rows, width), BF16)] * 2 + [((4 * rows, width), BF16)]
        scratch = [
            pltpu.VMEM((joined, total), F32),
            pltpu.VMEM((inner, total), F32),
            pltpu.VMEM((heads, size, total), BF16),
            pltpu.VMEM((heads, total, size), BF16),
            pltpu.VMEM((heads, total, size), BF16),
            pltpu.VMEM((heads, blocks, size, rows), BF16),
            pltpu.VMEM((heads, total, size), BF16),
            pltpu.VMEM((heads, blocks, size + 16, rows), BF16),
            pltpu.VMEM((blocks, rows, total), BF16),
            pltpu.VMEM((heads, size, total), F32),
            pltpu.VMEM((heads, total, size), F32),
            pltpu.VMEM((heads, total, size), F32),
            pltpu.VMEM((inner, total), BF16),
            pltpu.VMEM((joined, total), BF16),
        ]
        if last:
            outs += qp_pieces + [((2 * inner, 1), F32), ((1, width), F32)]
            scratch += [pltpu.VMEM((joined + inner, width), F32)]
        else:
            outs += [((joined + inner, width), F32), ((2 * inner, 1), F32)]
        res = call(
            functools.partial(att_kernel, first, last, blocks, heads, size), outs, 2,
            lengths[i : i + 1], att_pos, own[i], near[i], far[i], cross[i],
            w_t, w_proj, qg, kg, *o_ff, *n_ff, *state,
            scratch=scratch,
            flops=6 * 8 * heads * total * total * size + 8 * total * width * (joined + inner),
        )
        keep_near, keep_far, send = res[:3]
        got = swap(send, "tp", 1)
        summed = (keep_far.astype(F32) + got[2 * rows :].astype(F32)).astype(BF16)
        keeps.extend([keep_near, got, swap(summed, "tp", 2)])
        return res[3:]

    def reduce_weight(keep_a, send_a, keep_b, *send_b):
        half = keep_a + swap(send_a, "dp", 1).astype(F32)
        done_b = keep_b
        for k in range(1, n):
            done_b = done_b + swap(send_b[k - 1], "dp", 2 * k).astype(F32)
        step = keep_b.shape[0]
        piece = lambda k: lax.dynamic_slice_in_dim(half, (z ^ k) * step, step, 0)
        cut = step // 2
        done_a = piece(0)
        for k in range(1, n):
            done_a = done_a + swap(piece(k).astype(BF16), "dp", 2 * k).astype(F32)
        done_a = done_a.astype(BF16)
        sent = lax.dynamic_slice_in_dim(done_b, (1 - x) * cut, cut, 0).astype(BF16)
        done_b = lax.dynamic_slice_in_dim(done_b, x * cut, cut, 0) + swap(sent, "dp", 1).astype(F32)
        done_b = done_b.astype(BF16)
        pair = jnp.concatenate([done_b, swap(done_b, "dp", 1)], axis=0)
        near_a = [done_a] + [swap(done_a, "dp", 2 * k) for k in range(1, n)]
        pairs = [pair] + [swap(pair, "dp", 2 * k) for k in range(1, n)]
        far_a = swap(jnp.concatenate(near_a, axis=0), "dp", 1)
        return near_a + [far_a] + pairs

    def join(parts, shapes, flip):
        return call(
            functools.partial(join_kernel, n, flip), [(s, F32) for s in shapes], 1, pos, *parts,
            scratch=[pltpu.VMEM((3 * n * parts[0].shape[0], width), F32)],
        )

    def small_sum(v, axis):
        count = tp_size if axis == "tp" else dp_size
        mask = 1
        while mask < count:
            v = v + swap(v, axis, mask)
            mask *= 2
        return v

    oa, na, state = ff(True, False, [b for i in range(images) for b in (own[i], near[i])], tuple(range(0, 2 * images, 2)), [])
    forward(0, oa[0])
    ob, nb, state = ff(False, False, [far[0], cross[0]], (), state)
    forward(1, ob[0])
    att_state = att(0, [oa[0], ob[0]], [na[0], nb[0]], [])
    for i in range(2, images):
        forward(i, att_state[1])
    oc, nc, state = ff(False, True, [b for i in range(1, images) for b in (far[i], cross[i])], (), state)
    *ff_out, small, ln_ff = state
    fc_parts = reduce_weight(*ff_out)
    for i in range(1, images):
        att_state = att(i, [oa[i], oc[i - 1]], [na[i], nc[i - 1]], att_state)
    *qp_out, gain_col, ln_att = att_state
    qp_parts = reduce_weight(*qp_out)
    pad = jnp.zeros((1, width - 2 * inner), F32)
    late = jnp.concatenate(
        [
            jnp.concatenate([gain_col.reshape(1, -1), pad], axis=1),
            small[0:1],
            small[1:2],
            ln_att + ln_ff.reshape(1, -1),
        ],
        axis=0,
    )
    late = small_sum(late, "dp")
    d_q_gain = late[0, :inner].reshape(heads, size)
    d_k_gain = late[0, inner : 2 * inner].reshape(heads, size)
    d_bias_one = late[1]
    both = small_sum(late[2:4], "tp")
    d_bias_two = both[0]
    d_ln_gain = both[1] / ln_gain

    d_fc1, d_fc2 = join(fc_parts, [(width, hidden), (hidden, width)], False)
    d_qkv, d_proj = join(qp_parts, [(width, joined), (inner, width)], True)
    output, d_tokens = call(
        functools.partial(final_kernel, images),
        [((images, rows, width), BF16), ((images, rows, width), F32)], 0,
        tokens, d_out, ln_gain[None, :], b_fc2[None, :], *keeps,
    )
    return (output, d_tokens, d_ln_gain, d_qkv, d_q_gain, d_k_gain, d_proj, d_fc1, d_bias_one, d_fc2, d_bias_two)


def solution(mesh):
    rows = P("dp", "tp", None)
    wide = P(None, "tp")
    tall = P("tp", None)
    return jax.shard_map(
        functools.partial(block, mesh.shape["dp"], mesh.shape["tp"]),
        mesh=mesh,
        in_specs=(rows, P("dp"), P(), wide, tall, tall, tall, wide, P("tp"), tall, P(), rows),
        out_specs=(rows, rows, P(), wide, tall, tall, tall, wide, P("tp"), tall, P()),
        check_vma=False,
    )
```

```python
import functools
import math

import jax
import jax.numpy as jnp
from jax import lax
from jax.experimental import pallas as pl
from jax.experimental.pallas import tpu as pltpu
from jax.sharding import PartitionSpec as P


EPS = 1e-06
F32 = jnp.float32
BF16 = jnp.bfloat16
NN = (((1,), (0,)), ((), ()))
NT = (((1,), (1,)), ((), ()))
TN = (((0,), (0,)), ((), ()))
VMEM_SPEC = pl.BlockSpec(memory_space=pltpu.VMEM)
ANY_SPEC = pl.BlockSpec(memory_space=pl.ANY)
SMEM_SPEC = pl.BlockSpec(memory_space=pltpu.SMEM)


def mm(a, b, dims=NN):
    return lax.dot_general(a, b, dims, preferred_element_type=F32)


def call(kernel, outs, n_smem, *args, n_any=0, scratch=(), flops=0):
    in_specs = [SMEM_SPEC] * n_smem + [ANY_SPEC] * n_any + [VMEM_SPEC] * (len(args) - n_smem - n_any)
    moved = sum(a.size * a.dtype.itemsize for a in args)
    moved += sum(math.prod(s) * jnp.dtype(d).itemsize for s, d in outs)
    return pl.pallas_call(
        kernel,
        out_shape=[jax.ShapeDtypeStruct(s, d) for s, d in outs],
        in_specs=in_specs,
        out_specs=[VMEM_SPEC] * len(outs),
        scratch_shapes=list(scratch),
        compiler_params=pltpu.CompilerParams(vmem_limit_bytes=60 * 1024 * 1024),
        cost_estimate=pl.CostEstimate(flops=flops, transcendentals=0, bytes_accessed=moved),
    )(*args)


def norm_kernel(tokens_ref, d_out_ref, gain_ref, *out_refs):
    rows = tokens_ref.shape[1]
    for i, out in enumerate(out_refs):
        v = tokens_ref[i].astype(F32)
        c = v - jnp.mean(v, axis=-1, keepdims=True)
        r = lax.rsqrt(jnp.mean(c * c, axis=-1, keepdims=True) + EPS)
        out[0:rows] = (c * r * gain_ref[...].reshape(1, -1)).astype(BF16)
        out[rows : 2 * rows] = d_out_ref[i]


def emit_pieces(acc, pos, keep_a, send_a, keep_b, *send_b):
    third = acc.shape[0] // 3
    half, step = third, keep_b.shape[0]
    keep_a[...] = acc[pl.ds(pl.multiple_of(pos[0] * half, half), half), :]
    send_a[...] = acc[pl.ds(pl.multiple_of((1 - pos[0]) * half, half), half), :].astype(BF16)
    for k, out in enumerate((keep_b,) + send_b):
        at = pl.multiple_of(2 * third + (pos[1] ^ k) * step, step)
        out[...] = acc[pl.ds(at, step), :].astype(out.dtype)


def ff_kernel(first, last, blocks, owned, *refs):
    refs = list(refs)
    take = lambda n: [refs.pop(0) for _ in range(n)]
    packs = take(blocks)
    prior = [] if first else take(1)
    w1, w2, b1 = take(3)
    prior_bias = [] if first else take(1)
    o_ff, n_ff = take(2)
    if last:
        summed, accb, ln_col = take(3)
    else:
        acc, accb = take(2)
    buf, sem, prior_sem = take(3)
    if last:
        (acc,) = take(1)
    rows = packs[0].shape[0] // 2
    width = w1.shape[0]
    inv_sqrt2 = 2.0**-0.5

    def fetch(j, slot):
        return pltpu.make_async_copy(packs[j], buf.at[slot], sem.at[slot])

    fetch(0, 0).start()
    if prior:
        held = pltpu.make_async_copy(prior[0], acc, prior_sem)
        held.start()
        accb[...] = prior_bias[0][...]
    else:
        acc[...] = jnp.zeros(acc.shape, F32)
        accb[...] = jnp.zeros(accb.shape, F32)

    def step(k, carry):
        slot = k & 1
        fetch(0, slot).wait()
        for j in range(1, blocks):

            @pl.when(k + 1 == j)
            def _(j=j):
                fetch(j, 1 - slot).start()

        sl = pl.ds(pl.multiple_of(k * rows, rows), rows)
        x = buf[slot, 0:rows]
        g = buf[slot, rows : 2 * rows]
        h = mm(x, w1[...]) + b1[...].reshape(1, -1)
        da = mm(g, w2[...], NT)
        cdf = 0.5 * (1.0 + lax.erf(h * inv_sqrt2))
        pdf = jnp.exp(-0.5 * h * h) * (1.0 / math.sqrt(2.0 * math.pi))
        act = (h * cdf).astype(BF16)
        dh = (da * (cdf + h * pdf)).astype(BF16)
        o_ff[sl, :] = mm(act, w2[...]).astype(BF16)
        n_ff[sl, :] = mm(dh, w1[...], NT).astype(BF16)
        accb[0:1] += jnp.sum(dh.astype(F32), axis=0, keepdims=True)
        if owned:

            @pl.when(k % 2 == 0)
            def _():
                accb[1:2] += jnp.sum(g.astype(F32), axis=0, keepdims=True)

        if prior:

            @pl.when(k == 0)
            def _():
                held.wait()

        acc[0:width] += mm(x, dh, TN)
        acc[width:] += mm(act, g, TN)
        return carry

    lax.fori_loop(0, blocks, step, 0)
    if last:
        ln_col[...] = jnp.sum(w1[...].astype(F32) * acc[0:width], axis=1, keepdims=True)
        summed[...] = acc[...].astype(BF16)


def att_kernel(first, last, blocks, heads, size, starts, *refs):
    refs = list(refs)
    take = lambda n: [refs.pop(0) for _ in range(n)]
    length, pos = take(2)
    ff_parts = take(4)
    prior = [] if first else take(1)
    packs = take(blocks)
    wqkv, wproj, qg, kg = take(4)
    prior_gain = [] if first else take(1)
    keep_near, keep_far, send = take(3)
    if last:
        pieces = take(len(refs) - 20)
        accg, ln_row = take(2)
    else:
        acc, accg = take(2)
    jt, dot_s, qs_t, q_s, k_s, kt_s, v_s, vt_s, es, dqt, dk, dv, ot, djt = take(14)
    ff_s, ff_sem, prior_sem = take(3)
    if last:
        (acc,) = take(1)
    rows = packs[0].shape[0] // 2
    later = []
    for k in range(4):
        rows_of = pl.ds(starts[k // 2], 2 * rows)
        later.append(pltpu.make_async_copy(ff_parts[k].at[rows_of], ff_s.at[k % 2, k // 2], ff_sem.at[k]))
        later[-1].start()
    if prior:
        later.append(pltpu.make_async_copy(prior[0], acc, prior_sem))
        later[-1].start()
    xs = [p.at[0:rows] for p in packs]
    gs = [p.at[rows : 2 * rows] for p in packs]
    joined = wqkv.shape[0]
    total = rows * blocks
    scale = size**-0.5
    up = scale * math.log2(math.e)
    for k in range(blocks):
        cols = slice(k * rows, (k + 1) * rows)
        jt[:, cols] = mm(wqkv[...], xs[k][...], NT)
        dot_s[:, cols] = mm(wproj[...], gs[k][...], NT)

    def normed(u):
        c = u - jnp.mean(u, axis=0, keepdims=True)
        r = lax.rsqrt(jnp.mean(c * c, axis=0, keepdims=True) + EPS)
        return c * r, r

    ones = jnp.concatenate(
        [jnp.ones((1, rows), F32), jnp.zeros((15, rows), F32)], axis=0
    ).astype(BF16)
    for h in range(heads):
        base = h * 3 * size
        gh = slice(h * size, (h + 1) * size)
        qt = normed(jt[base : base + size])[0] * qg[gh]
        kt = normed(jt[base + size : base + 2 * size])[0] * kg[gh]
        vt = jt[base + 2 * size : base + 3 * size]
        qs_t[h] = (qt * up).astype(BF16)
        q_s[h] = qt.T.astype(BF16)
        k_s[h] = kt.T.astype(BF16)
        v_s[h] = vt.T.astype(BF16)
        for k in range(blocks):
            cols = slice(k * rows, (k + 1) * rows)
            kt_s[h, k] = kt[:, cols].astype(BF16)
            vt_s[h, k, 0:size] = vt[:, cols].astype(BF16)
            vt_s[h, k, size : size + 16] = ones

    live = length[0]
    count = (live + rows - 1) // rows

    dk[...] = jnp.zeros(dk.shape, F32)
    dv[...] = jnp.zeros(dv.shape, F32)

    def head(h, carry):
        def forward(j, acc):
            b = j ^ pos[0]
            start = pl.multiple_of(b * rows, rows)
            s = mm(k_s[h, pl.ds(start, rows), :], qs_t[h])
            slot = lax.broadcasted_iota(jnp.int32, (rows, 1), 0) + j * rows
            e = jnp.where(slot < live, jnp.exp2(s), 0.0).astype(BF16)
            es[b] = e
            return acc + mm(vt_s[h, b], e)

        acc = lax.fori_loop(0, count, forward, jnp.zeros((size + 16, total), F32))
        inv = 1.0 / acc[size : size + 1]
        o = acc[0:size] * inv
        hs = pl.ds(pl.multiple_of(h * size, size), size)
        ot[hs, :] = o.astype(BF16)
        dof = dot_s[hs, :] * inv
        dot_b = dof.astype(BF16)
        do_b = dof.T.astype(BF16)
        r = jnp.sum(dot_b.astype(F32) * o, axis=0, keepdims=True)
        q_h = q_s[h]

        def backward(j, acc):
            b = j ^ pos[0]
            start = pl.multiple_of(b * rows, rows)
            dp = mm(v_s[h, pl.ds(start, rows), :], dot_b)
            e = es[b]
            ds = (e.astype(F32) * (dp - r)).astype(BF16)
            dv[h, pl.ds(start, rows), :] = mm(e, do_b)
            dk[h, pl.ds(start, rows), :] = mm(ds, q_h)
            return acc + mm(kt_s[h, b], ds)

        dqt[h] = lax.fori_loop(0, count, backward, jnp.zeros((size, total), F32))
        return carry

    lax.fori_loop(0, heads, head, 0)

    gains = []
    for h in range(heads):
        base = h * 3 * size
        gh = slice(h * size, (h + 1) * size)
        for c, gain, grad in ((0, qg, dqt[h]), (1, kg, dk[h].T)):
            n, r = normed(jt[base + c * size : base + (c + 1) * size])
            grad = grad * scale
            y = grad * gain[gh]
            back = r * (
                y
                - jnp.mean(y, axis=0, keepdims=True)
                - n * jnp.mean(y * n, axis=0, keepdims=True)
            )
            djt[base + c * size : base + (c + 1) * size] = back.astype(BF16)
            gains.append(jnp.sum(grad * n, axis=1, keepdims=True))
        djt[base + 2 * size : base + 3 * size] = dv[h].T.astype(BF16)
    gain_col = jnp.concatenate(gains[0::2] + gains[1::2], axis=0)

    for copy in later:
        copy.wait()
    tq = tp = None
    for k in range(blocks):
        cols = slice(k * rows, (k + 1) * rows)
        p = mm(djt[:, cols], xs[k][...])
        tq = p if tq is None else tq + p
        p = mm(ot[:, cols], gs[k][...])
        tp = p if tp is None else tp + p
        part = slice((k % 2) * rows, (k % 2 + 1) * rows)
        n = ff_s[1, k // 2, part].astype(F32) + mm(djt[:, cols], wqkv[...], TN)
        o = ff_s[0, k // 2, part].astype(F32) + mm(ot[:, cols], wproj[...], TN)
        if k % 2 == 0:
            out, base = (keep_near, keep_far)[k // 2], 0
        else:
            out, base = send, (k // 2) * 2 * rows
        out[base : base + rows] = o.astype(BF16)
        out[base + rows : base + 2 * rows] = n.astype(BF16)
    if prior:
        tq = tq + acc[0:joined]
        tp = tp + acc[joined:]
        gain_col = gain_col + prior_gain[0][...]
    accg[...] = gain_col
    acc[0:joined] = tq
    acc[joined:] = tp
    if last:
        ln_row[...] = jnp.sum(wqkv[...].astype(F32) * tq, axis=0, keepdims=True)
        emit_pieces(acc, pos.at[1:3], *pieces)


def final_kernel(images, *refs):
    tokens, d_out, gain, bias = refs[:4]
    ins = refs[4 : 4 + 3 * images]
    out, d_tokens = refs[-2:]
    rows = tokens.shape[1]
    for i in range(images):

        @pl.when(pl.program_id(0) == i)
        def _(i=i):
            keep, near, far = ins[3 * i : 3 * i + 3]
            both = [
                keep[at].astype(F32) + near[at].astype(F32) + far[at].astype(F32)
                for at in (slice(0, rows), slice(rows, 2 * rows))
            ]
            v = tokens[0].astype(F32)
            c = v - jnp.mean(v, axis=-1, keepdims=True)
            r = lax.rsqrt(jnp.mean(c * c, axis=-1, keepdims=True) + EPS)
            xhat = c * r
            out[0] = (v + both[0] + bias[...].reshape(1, -1)).astype(BF16)
            z = both[1] * gain[...].reshape(1, -1)
            back = r * (
                z
                - jnp.mean(z, axis=-1, keepdims=True)
                - xhat * jnp.mean(z * xhat, axis=-1, keepdims=True)
            )
            d_tokens[0] = d_out[0].astype(F32) + back


def join_kernel(n, *refs):
    pos, own, far, pairs = refs[0], refs[1 : 1 + n], refs[1 + n], refs[2 + n : 2 + 2 * n]
    one, two, whole = refs[2 + 2 * n :]
    step = own[0].shape[0]
    third = step * n
    for k in range(n):
        z = pos[1] ^ k
        at = pl.multiple_of(pos[0] * third + z * step, step)
        whole[pl.ds(at, step), :] = own[k][...].astype(F32)
        at = pl.multiple_of((1 - pos[0]) * third + z * step, step)
        whole[pl.ds(at, step), :] = far[k * step : (k + 1) * step].astype(F32)
        half = step // 2
        for s in range(2):
            at = pl.multiple_of(2 * third + z * step + (pos[0] ^ s) * half, half)
            whole[pl.ds(at, half), :] = pairs[k][s * half : (s + 1) * half].astype(F32)
    cut = one.shape[0]
    one[...] = whole[0:cut]
    two[...] = whole[cut:]


def block(dp_size, tp_size, *args):
    (tokens, lengths, ln_gain, w_qkv, q_gain, k_gain, w_proj, w_fc1, b_fc1, w_fc2, b_fc2, d_out) = args
    images, rows, width = tokens.shape
    heads, size = q_gain.shape
    hidden = w_fc1.shape[1]
    total = rows * tp_size
    blocks = tp_size
    joined = heads * 3 * size
    inner = heads * size
    n = dp_size // 2
    t = lax.axis_index("tp").astype(jnp.int32)
    d = lax.axis_index("dp").astype(jnp.int32)
    x, z = d & 1, d >> 1

    def swap(v, axis, mask):
        count = tp_size if axis == "tp" else dp_size
        return lax.ppermute(v, axis, [(i, i ^ mask) for i in range(count)])

    def after(v, dep):
        return lax.optimization_barrier((v, dep))[0]

    own = call(norm_kernel, [((2 * rows, width), BF16)] * images, 0, tokens, d_out, ln_gain)
    far = [swap(v, "tp", 2) for v in own]
    near = [swap(v, "tp", 1) for v in own]
    cross = [None] * images

    def forward(i, dep):
        cross[i] = swap(after(far[i], dep), "tp", 1)

    b1 = b_fc1
    pos = jnp.stack([x, z])

    def pieces_of(third, columns):
        step = third // n
        return [((third, columns), F32), ((third, columns), BF16), ((step, columns), F32)] + [
            ((step, columns), BF16)
        ] * (n - 1)

    qp_pieces = pieces_of((joined + inner) // 3, width)

    def ff(first, last, packs, state):
        count = len(packs)
        outs = [((count * rows, width), BF16)] * 2
        scratch = [
            pltpu.VMEM((2, 2 * rows, width), BF16),
            pltpu.SemaphoreType.DMA((2,)),
            pltpu.SemaphoreType.DMA,
        ]
        if last:
            outs += [((width + hidden, width), BF16), ((2, width), F32), ((width, 1), F32)]
            scratch += [pltpu.VMEM((width + hidden, width), F32)]
        else:
            outs += [((width + hidden, width), F32), ((2, width), F32)]
        res = call(
            functools.partial(ff_kernel, first, last, count, first), outs, 0,
            *packs, *state[:1], w_fc1, w_fc2, b1, *state[1:], n_any=count + len(state[:1]),
            scratch=scratch, flops=12 * count * rows * width * hidden,
        )
        return res[0], res[1], res[2:]

    qg = q_gain.reshape(-1, 1)
    kg = k_gain.reshape(-1, 1)
    w_t = w_qkv.T
    att_pos = jnp.stack([t, x, z])
    keeps = []

    def att(i, ff_parts, starts, state):
        first, last = i == 0, i == images - 1
        outs = [((2 * rows, width), BF16)] * 2 + [((4 * rows, width), BF16)]
        scratch = [
            pltpu.VMEM((joined, total), F32),
            pltpu.VMEM((inner, total), F32),
            pltpu.VMEM((heads, size, total), BF16),
            pltpu.VMEM((heads, total, size), BF16),
            pltpu.VMEM((heads, total, size), BF16),
            pltpu.VMEM((heads, blocks, size, rows), BF16),
            pltpu.VMEM((heads, total, size), BF16),
            pltpu.VMEM((heads, blocks, size + 16, rows), BF16),
            pltpu.VMEM((blocks, rows, total), BF16),
            pltpu.VMEM((heads, size, total), F32),
            pltpu.VMEM((heads, total, size), F32),
            pltpu.VMEM((heads, total, size), F32),
            pltpu.VMEM((inner, total), BF16),
            pltpu.VMEM((joined, total), BF16),
            pltpu.VMEM((2, 2, 2 * rows, width), BF16),
            pltpu.SemaphoreType.DMA((4,)),
            pltpu.SemaphoreType.DMA,
        ]
        if last:
            outs += qp_pieces + [((2 * inner, 1), F32), ((1, width), F32)]
            scratch += [pltpu.VMEM((joined + inner, width), F32)]
        else:
            outs += [((joined + inner, width), F32), ((2 * inner, 1), F32)]
        res = call(
            functools.partial(att_kernel, first, last, blocks, heads, size, starts), outs, 2,
            lengths[i : i + 1], att_pos, *ff_parts, *state[:1], own[i], near[i], far[i], cross[i],
            w_t, w_proj, qg, kg, *state[1:], n_any=4 + len(state[:1]),
            scratch=scratch,
            flops=6 * 8 * heads * total * total * size + 8 * total * width * (joined + inner),
        )
        keep_near, keep_far, send = res[:3]
        got = swap(send, "tp", 1)
        summed = (keep_far.astype(F32) + got[2 * rows :].astype(F32)).astype(BF16)
        keeps.extend([keep_near, got, swap(summed, "tp", 2)])
        return res[3:]

    def reduce_weight(small, keep_a, send_a, keep_b, *send_b):
        small = small.astype(BF16)
        extra = small.shape[0]
        got = swap(jnp.concatenate([send_a, small], axis=0), "dp", 1)
        half = keep_a + got[:-extra].astype(F32)
        small = (small.astype(F32) + got[-extra:].astype(F32)).astype(BF16)
        done_b = keep_b
        for k in range(1, n):
            done_b = done_b + swap(send_b[k - 1], "dp", 2 * k).astype(F32)
        step = keep_b.shape[0]
        piece = lambda k: lax.dynamic_slice_in_dim(half, (z ^ k) * step, step, 0)
        cut = step // 2
        sent = lax.dynamic_slice_in_dim(done_b, (1 - x) * cut, cut, 0).astype(BF16)
        done_b = lax.dynamic_slice_in_dim(done_b, x * cut, cut, 0) + swap(sent, "dp", 1).astype(F32)
        done_b = done_b.astype(BF16)
        done_a = piece(0)
        smalls = [small]
        for k in range(1, n):
            got = swap(jnp.concatenate([piece(k).astype(BF16), small], axis=0), "dp", 2 * k)
            done_a = done_a + got[:-extra].astype(F32)
            smalls.append(got[-extra:])
        done_a = done_a.astype(BF16)
        smalls = jnp.stack(smalls).astype(F32)
        small = sum(lax.dynamic_index_in_dim(smalls, z ^ k, 0, keepdims=False) for k in range(n))
        pair = jnp.concatenate([done_b, swap(done_b, "dp", 1)], axis=0)
        near_a = [done_a] + [swap(done_a, "dp", 2 * k) for k in range(1, n)]
        pairs = [pair] + [swap(pair, "dp", 2 * k) for k in range(1, n)]
        far_a = swap(jnp.concatenate(near_a, axis=0), "dp", 1)
        return near_a + [far_a] + pairs, small

    def join(parts, shapes):
        return call(
            functools.partial(join_kernel, n), [(s, F32) for s in shapes], 1, pos, *parts,
            scratch=[pltpu.VMEM((3 * n * parts[0].shape[0], width), F32)],
        )

    a_parts = ff(True, False, [b for i in range(images) for b in (own[i], near[i])], [])
    forward(0, a_parts[0])
    b_parts = ff(False, False, [far[0], cross[0]], a_parts[2])
    forward(1, b_parts[0])
    att_state = att(0, a_parts[:2] + b_parts[:2], (0, 0), [])
    for i in range(2, images):
        forward(i, att_state[1])
    c_parts = ff(False, True, [b for i in range(1, images) for b in (far[i], cross[i])], b_parts[2])
    state = c_parts[2]
    ff_out, small, ln_ff = state
    fc = lax.psum(ff_out, "dp")
    for i in range(1, images):
        att_state = att(i, a_parts[:2] + c_parts[:2], (2 * rows * i, 2 * rows * (i - 1)), att_state)
    *qp_out, gain_col, ln_att = att_state
    pad = jnp.zeros((1, width - 2 * inner), F32)
    late = jnp.concatenate(
        [
            jnp.concatenate([gain_col.reshape(1, -1), pad], axis=1),
            small,
            ln_att + ln_ff.reshape(1, -1),
            jnp.zeros((4, width), F32),
        ],
        axis=0,
    )
    qp_parts, late = reduce_weight(late, *qp_out)
    d_q_gain = late[0, :inner].reshape(heads, size)
    d_k_gain = late[0, inner : 2 * inner].reshape(heads, size)
    d_bias_one = late[1]
    both = late[2:4]
    both = both + swap(both, "tp", 1)
    both = both + swap(both, "tp", 2)
    d_bias_two = both[0]
    d_ln_gain = both[1] / ln_gain

    d_fc1, d_fc2 = fc[:width].astype(F32), fc[width:].astype(F32)
    d_qkv_t, d_proj = join(qp_parts, [(joined, width), (inner, width)])
    d_qkv = d_qkv_t.T

    def finish(begin, end, earlier):
        block = pl.BlockSpec((1, rows, width), lambda i: (begin + i, 0, 0))
        vector = pl.BlockSpec((width,), lambda i: (0,))
        first = pl.BlockSpec((2 * rows, width), lambda i: (0, 0))
        ins = keeps[3 * begin : 3 * end]
        return pl.pallas_call(
            functools.partial(final_kernel, end - begin),
            grid=(end - begin,),
            out_shape=[
                jax.ShapeDtypeStruct((images, rows, width), BF16),
                jax.ShapeDtypeStruct((images, rows, width), F32),
            ],
            in_specs=[block, block, vector, vector] + [first] * len(ins) + [ANY_SPEC] * len(earlier),
            out_specs=[block, block],
            input_output_aliases={4 + len(ins) + k: k for k in range(len(earlier))},
        )(tokens, d_out, ln_gain, b_fc2, *ins, *earlier)

    results = finish(0, images - 1, [])
    output, d_tokens = finish(images - 1, images, results)
    return (output, d_tokens, d_ln_gain, d_qkv, d_q_gain, d_k_gain, d_proj, d_fc1, d_bias_one, d_fc2, d_bias_two)


def solution(mesh):
    rows = P("dp", "tp", None)
    wide = P(None, "tp")
    tall = P("tp", None)
    return jax.shard_map(
        functools.partial(block, mesh.shape["dp"], mesh.shape["tp"]),
        mesh=mesh,
        in_specs=(rows, P("dp"), P(), wide, tall, tall, tall, wide, P("tp"), tall, P(), rows),
        out_specs=(rows, rows, P(), wide, tall, tall, tall, wide, P("tp"), tall, P()),
        check_vma=False,
    )
```

```python
import functools
import math

import jax
import jax.numpy as jnp
from jax import lax
from jax.experimental import pallas as pl
from jax.experimental.pallas import tpu as pltpu
from jax.sharding import PartitionSpec as P


EPS = 1e-06
F32 = jnp.float32
BF16 = jnp.bfloat16
NN = (((1,), (0,)), ((), ()))
NT = (((1,), (1,)), ((), ()))
TN = (((0,), (0,)), ((), ()))
VMEM_SPEC = pl.BlockSpec(memory_space=pltpu.VMEM)
ANY_SPEC = pl.BlockSpec(memory_space=pl.ANY)
SMEM_SPEC = pl.BlockSpec(memory_space=pltpu.SMEM)


def mm(a, b, dims=NN):
    return lax.dot_general(a, b, dims, preferred_element_type=F32)


def call(kernel, outs, n_smem, *args, n_any=0, any_outs=0, scratch=(), flops=0):
    in_specs = [SMEM_SPEC] * n_smem + [ANY_SPEC] * n_any + [VMEM_SPEC] * (len(args) - n_smem - n_any)
    moved = sum(a.size * a.dtype.itemsize for a in args)
    moved += sum(math.prod(s) * jnp.dtype(d).itemsize for s, d in outs)
    return pl.pallas_call(
        kernel,
        out_shape=[jax.ShapeDtypeStruct(s, d) for s, d in outs],
        in_specs=in_specs,
        out_specs=[ANY_SPEC] * any_outs + [VMEM_SPEC] * (len(outs) - any_outs),
        scratch_shapes=list(scratch),
        compiler_params=pltpu.CompilerParams(vmem_limit_bytes=60 * 1024 * 1024),
        cost_estimate=pl.CostEstimate(flops=flops, transcendentals=0, bytes_accessed=moved),
    )(*args)


def norm_kernel(begin, tokens, d_out, gain_ref, *refs):
    out_refs, (held, sem, sem_out) = refs[:-3], refs[-3:]
    rows = tokens.shape[1]
    reads, copies = [], []
    for i, out in enumerate(out_refs):
        reads.append(pltpu.make_async_copy(tokens.at[begin + i], held.at[i], sem.at[i]))
        reads[-1].start()
    for i, out in enumerate(out_refs):
        copies.append(pltpu.make_async_copy(d_out.at[begin + i], out.at[pl.ds(rows, rows)], sem_out.at[i]))
        copies[-1].start()
    for i, out in enumerate(out_refs):
        reads[i].wait()
        v = held[i].astype(F32)
        c = v - jnp.mean(v, axis=-1, keepdims=True)
        r = lax.rsqrt(jnp.mean(c * c, axis=-1, keepdims=True) + EPS)
        out[0:rows] = (c * r * gain_ref[...].reshape(1, -1)).astype(BF16)
    for copy in copies:
        copy.wait()


def as_row(column):
    return jnp.broadcast_to(column, (column.shape[0], 128)).T[0:1]


def emit_pieces(acc, pos, keep_a, send_a, keep_b, *send_b):
    third = acc.shape[0] // 3
    half, step = third, keep_b.shape[0]
    keep_a[...] = acc[pl.ds(pl.multiple_of(pos[0] * half, half), half), :]
    send_a[0:half] = acc[pl.ds(pl.multiple_of((1 - pos[0]) * half, half), half), :].astype(BF16)
    for k, out in enumerate((keep_b,) + send_b):
        at = pl.multiple_of(2 * third + (pos[1] ^ k) * step, step)
        out[...] = acc[pl.ds(at, step), :].astype(out.dtype)


def ff_kernel(first, last, blocks, owned, *refs):
    refs = list(refs)
    take = lambda n: [refs.pop(0) for _ in range(n)]
    packs = take(blocks)
    prior = [] if first else take(1)
    w1, w2, b1 = take(3)
    prior_bias = [] if first else take(1)
    o_ff, n_ff = take(2)
    if last:
        summed, accb = take(2)
    else:
        acc, accb = take(2)
    buf, sem, prior_sem = take(3)
    if last:
        (acc,) = take(1)
    rows = packs[0].shape[0] // 2
    width = w1.shape[0]
    inv_sqrt2 = 2.0**-0.5

    def fetch(j, slot):
        return pltpu.make_async_copy(packs[j], buf.at[slot], sem.at[slot])

    fetch(0, 0).start()
    if prior:
        held = pltpu.make_async_copy(prior[0], acc, prior_sem)
        held.start()
        accb[...] = prior_bias[0][...]
    else:
        acc[...] = jnp.zeros(acc.shape, F32)
        accb[...] = jnp.zeros(accb.shape, F32)

    def step(k, carry):
        slot = k & 1
        fetch(0, slot).wait()
        for j in range(1, blocks):

            @pl.when(k + 1 == j)
            def _(j=j):
                fetch(j, 1 - slot).start()

        sl = pl.ds(pl.multiple_of(k * rows, rows), rows)
        x = buf[slot, 0:rows]
        g = buf[slot, rows : 2 * rows]
        h = mm(x, w1[...]) + b1[...].reshape(1, -1)
        da = mm(g, w2[...], NT)
        cdf = 0.5 * (1.0 + lax.erf(h * inv_sqrt2))
        pdf = jnp.exp(-0.5 * h * h) * (1.0 / math.sqrt(2.0 * math.pi))
        act = (h * cdf).astype(BF16)
        dh = (da * (cdf + h * pdf)).astype(BF16)
        o_ff[sl, :] = mm(act, w2[...]).astype(BF16)
        n_ff[sl, :] = mm(dh, w1[...], NT).astype(BF16)
        accb[0:1] += jnp.sum(dh.astype(F32), axis=0, keepdims=True)
        if owned:

            @pl.when(k % 2 == 0)
            def _():
                accb[1:2] += jnp.sum(g.astype(F32), axis=0, keepdims=True)

        if prior:

            @pl.when(k == 0)
            def _():
                held.wait()

        acc[0:width] += mm(x, dh, TN)
        acc[width:] += mm(act, g, TN)
        return carry

    lax.fori_loop(0, blocks, step, 0)
    if last:
        accb[2:3] = as_row(jnp.sum(w1[...].astype(F32) * acc[0:width], axis=1, keepdims=True))
        summed[...] = acc[...].astype(BF16)


def att_kernel(first, last, blocks, heads, size, starts, *refs):
    refs = list(refs)
    take = lambda n: [refs.pop(0) for _ in range(n)]
    length, pos = take(2)
    ff_parts = take(4)
    prior = [] if first else take(1)
    packs = take(blocks)
    wqkv, wproj, qg, kg = take(4)
    prior_gain = [] if first else take(1)
    ff_small = take(1) if last else []
    keep_near, keep_far, send = take(3)
    if last:
        pieces = take(len(refs) - 22)
        (small,) = take(1)
    else:
        acc, accg = take(2)
    jt, dot_s, qs_t, q_s, k_s, kt_s, v_s, vt_s, es, dqt, dk, dv, ot, djt = take(14)
    ff_s, ff_sem, prior_sem, out_s, out_sem = take(5)
    if last:
        acc, accg = take(2)
    rows = packs[0].shape[0] // 2
    later = []
    for k in range(4):
        rows_of = pl.ds(starts[k // 2], 2 * rows)
        later.append(pltpu.make_async_copy(ff_parts[k].at[rows_of], ff_s.at[k % 2, k // 2], ff_sem.at[k]))
        later[-1].start()
    if prior:
        later.append(pltpu.make_async_copy(prior[0], acc, prior_sem))
        later[-1].start()
    xs = [p.at[0:rows] for p in packs]
    gs = [p.at[rows : 2 * rows] for p in packs]
    joined = wqkv.shape[0]
    total = rows * blocks
    scale = size**-0.5
    up = scale * math.log2(math.e)
    for k in range(blocks):
        cols = slice(k * rows, (k + 1) * rows)
        jt[:, cols] = mm(wqkv[...], xs[k][...], NT)
        dot_s[:, cols] = mm(wproj[...], gs[k][...], NT)

    def normed(u):
        c = u - jnp.mean(u, axis=0, keepdims=True)
        r = lax.rsqrt(jnp.mean(c * c, axis=0, keepdims=True) + EPS)
        return c * r, r

    ones = jnp.concatenate(
        [jnp.ones((1, rows), F32), jnp.zeros((15, rows), F32)], axis=0
    ).astype(BF16)

    def prepare(h, carry):
        base = pl.multiple_of(h * 3 * size, size)
        gh = pl.ds(pl.multiple_of(h * size, size), size)
        part = lambda c: jt[pl.ds(pl.multiple_of(base + c * size, size), size), :]
        qt = normed(part(0))[0] * qg[gh, :]
        kt = normed(part(1))[0] * kg[gh, :]
        vt = part(2)
        qs_t[h] = (qt * up).astype(BF16)
        q_s[h] = qt.T.astype(BF16)
        k_s[h] = kt.T.astype(BF16)
        v_s[h] = vt.T.astype(BF16)
        for k in range(blocks):
            cols = slice(k * rows, (k + 1) * rows)
            kt_s[h, k] = kt[:, cols].astype(BF16)
            vt_s[h, k, 0:size] = vt[:, cols].astype(BF16)
            vt_s[h, k, size : size + 16] = ones
        return carry

    lax.fori_loop(0, heads, prepare, 0)

    live = length[0]
    count = (live + rows - 1) // rows

    dk[...] = jnp.zeros(dk.shape, F32)
    dv[...] = jnp.zeros(dv.shape, F32)

    def head(h, carry):
        def forward(j, acc):
            b = j ^ pos[0]
            start = pl.multiple_of(b * rows, rows)
            s = mm(k_s[h, pl.ds(start, rows), :], qs_t[h])
            slot = lax.broadcasted_iota(jnp.int32, (rows, 1), 0) + j * rows
            e = jnp.where(slot < live, jnp.exp2(s), 0.0).astype(BF16)
            es[b] = e
            return acc + mm(vt_s[h, b], e)

        acc = lax.fori_loop(0, count, forward, jnp.zeros((size + 16, total), F32))
        inv = 1.0 / acc[size : size + 1]
        o = acc[0:size] * inv
        hs = pl.ds(pl.multiple_of(h * size, size), size)
        ot[hs, :] = o.astype(BF16)
        dof = dot_s[hs, :] * inv
        dot_b = dof.astype(BF16)
        do_b = dof.T.astype(BF16)
        r = jnp.sum(dot_b.astype(F32) * o, axis=0, keepdims=True)
        q_h = q_s[h]

        def backward(j, acc):
            b = j ^ pos[0]
            start = pl.multiple_of(b * rows, rows)
            dp = mm(v_s[h, pl.ds(start, rows), :], dot_b)
            e = es[b]
            ds = (e.astype(F32) * (dp - r)).astype(BF16)
            dv[h, pl.ds(start, rows), :] = mm(e, do_b)
            dk[h, pl.ds(start, rows), :] = mm(ds, q_h)
            return acc + mm(kt_s[h, b], ds)

        dqt[h] = lax.fori_loop(0, count, backward, jnp.zeros((size, total), F32))
        return carry

    lax.fori_loop(0, heads, head, 0)

    def undo(h, carry):
        base = pl.multiple_of(h * 3 * size, size)
        gh = pl.multiple_of(h * size, size)
        for c, gain, grad in ((0, qg, dqt[h]), (1, kg, dk[h].T)):
            at = pl.ds(pl.multiple_of(base + c * size, size), size)
            n, r = normed(jt[at, :])
            grad = grad * scale
            y = grad * gain[pl.ds(gh, size), :]
            back = r * (
                y
                - jnp.mean(y, axis=0, keepdims=True)
                - n * jnp.mean(y * n, axis=0, keepdims=True)
            )
            djt[at, :] = back.astype(BF16)
            accg[pl.ds(pl.multiple_of(c * heads * size + gh, size), size), :] = jnp.sum(grad * n, axis=1, keepdims=True)
        djt[pl.ds(pl.multiple_of(base + 2 * size, size), size), :] = dv[h].T.astype(BF16)
        return carry

    lax.fori_loop(0, heads, undo, 0)
    if prior:
        accg[...] += prior_gain[0][...]

    for copy in later:
        copy.wait()

    targets = [keep_near, send.at[pl.ds(0, 2 * rows)], keep_far, send.at[pl.ds(2 * rows, 2 * rows)]]
    writes = [pltpu.make_async_copy(out_s.at[k], targets[k], out_sem.at[k]) for k in range(blocks)]

    def give(k, carry):
        cols = pl.ds(pl.multiple_of(k * rows, rows), rows)
        part = pl.ds(pl.multiple_of((k & 1) * rows, rows), rows)
        n = ff_s[1, k >> 1, part, :].astype(F32) + mm(djt[:, cols], wqkv[...], TN)
        o = ff_s[0, k >> 1, part, :].astype(F32) + mm(ot[:, cols], wproj[...], TN)
        out_s[k, 0:rows] = o.astype(BF16)
        out_s[k, rows : 2 * rows] = n.astype(BF16)
        for j in range(blocks):

            @pl.when(k == j)
            def _(j=j):
                writes[j].start()

        return carry

    lax.fori_loop(0, blocks, give, 0)
    tq = tp = None
    for k in range(blocks):
        cols = slice(k * rows, (k + 1) * rows)
        p = mm(djt[:, cols], xs[k][...])
        tq = p if tq is None else tq + p
        p = mm(ot[:, cols], gs[k][...])
        tp = p if tp is None else tp + p
    if prior:
        tq = tq + acc[0:joined]
        tp = tp + acc[joined:]
    acc[0:joined] = tq
    acc[joined:] = tp
    if last:
        ln = jnp.sum(wqkv[...].astype(F32) * tq, axis=0, keepdims=True) + ff_small[0][2:3]
        gain_row = as_row(accg[...])
        pad = jnp.zeros((1, ln.shape[1] - gain_row.shape[1]), F32)
        lines = [jnp.concatenate([gain_row, pad], axis=1), ff_small[0][0:2], ln, jnp.zeros((4, ln.shape[1]), F32)]
        small[...] = jnp.concatenate(lines, axis=0).astype(BF16)
        emit_pieces(acc, pos.at[1:3], *pieces)
        third = pieces[0].shape[0]
        pieces[1][third : third + 8] = small[...]
    for write in writes:
        write.wait()


def final_kernel(images, *refs):
    tokens, d_out, gain, bias = refs[:4]
    ins = refs[4 : 4 + 3 * images]
    out, d_tokens = refs[-2:]
    rows = tokens.shape[1]
    for i in range(images):

        @pl.when(pl.program_id(0) == i)
        def _(i=i):
            keep, near, far = ins[3 * i : 3 * i + 3]
            both = [
                keep[at].astype(F32) + near[at].astype(F32) + far[at].astype(F32)
                for at in (slice(0, rows), slice(rows, 2 * rows))
            ]
            v = tokens[0].astype(F32)
            c = v - jnp.mean(v, axis=-1, keepdims=True)
            r = lax.rsqrt(jnp.mean(c * c, axis=-1, keepdims=True) + EPS)
            xhat = c * r
            out[0] = (v + both[0] + bias[...].reshape(1, -1)).astype(BF16)
            z = both[1] * gain[...].reshape(1, -1)
            back = r * (
                z
                - jnp.mean(z, axis=-1, keepdims=True)
                - xhat * jnp.mean(z * xhat, axis=-1, keepdims=True)
            )
            d_tokens[0] = d_out[0].astype(F32) + back


def join_kernel(n, *refs):
    pos, own, far, pairs = refs[0], refs[1 : 1 + n], refs[1 + n], refs[2 + n : 2 + 2 * n]
    one, two, whole = refs[2 + 2 * n :]
    step = own[0].shape[0]
    third = step * n
    for k in range(n):
        z = pos[1] ^ k
        at = pl.multiple_of(pos[0] * third + z * step, step)
        whole[pl.ds(at, step), :] = own[k][...].astype(F32)
        at = pl.multiple_of((1 - pos[0]) * third + z * step, step)
        whole[pl.ds(at, step), :] = far[k * step : (k + 1) * step].astype(F32)
        half = step // 2
        for s in range(2):
            at = pl.multiple_of(2 * third + z * step + (pos[0] ^ s) * half, half)
            whole[pl.ds(at, half), :] = pairs[k][s * half : (s + 1) * half].astype(F32)
    cut = one.shape[0]
    one[...] = whole[0:cut]
    two[...] = whole[cut:]


def block(dp_size, tp_size, *args):
    (tokens, lengths, ln_gain, w_qkv, q_gain, k_gain, w_proj, w_fc1, b_fc1, w_fc2, b_fc2, d_out) = args
    images, rows, width = tokens.shape
    heads, size = q_gain.shape
    hidden = w_fc1.shape[1]
    total = rows * tp_size
    blocks = tp_size
    joined = heads * 3 * size
    inner = heads * size
    n = dp_size // 2
    t = lax.axis_index("tp").astype(jnp.int32)
    d = lax.axis_index("dp").astype(jnp.int32)
    x, z = d & 1, d >> 1

    def swap(v, axis, mask):
        count = tp_size if axis == "tp" else dp_size
        return lax.ppermute(v, axis, [(i, i ^ mask) for i in range(count)])

    def after(v, dep):
        return lax.optimization_barrier((v, dep))[0]

    def norm(begin, end):
        count = end - begin
        return call(
            functools.partial(norm_kernel, begin), [((2 * rows, width), BF16)] * count, 0,
            tokens, d_out, ln_gain, n_any=2,
            scratch=[
                pltpu.VMEM((count, rows, width), BF16),
                pltpu.SemaphoreType.DMA((count,)),
                pltpu.SemaphoreType.DMA((count,)),
            ],
        )

    own = norm(0, images)
    far = [swap(v, "tp", 2) for v in own]
    near = [swap(v, "tp", 1) for v in own]
    cross = [None] * images

    def forward(i, dep):
        cross[i] = swap(after(far[i], dep), "tp", 1)

    b1 = b_fc1
    pos = jnp.stack([x, z])

    def pieces_of(third, columns):
        step = third // n
        return [((third, columns), F32), ((third + 8, columns), BF16), ((step, columns), F32)] + [
            ((step, columns), BF16)
        ] * (n - 1)

    qp_pieces = pieces_of((joined + inner) // 3, width)

    def ff(first, last, packs, state):
        count = len(packs)
        outs = [((count * rows, width), BF16)] * 2
        scratch = [
            pltpu.VMEM((2, 2 * rows, width), BF16),
            pltpu.SemaphoreType.DMA((2,)),
            pltpu.SemaphoreType.DMA,
        ]
        if last:
            outs += [((width + hidden, width), BF16), ((8, width), F32)]
            scratch += [pltpu.VMEM((width + hidden, width), F32)]
        else:
            outs += [((width + hidden, width), F32), ((8, width), F32)]
        res = call(
            functools.partial(ff_kernel, first, last, count, first), outs, 0,
            *packs, *state[:1], w_fc1, w_fc2, b1, *state[1:], n_any=count + len(state[:1]),
            scratch=scratch, flops=12 * count * rows * width * hidden,
        )
        return res[0], res[1], res[2:]

    qg = q_gain.reshape(-1, 1)
    kg = k_gain.reshape(-1, 1)
    w_t = w_qkv.T
    att_pos = jnp.stack([t, x, z])
    keeps = []

    def att(i, ff_parts, starts, state, ff_small=()):
        first, last = i == 0, i == images - 1
        outs = [((2 * rows, width), BF16)] * 2 + [((4 * rows, width), BF16)]
        scratch = [
            pltpu.VMEM((joined, total), F32),
            pltpu.VMEM((inner, total), F32),
            pltpu.VMEM((heads, size, total), BF16),
            pltpu.VMEM((heads, total, size), BF16),
            pltpu.VMEM((heads, total, size), BF16),
            pltpu.VMEM((heads, blocks, size, rows), BF16),
            pltpu.VMEM((heads, total, size), BF16),
            pltpu.VMEM((heads, blocks, size + 16, rows), BF16),
            pltpu.VMEM((blocks, rows, total), BF16),
            pltpu.VMEM((heads, size, total), F32),
            pltpu.VMEM((heads, total, size), F32),
            pltpu.VMEM((heads, total, size), F32),
            pltpu.VMEM((inner, total), BF16),
            pltpu.VMEM((joined, total), BF16),
            pltpu.VMEM((2, 2, 2 * rows, width), BF16),
            pltpu.SemaphoreType.DMA((4,)),
            pltpu.SemaphoreType.DMA,
            pltpu.VMEM((blocks, 2 * rows, width), BF16),
            pltpu.SemaphoreType.DMA((blocks,)),
        ]
        if last:
            outs += qp_pieces + [((8, width), BF16)]
            scratch += [pltpu.VMEM((joined + inner, width), F32), pltpu.VMEM((2 * inner, 1), F32)]
        else:
            outs += [((joined + inner, width), F32), ((2 * inner, 1), F32)]
        res = call(
            functools.partial(att_kernel, first, last, blocks, heads, size, starts), outs, 2,
            lengths[i : i + 1], att_pos, *ff_parts, *state[:1], own[i], near[i], far[i], cross[i],
            w_t, w_proj, qg, kg, *state[1:], *ff_small, n_any=4 + len(state[:1]), any_outs=3,
            scratch=scratch,
            flops=6 * 8 * heads * total * total * size + 8 * total * width * (joined + inner),
        )
        keep_near, keep_far, send = res[:3]
        got = swap(send, "tp", 1)
        summed = (keep_far.astype(F32) + got[2 * rows :].astype(F32)).astype(BF16)
        keeps.extend([keep_near, got, swap(summed, "tp", 2)])
        return res[3:]

    def reduce_weight(small, keep_a, send_a, keep_b, *send_b):
        extra = small.shape[0]
        got = swap(send_a, "dp", 1)
        half = keep_a + got[:-extra].astype(F32)
        small = (small.astype(F32) + got[-extra:].astype(F32)).astype(BF16)
        done_b = keep_b
        for k in range(1, n):
            done_b = done_b + swap(send_b[k - 1], "dp", 2 * k).astype(F32)
        step = keep_b.shape[0]
        piece = lambda k: lax.dynamic_slice_in_dim(half, (z ^ k) * step, step, 0)
        cut = step // 2
        sent = lax.dynamic_slice_in_dim(done_b, (1 - x) * cut, cut, 0).astype(BF16)
        done_b = lax.dynamic_slice_in_dim(done_b, x * cut, cut, 0) + swap(sent, "dp", 1).astype(F32)
        done_b = done_b.astype(BF16)
        done_a = piece(0)
        smalls = [small]
        for k in range(1, n):
            got = swap(jnp.concatenate([piece(k).astype(BF16), small], axis=0), "dp", 2 * k)
            done_a = done_a + got[:-extra].astype(F32)
            smalls.append(got[-extra:])
        done_a = done_a.astype(BF16)
        smalls = jnp.stack(smalls).astype(F32)
        small = sum(lax.dynamic_index_in_dim(smalls, z ^ k, 0, keepdims=False) for k in range(n))
        pair = jnp.concatenate([done_b, swap(done_b, "dp", 1)], axis=0)
        near_a = [done_a] + [swap(done_a, "dp", 2 * k) for k in range(1, n)]
        pairs = [pair] + [swap(pair, "dp", 2 * k) for k in range(1, n)]
        far_a = swap(jnp.concatenate(near_a, axis=0), "dp", 1)
        return near_a + [far_a] + pairs, small

    def join(parts, shapes):
        return call(
            functools.partial(join_kernel, n), [(s, F32) for s in shapes], 1, pos, *parts,
            scratch=[pltpu.VMEM((3 * n * parts[0].shape[0], width), F32)],
        )

    a_parts = ff(True, False, [b for i in range(images) for b in (own[i], near[i])], [])
    forward(0, a_parts[0])
    b_parts = ff(False, False, [far[0], cross[0]], a_parts[2])
    forward(1, b_parts[0])
    att_state = att(0, a_parts[:2] + b_parts[:2], (0, 0), [])
    for i in range(2, images):
        forward(i, att_state[1])
    c_parts = ff(False, True, [b for i in range(1, images) for b in (far[i], cross[i])], b_parts[2])
    state = c_parts[2]
    ff_out, ff_small = state
    fc = lax.psum(ff_out, "dp")
    for i in range(1, images):
        starts = (2 * rows * i, 2 * rows * (i - 1))
        att_state = att(i, a_parts[:2] + c_parts[:2], starts, att_state, [ff_small] if i == images - 1 else [])
    *qp_out, small = att_state
    qp_parts, late = reduce_weight(small, *qp_out)
    d_q_gain = late[0, :inner].reshape(heads, size)
    d_k_gain = late[0, inner : 2 * inner].reshape(heads, size)
    d_bias_one = late[1]
    both = late[2:4]
    both = both + swap(both, "tp", 1)
    both = both + swap(both, "tp", 2)
    d_bias_two = both[0]
    d_ln_gain = both[1] / ln_gain

    d_fc1, d_fc2 = fc[:width].astype(F32), fc[width:].astype(F32)
    d_qkv_t, d_proj = join(qp_parts, [(joined, width), (inner, width)])
    d_qkv = d_qkv_t.T

    def finish(begin, end, earlier):
        block = pl.BlockSpec((1, rows, width), lambda i: (begin + i, 0, 0))
        vector = pl.BlockSpec((width,), lambda i: (0,))
        first = pl.BlockSpec((2 * rows, width), lambda i: (0, 0))
        ins = keeps[3 * begin : 3 * end]
        return pl.pallas_call(
            functools.partial(final_kernel, end - begin),
            grid=(end - begin,),
            out_shape=[
                jax.ShapeDtypeStruct((images, rows, width), BF16),
                jax.ShapeDtypeStruct((images, rows, width), F32),
            ],
            in_specs=[block, block, vector, vector] + [first] * len(ins) + [ANY_SPEC] * len(earlier),
            out_specs=[block, block],
            input_output_aliases={4 + len(ins) + k: k for k in range(len(earlier))},
        )(tokens, d_out, ln_gain, b_fc2, *ins, *earlier)

    results = finish(0, images - 1, [])
    output, d_tokens = finish(images - 1, images, results)
    return (output, d_tokens, d_ln_gain, d_qkv, d_q_gain, d_k_gain, d_proj, d_fc1, d_bias_one, d_fc2, d_bias_two)


def solution(mesh):
    rows = P("dp", "tp", None)
    wide = P(None, "tp")
    tall = P("tp", None)
    return jax.shard_map(
        functools.partial(block, mesh.shape["dp"], mesh.shape["tp"]),
        mesh=mesh,
        in_specs=(rows, P("dp"), P(), wide, tall, tall, tall, wide, P("tp"), tall, P(), rows),
        out_specs=(rows, rows, P(), wide, tall, tall, tall, wide, P("tp"), tall, P()),
        check_vma=False,
    )
```

```python
import functools
import math

import jax
import jax.numpy as jnp
from jax import lax
from jax.experimental import pallas as pl
from jax.experimental.pallas import tpu as pltpu
from jax.sharding import PartitionSpec as P


EPS = 1e-06
F32 = jnp.float32
BF16 = jnp.bfloat16
NN = (((1,), (0,)), ((), ()))
NT = (((1,), (1,)), ((), ()))
TN = (((0,), (0,)), ((), ()))
VMEM_SPEC = pl.BlockSpec(memory_space=pltpu.VMEM)
ANY_SPEC = pl.BlockSpec(memory_space=pl.ANY)
SMEM_SPEC = pl.BlockSpec(memory_space=pltpu.SMEM)


def mm(a, b, dims=NN):
    return lax.dot_general(a, b, dims, preferred_element_type=F32)


def call(kernel, outs, n_smem, *args, n_any=0, any_outs=0, scratch=(), flops=0):
    in_specs = [SMEM_SPEC] * n_smem + [ANY_SPEC] * n_any + [VMEM_SPEC] * (len(args) - n_smem - n_any)
    moved = sum(a.size * a.dtype.itemsize for a in args)
    moved += sum(math.prod(s) * jnp.dtype(d).itemsize for s, d in outs)
    return pl.pallas_call(
        kernel,
        out_shape=[jax.ShapeDtypeStruct(s, d) for s, d in outs],
        in_specs=in_specs,
        out_specs=[ANY_SPEC] * any_outs + [VMEM_SPEC] * (len(outs) - any_outs),
        scratch_shapes=list(scratch),
        compiler_params=pltpu.CompilerParams(vmem_limit_bytes=60 * 1024 * 1024),
        cost_estimate=pl.CostEstimate(flops=flops, transcendentals=0, bytes_accessed=moved),
    )(*args)


def norm_kernel(begin, tokens, d_out, gain_ref, *refs):
    out_refs, (held, sem, sem_out) = refs[:-3], refs[-3:]
    rows = tokens.shape[1]
    reads, copies = [], []
    for i, out in enumerate(out_refs):
        reads.append(pltpu.make_async_copy(tokens.at[begin + i], held.at[i], sem.at[i]))
        reads[-1].start()
    for i, out in enumerate(out_refs):
        copies.append(pltpu.make_async_copy(d_out.at[begin + i], out.at[pl.ds(rows, rows)], sem_out.at[i]))
        copies[-1].start()
    for i, out in enumerate(out_refs):
        reads[i].wait()
        v = held[i].astype(F32)
        c = v - jnp.mean(v, axis=-1, keepdims=True)
        r = lax.rsqrt(jnp.mean(c * c, axis=-1, keepdims=True) + EPS)
        out[0:rows] = (c * r * gain_ref[...].reshape(1, -1)).astype(BF16)
    for copy in copies:
        copy.wait()


def as_row(column):
    return jnp.broadcast_to(column, (column.shape[0], 128)).T[0:1]


def emit_pieces(acc, pos, keep_a, send_a, keep_b, *send_b):
    third = acc.shape[0] // 3
    half, step = third, keep_b.shape[0]
    keep_a[...] = acc[pl.ds(pl.multiple_of(pos[0] * half, half), half), :]
    send_a[0:half] = acc[pl.ds(pl.multiple_of((1 - pos[0]) * half, half), half), :].astype(BF16)
    for k, out in enumerate((keep_b,) + send_b):
        at = pl.multiple_of(2 * third + (pos[1] ^ k) * step, step)
        out[...] = acc[pl.ds(at, step), :].astype(out.dtype)


def ff_kernel(first, last, blocks, owned, *refs):
    refs = list(refs)
    take = lambda n: [refs.pop(0) for _ in range(n)]
    packs = take(blocks)
    prior = [] if first else take(1)
    w1, w2, b1 = take(3)
    prior_bias = [] if first else take(1)
    o_ff, n_ff = take(2)
    if last:
        summed, accb = take(2)
    else:
        acc, accb = take(2)
    buf, sem, prior_sem = take(3)
    if last:
        (acc,) = take(1)
    rows = packs[0].shape[0] // 2
    width = w1.shape[0]
    inv_sqrt2 = 2.0**-0.5

    def fetch(j, slot):
        return pltpu.make_async_copy(packs[j], buf.at[slot], sem.at[slot])

    fetch(0, 0).start()
    if prior:
        held = pltpu.make_async_copy(prior[0], acc, prior_sem)
        held.start()
        accb[...] = prior_bias[0][...]
    else:
        acc[...] = jnp.zeros(acc.shape, F32)
        accb[...] = jnp.zeros(accb.shape, F32)

    def step(k, carry):
        slot = k & 1
        fetch(0, slot).wait()
        for j in range(1, blocks):

            @pl.when(k + 1 == j)
            def _(j=j):
                fetch(j, 1 - slot).start()

        sl = pl.ds(pl.multiple_of(k * rows, rows), rows)
        x = buf[slot, 0:rows]
        g = buf[slot, rows : 2 * rows]
        h = mm(x, w1[...]) + b1[...].reshape(1, -1)
        da = mm(g, w2[...], NT)
        cdf = 0.5 * (1.0 + lax.erf(h * inv_sqrt2))
        pdf = jnp.exp(-0.5 * h * h) * (1.0 / math.sqrt(2.0 * math.pi))
        act = (h * cdf).astype(BF16)
        dh = (da * (cdf + h * pdf)).astype(BF16)
        o_ff[sl, :] = mm(act, w2[...]).astype(BF16)
        n_ff[sl, :] = mm(dh, w1[...], NT).astype(BF16)
        accb[0:1] += jnp.sum(dh.astype(F32), axis=0, keepdims=True)
        if owned:

            @pl.when(k % 2 == 0)
            def _():
                accb[1:2] += jnp.sum(g.astype(F32), axis=0, keepdims=True)

        if prior:

            @pl.when(k == 0)
            def _():
                held.wait()

        acc[0:width] += mm(x, dh, TN)
        acc[width:] += mm(act, g, TN)
        return carry

    lax.fori_loop(0, blocks, step, 0)
    if last:
        accb[2:3] = as_row(jnp.sum(w1[...].astype(F32) * acc[0:width], axis=1, keepdims=True))
        summed[...] = acc[...].astype(BF16)


def att_kernel(first, last, blocks, heads, size, starts, *refs):
    refs = list(refs)
    take = lambda n: [refs.pop(0) for _ in range(n)]
    length, pos = take(2)
    parts = take(blocks)
    ff_parts = take(4)
    prior = [] if first else take(1)
    wqkv, wproj, qg, kg = take(4)
    prior_gain = [] if first else take(1)
    ff_small = take(1) if last else []
    keep_near, keep_far, send = take(3)
    if last:
        pieces = take(len(refs) - 26)
        (small,) = take(1)
    else:
        acc, accg = take(2)
    jt, dot_s, qs_t, qt_s, k_s, kt_s, v_s, vt_s, es, dqt, dk, dv, ot, djt = take(14)
    ff_s, ff_sem, prior_sem, out_s, out_sem, dot_bs, r_s, pack_s, pack_sem = take(9)
    if last:
        acc, accg = take(2)
    rows = parts[0].shape[0] // 2
    joined = wqkv.shape[0]
    total = rows * blocks
    scale = size**-0.5
    up = scale * math.log2(math.e)
    for k in range(blocks):
        pltpu.make_async_copy(parts[k], pack_s.at[k], pack_sem.at[k]).start()

    def project(k, carry):
        pltpu.make_async_copy(parts[0], pack_s.at[k], pack_sem.at[k]).wait()
        cols = pl.ds(pl.multiple_of(k * rows, rows), rows)
        jt[:, cols] = mm(wqkv[...], pack_s[k, 0:rows], NT)
        dot_s[:, cols] = mm(wproj[...], pack_s[k, rows : 2 * rows], NT)
        return carry

    lax.fori_loop(0, blocks, project, 0)
    later = []
    for k in range(4):
        rows_of = pl.ds(starts[k // 2], 2 * rows)
        later.append(pltpu.make_async_copy(ff_parts[k].at[rows_of], ff_s.at[k % 2, k // 2], ff_sem.at[k]))
        later[-1].start()
    if prior:
        later.append(pltpu.make_async_copy(prior[0], acc, prior_sem))
        later[-1].start()
    else:
        acc[...] = jnp.zeros(acc.shape, F32)

    def normed(u):
        c = u - jnp.mean(u, axis=0, keepdims=True)
        r = lax.rsqrt(jnp.mean(c * c, axis=0, keepdims=True) + EPS)
        return c * r, r

    ones = jnp.concatenate(
        [jnp.ones((1, rows), F32), jnp.zeros((15, rows), F32)], axis=0
    ).astype(BF16)

    def prepare(h, carry):
        base = pl.multiple_of(h * 3 * size, size)
        gh = pl.ds(pl.multiple_of(h * size, size), size)
        part = lambda c: jt[pl.ds(pl.multiple_of(base + c * size, size), size), :]
        qt = normed(part(0))[0] * qg[gh, :]
        kt = normed(part(1))[0] * kg[gh, :]
        vt = part(2)
        qs_t[h] = (qt * up).astype(BF16)
        qt_s[h] = qt.astype(BF16)
        k_s[h] = kt.T.astype(BF16)
        v_s[h] = vt.T.astype(BF16)
        for k in range(blocks):
            cols = slice(k * rows, (k + 1) * rows)
            kt_s[h, k] = kt[:, cols].astype(BF16)
            vt_s[h, k, 0:size] = vt[:, cols].astype(BF16)
            vt_s[h, k, size : size + 16] = ones
        return carry

    lax.fori_loop(0, heads, prepare, 0)

    live = length[0]
    count = (live + rows - 1) // rows

    dk[...] = jnp.zeros(dk.shape, F32)
    dv[...] = jnp.zeros(dv.shape, F32)

    def forward(j, accs):
        b = j ^ pos[0]
        start = pl.multiple_of(b * rows, rows)
        slot = lax.broadcasted_iota(jnp.int32, (rows, 1), 0) + j * rows
        out = []
        for h in range(heads):
            s = mm(k_s[h, pl.ds(start, rows), :], qs_t[h])
            e = jnp.where(slot < live, jnp.exp2(s), 0.0).astype(BF16)
            es[h, b] = e
            out.append(accs[h] + mm(vt_s[h, b], e))
        return tuple(out)

    zero = jnp.zeros((size + 16, total), F32)
    accs = lax.fori_loop(0, count, forward, (zero,) * heads)
    for h in range(heads):
        inv = 1.0 / accs[h][size : size + 1]
        o = accs[h][0:size] * inv
        hs = slice(h * size, (h + 1) * size)
        ot[hs] = o.astype(BF16)
        dot_b = (dot_s[hs] * inv).astype(BF16)
        dot_bs[hs] = dot_b
        r_s[h : h + 1] = jnp.sum(dot_b.astype(F32) * o, axis=0, keepdims=True)

    def backward(j, accs):
        b = j ^ pos[0]
        start = pl.multiple_of(b * rows, rows)
        out = []
        for h in range(heads):
            dot_b = dot_bs[h * size : (h + 1) * size]
            dp = mm(v_s[h, pl.ds(start, rows), :], dot_b)
            e = es[h, b]
            ds = (e.astype(F32) * (dp - r_s[h : h + 1])).astype(BF16)
            dv[h, b] = mm(dot_b, e, NT)
            dk[h, b] = mm(qt_s[h], ds, NT)
            out.append(accs[h] + mm(kt_s[h, b], ds))
        return tuple(out)

    zero = jnp.zeros((size, total), F32)
    accs = lax.fori_loop(0, count, backward, (zero,) * heads)
    for h in range(heads):
        dqt[h] = accs[h]

    def undo(h, carry):
        base = pl.multiple_of(h * 3 * size, size)
        gh = pl.multiple_of(h * size, size)
        for c, gain, grad in ((0, qg, dqt[h]), (1, kg, jnp.concatenate([dk[h, k] for k in range(blocks)], axis=1))):
            at = pl.ds(pl.multiple_of(base + c * size, size), size)
            n, r = normed(jt[at, :])
            grad = grad * scale
            y = grad * gain[pl.ds(gh, size), :]
            back = r * (
                y
                - jnp.mean(y, axis=0, keepdims=True)
                - n * jnp.mean(y * n, axis=0, keepdims=True)
            )
            djt[at, :] = back.astype(BF16)
            accg[pl.ds(pl.multiple_of(c * heads * size + gh, size), size), :] = jnp.sum(grad * n, axis=1, keepdims=True)
        values = jnp.concatenate([dv[h, k] for k in range(blocks)], axis=1)
        djt[pl.ds(pl.multiple_of(base + 2 * size, size), size), :] = values.astype(BF16)
        return carry

    lax.fori_loop(0, heads, undo, 0)
    if prior:
        accg[...] += prior_gain[0][...]

    for copy in later:
        copy.wait()

    targets = [keep_near, send.at[pl.ds(0, 2 * rows)], keep_far, send.at[pl.ds(2 * rows, 2 * rows)]]
    writes = [pltpu.make_async_copy(out_s.at[k], targets[k], out_sem.at[k]) for k in range(blocks)]

    def give(k, carry):
        cols = pl.ds(pl.multiple_of(k * rows, rows), rows)
        part = pl.ds(pl.multiple_of((k & 1) * rows, rows), rows)
        n = ff_s[1, k >> 1, part, :].astype(F32) + mm(djt[:, cols], wqkv[...], TN)
        o = ff_s[0, k >> 1, part, :].astype(F32) + mm(ot[:, cols], wproj[...], TN)
        out_s[k, 0:rows] = o.astype(BF16)
        out_s[k, rows : 2 * rows] = n.astype(BF16)
        acc[0:joined] += mm(djt[:, cols], pack_s[k, 0:rows])
        acc[joined:] += mm(ot[:, cols], pack_s[k, rows : 2 * rows])
        for j in range(blocks):

            @pl.when(k == j)
            def _(j=j):
                writes[j].start()

        return carry

    lax.fori_loop(0, blocks, give, 0)
    if last:
        ln = jnp.sum(wqkv[...].astype(F32) * acc[0:joined], axis=0, keepdims=True) + ff_small[0][2:3]
        gain_row = as_row(accg[...])
        pad = jnp.zeros((1, ln.shape[1] - gain_row.shape[1]), F32)
        lines = [jnp.concatenate([gain_row, pad], axis=1), ff_small[0][0:2], ln, jnp.zeros((4, ln.shape[1]), F32)]
        small[...] = jnp.concatenate(lines, axis=0).astype(BF16)
        emit_pieces(acc, pos.at[1:3], *pieces)
        third = pieces[0].shape[0]
        pieces[1][third : third + 8] = small[...]
    for write in writes:
        write.wait()


def final_kernel(images, *refs):
    tokens, d_out, gain, bias = refs[:4]
    ins = refs[4 : 4 + 3 * images]
    out, d_tokens = refs[-2:]
    rows = tokens.shape[1]
    for i in range(images):

        @pl.when(pl.program_id(0) == i)
        def _(i=i):
            keep, near, far = ins[3 * i : 3 * i + 3]
            both = [
                keep[at].astype(F32) + near[at].astype(F32) + far[at].astype(F32)
                for at in (slice(0, rows), slice(rows, 2 * rows))
            ]
            v = tokens[0].astype(F32)
            c = v - jnp.mean(v, axis=-1, keepdims=True)
            r = lax.rsqrt(jnp.mean(c * c, axis=-1, keepdims=True) + EPS)
            xhat = c * r
            out[0] = (v + both[0] + bias[...].reshape(1, -1)).astype(BF16)
            z = both[1] * gain[...].reshape(1, -1)
            back = r * (
                z
                - jnp.mean(z, axis=-1, keepdims=True)
                - xhat * jnp.mean(z * xhat, axis=-1, keepdims=True)
            )
            d_tokens[0] = d_out[0].astype(F32) + back


def join_kernel(n, *refs):
    pos, own, far, pairs = refs[0], refs[1 : 1 + n], refs[1 + n], refs[2 + n : 2 + 2 * n]
    one, two, whole = refs[2 + 2 * n :]
    step = own[0].shape[0]
    third = step * n
    for k in range(n):
        z = pos[1] ^ k
        at = pl.multiple_of(pos[0] * third + z * step, step)
        whole[pl.ds(at, step), :] = own[k][...].astype(F32)
        at = pl.multiple_of((1 - pos[0]) * third + z * step, step)
        whole[pl.ds(at, step), :] = far[k * step : (k + 1) * step].astype(F32)
        half = step // 2
        for s in range(2):
            at = pl.multiple_of(2 * third + z * step + (pos[0] ^ s) * half, half)
            whole[pl.ds(at, half), :] = pairs[k][s * half : (s + 1) * half].astype(F32)
    cut = one.shape[0]
    one[...] = whole[0:cut]
    two[...] = whole[cut:]


def block(dp_size, tp_size, *args):
    (tokens, lengths, ln_gain, w_qkv, q_gain, k_gain, w_proj, w_fc1, b_fc1, w_fc2, b_fc2, d_out) = args
    images, rows, width = tokens.shape
    heads, size = q_gain.shape
    hidden = w_fc1.shape[1]
    total = rows * tp_size
    blocks = tp_size
    joined = heads * 3 * size
    inner = heads * size
    n = dp_size // 2
    t = lax.axis_index("tp").astype(jnp.int32)
    d = lax.axis_index("dp").astype(jnp.int32)
    x, z = d & 1, d >> 1

    def swap(v, axis, mask):
        count = tp_size if axis == "tp" else dp_size
        return lax.ppermute(v, axis, [(i, i ^ mask) for i in range(count)])

    def after(v, dep):
        return lax.optimization_barrier((v, dep))[0]

    def norm(begin, end):
        count = end - begin
        return call(
            functools.partial(norm_kernel, begin), [((2 * rows, width), BF16)] * count, 0,
            tokens, d_out, ln_gain, n_any=2,
            scratch=[
                pltpu.VMEM((count, rows, width), BF16),
                pltpu.SemaphoreType.DMA((count,)),
                pltpu.SemaphoreType.DMA((count,)),
            ],
        )

    own = norm(0, images)
    far = [swap(v, "tp", 2) for v in own]
    near = [swap(v, "tp", 1) for v in own]
    cross = [None] * images

    def forward(i, dep):
        cross[i] = swap(after(far[i], dep), "tp", 1)

    b1 = b_fc1
    pos = jnp.stack([x, z])

    def pieces_of(third, columns):
        step = third // n
        return [((third, columns), F32), ((third + 8, columns), BF16), ((step, columns), F32)] + [
            ((step, columns), BF16)
        ] * (n - 1)

    qp_pieces = pieces_of((joined + inner) // 3, width)

    def ff(first, last, packs, state):
        count = len(packs)
        outs = [((count * rows, width), BF16)] * 2
        scratch = [
            pltpu.VMEM((2, 2 * rows, width), BF16),
            pltpu.SemaphoreType.DMA((2,)),
            pltpu.SemaphoreType.DMA,
        ]
        if last:
            outs += [((width + hidden, width), BF16), ((8, width), F32)]
            scratch += [pltpu.VMEM((width + hidden, width), F32)]
        else:
            outs += [((width + hidden, width), F32), ((8, width), F32)]
        res = call(
            functools.partial(ff_kernel, first, last, count, first), outs, 0,
            *packs, *state[:1], w_fc1, w_fc2, b1, *state[1:], n_any=count + len(state[:1]),
            scratch=scratch, flops=12 * count * rows * width * hidden,
        )
        return res[0], res[1], res[2:]

    qg = q_gain.reshape(-1, 1)
    kg = k_gain.reshape(-1, 1)
    w_t = w_qkv.T
    att_pos = jnp.stack([t, x, z])
    keeps = []

    def att(i, ff_parts, starts, state, ff_small=()):
        first, last = i == 0, i == images - 1
        outs = [((2 * rows, width), BF16)] * 2 + [((4 * rows, width), BF16)]
        scratch = [
            pltpu.VMEM((joined, total), F32),
            pltpu.VMEM((inner, total), F32),
            pltpu.VMEM((heads, size, total), BF16),
            pltpu.VMEM((heads, size, total), BF16),
            pltpu.VMEM((heads, total, size), BF16),
            pltpu.VMEM((heads, blocks, size, rows), BF16),
            pltpu.VMEM((heads, total, size), BF16),
            pltpu.VMEM((heads, blocks, size + 16, rows), BF16),
            pltpu.VMEM((heads, blocks, rows, total), BF16),
            pltpu.VMEM((heads, size, total), F32),
            pltpu.VMEM((heads, blocks, size, rows), F32),
            pltpu.VMEM((heads, blocks, size, rows), F32),
            pltpu.VMEM((inner, total), BF16),
            pltpu.VMEM((joined, total), BF16),
            pltpu.VMEM((2, 2, 2 * rows, width), BF16),
            pltpu.SemaphoreType.DMA((4,)),
            pltpu.SemaphoreType.DMA,
            pltpu.VMEM((blocks, 2 * rows, width), BF16),
            pltpu.SemaphoreType.DMA((blocks,)),
            pltpu.VMEM((inner, total), BF16),
            pltpu.VMEM((8, total), F32),
            pltpu.VMEM((blocks, 2 * rows, width), BF16),
            pltpu.SemaphoreType.DMA((blocks,)),
        ]
        if last:
            outs += qp_pieces + [((8, width), BF16)]
            scratch += [pltpu.VMEM((joined + inner, width), F32), pltpu.VMEM((2 * inner, 1), F32)]
        else:
            outs += [((joined + inner, width), F32), ((2 * inner, 1), F32)]
        res = call(
            functools.partial(att_kernel, first, last, blocks, heads, size, starts), outs, 2,
            lengths[i : i + 1], att_pos, own[i], near[i], far[i], cross[i], *ff_parts, *state[:1],
            w_t, w_proj, qg, kg, *state[1:], *ff_small, n_any=blocks + 4 + len(state[:1]), any_outs=3,
            scratch=scratch,
            flops=6 * 8 * heads * total * total * size + 8 * total * width * (joined + inner),
        )
        keep_near, keep_far, send = res[:3]
        got = swap(send, "tp", 1)
        summed = (keep_far.astype(F32) + got[2 * rows :].astype(F32)).astype(BF16)
        keeps.extend([keep_near, got, swap(summed, "tp", 2)])
        return res[3:]

    def reduce_weight(small, keep_a, send_a, keep_b, *send_b):
        extra = small.shape[0]
        got = swap(send_a, "dp", 1)
        half = keep_a + got[:-extra].astype(F32)
        small = (small.astype(F32) + got[-extra:].astype(F32)).astype(BF16)
        done_b = keep_b
        for k in range(1, n):
            done_b = done_b + swap(send_b[k - 1], "dp", 2 * k).astype(F32)
        step = keep_b.shape[0]
        piece = lambda k: lax.dynamic_slice_in_dim(half, (z ^ k) * step, step, 0)
        cut = step // 2
        sent = lax.dynamic_slice_in_dim(done_b, (1 - x) * cut, cut, 0).astype(BF16)
        done_b = lax.dynamic_slice_in_dim(done_b, x * cut, cut, 0) + swap(sent, "dp", 1).astype(F32)
        done_b = done_b.astype(BF16)
        done_a = piece(0)
        smalls = [small]
        for k in range(1, n):
            got = swap(jnp.concatenate([piece(k).astype(BF16), small], axis=0), "dp", 2 * k)
            done_a = done_a + got[:-extra].astype(F32)
            smalls.append(got[-extra:])
        done_a = done_a.astype(BF16)
        smalls = jnp.stack(smalls).astype(F32)
        small = sum(lax.dynamic_index_in_dim(smalls, z ^ k, 0, keepdims=False) for k in range(n))
        pair = jnp.concatenate([done_b, swap(done_b, "dp", 1)], axis=0)
        near_a = [done_a] + [swap(done_a, "dp", 2 * k) for k in range(1, n)]
        pairs = [pair] + [swap(pair, "dp", 2 * k) for k in range(1, n)]
        far_a = swap(jnp.concatenate(near_a, axis=0), "dp", 1)
        return near_a + [far_a] + pairs, small

    def join(parts, shapes):
        return call(
            functools.partial(join_kernel, n), [(s, F32) for s in shapes], 1, pos, *parts,
            scratch=[pltpu.VMEM((3 * n * parts[0].shape[0], width), F32)],
        )

    a_parts = ff(True, False, [b for i in range(images) for b in (own[i], near[i])], [])
    forward(0, a_parts[0])
    b_parts = ff(False, False, [far[0], cross[0]], a_parts[2])
    forward(1, b_parts[0])
    att_state = att(0, a_parts[:2] + b_parts[:2], (0, 0), [])
    for i in range(2, images):
        forward(i, att_state[1])
    c_parts = ff(False, True, [b for i in range(1, images) for b in (far[i], cross[i])], b_parts[2])
    state = c_parts[2]
    ff_out, ff_small = state
    fc = lax.psum(ff_out, "dp")
    for i in range(1, images):
        starts = (2 * rows * i, 2 * rows * (i - 1))
        att_state = att(i, a_parts[:2] + c_parts[:2], starts, att_state, [ff_small] if i == images - 1 else [])
    *qp_out, small = att_state
    qp_parts, late = reduce_weight(small, *qp_out)
    d_q_gain = late[0, :inner].reshape(heads, size)
    d_k_gain = late[0, inner : 2 * inner].reshape(heads, size)
    d_bias_one = late[1]
    both = late[2:4]
    both = both + swap(both, "tp", 1)
    both = both + swap(both, "tp", 2)
    d_bias_two = both[0]
    d_ln_gain = both[1] / ln_gain

    d_fc1, d_fc2 = fc[:width].astype(F32), fc[width:].astype(F32)
    d_qkv_t, d_proj = join(qp_parts, [(joined, width), (inner, width)])
    d_qkv = d_qkv_t.T

    def finish(begin, end, earlier):
        block = pl.BlockSpec((1, rows, width), lambda i: (begin + i, 0, 0))
        vector = pl.BlockSpec((width,), lambda i: (0,))
        first = pl.BlockSpec((2 * rows, width), lambda i: (0, 0))
        ins = keeps[3 * begin : 3 * end]
        return pl.pallas_call(
            functools.partial(final_kernel, end - begin),
            grid=(end - begin,),
            out_shape=[
                jax.ShapeDtypeStruct((images, rows, width), BF16),
                jax.ShapeDtypeStruct((images, rows, width), F32),
            ],
            in_specs=[block, block, vector, vector] + [first] * len(ins) + [ANY_SPEC] * len(earlier),
            out_specs=[block, block],
            input_output_aliases={4 + len(ins) + k: k for k in range(len(earlier))},
        )(tokens, d_out, ln_gain, b_fc2, *ins, *earlier)

    results = finish(0, images - 1, [])
    output, d_tokens = finish(images - 1, images, results)
    return (output, d_tokens, d_ln_gain, d_qkv, d_q_gain, d_k_gain, d_proj, d_fc1, d_bias_one, d_fc2, d_bias_two)


def solution(mesh):
    rows = P("dp", "tp", None)
    wide = P(None, "tp")
    tall = P("tp", None)
    return jax.shard_map(
        functools.partial(block, mesh.shape["dp"], mesh.shape["tp"]),
        mesh=mesh,
        in_specs=(rows, P("dp"), P(), wide, tall, tall, tall, wide, P("tp"), tall, P(), rows),
        out_specs=(rows, rows, P(), wide, tall, tall, tall, wide, P("tp"), tall, P()),
        check_vma=False,
    )
```

```python
import functools
import math

import jax
import jax.numpy as jnp
from jax import lax
from jax.experimental import pallas as pl
from jax.experimental.pallas import tpu as pltpu
from jax.sharding import PartitionSpec as P


EPS = 1e-06
F32 = jnp.float32
BF16 = jnp.bfloat16
NN = (((1,), (0,)), ((), ()))
NT = (((1,), (1,)), ((), ()))
TN = (((0,), (0,)), ((), ()))
VMEM_SPEC = pl.BlockSpec(memory_space=pltpu.VMEM)
ANY_SPEC = pl.BlockSpec(memory_space=pl.ANY)
SMEM_SPEC = pl.BlockSpec(memory_space=pltpu.SMEM)


def mm(a, b, dims=NN):
    return lax.dot_general(a, b, dims, preferred_element_type=F32)


def call(kernel, outs, n_smem, *args, n_any=0, any_outs=0, scratch=(), flops=0):
    in_specs = [SMEM_SPEC] * n_smem + [ANY_SPEC] * n_any + [VMEM_SPEC] * (len(args) - n_smem - n_any)
    moved = sum(a.size * a.dtype.itemsize for a in args)
    moved += sum(math.prod(s) * jnp.dtype(d).itemsize for s, d in outs)
    return pl.pallas_call(
        kernel,
        out_shape=[jax.ShapeDtypeStruct(s, d) for s, d in outs],
        in_specs=in_specs,
        out_specs=[ANY_SPEC] * any_outs + [VMEM_SPEC] * (len(outs) - any_outs),
        scratch_shapes=list(scratch),
        compiler_params=pltpu.CompilerParams(vmem_limit_bytes=60 * 1024 * 1024),
        cost_estimate=pl.CostEstimate(flops=flops, transcendentals=0, bytes_accessed=moved),
    )(*args)


def norm_kernel(begin, tokens, d_out, gain_ref, *refs):
    out_refs, (held, sem, sem_out) = refs[:-3], refs[-3:]
    rows = tokens.shape[1]
    reads, copies = [], []
    for i, out in enumerate(out_refs):
        reads.append(pltpu.make_async_copy(tokens.at[begin + i], held.at[i], sem.at[i]))
        reads[-1].start()
    for i, out in enumerate(out_refs):
        copies.append(pltpu.make_async_copy(d_out.at[begin + i], out.at[pl.ds(rows, rows)], sem_out.at[i]))
        copies[-1].start()
    for i, out in enumerate(out_refs):
        reads[i].wait()
        v = held[i].astype(F32)
        c = v - jnp.mean(v, axis=-1, keepdims=True)
        r = lax.rsqrt(jnp.mean(c * c, axis=-1, keepdims=True) + EPS)
        out[0:rows] = (c * r * gain_ref[...].reshape(1, -1)).astype(BF16)
    for copy in copies:
        copy.wait()


def as_row(column):
    return jnp.broadcast_to(column, (column.shape[0], 128)).T[0:1]


def emit_halves(acc, pos, keep, send):
    half = acc.shape[0] // 2
    keep[...] = acc[pl.ds(pl.multiple_of(pos[0] * half, half), half), :]
    send[0:half] = acc[pl.ds(pl.multiple_of((1 - pos[0]) * half, half), half), :].astype(BF16)


def ff_kernel(first, last, blocks, owned, *refs):
    refs = list(refs)
    take = lambda n: [refs.pop(0) for _ in range(n)]
    packs = take(blocks)
    weights = take(3)
    prior = [] if first else take(2)
    o_ff, n_ff = take(2)
    if last:
        summed, accb = take(2)
    else:
        acc, accb = take(2)
    buf, w1, w2, b1, o_s, n_s, sem, weight_sem, prior_sem, o_sem, n_sem = take(11)
    if last:
        (acc,) = take(1)
    rows = packs[0].shape[0] // 2
    width = w1.shape[0]
    inv_sqrt2 = 2.0**-0.5

    def fetch(j, slot):
        return pltpu.make_async_copy(packs[j], buf.at[slot], sem.at[slot])

    def writes(k, slot):
        at = pl.ds(pl.multiple_of(k * rows, rows), rows)
        return (
            pltpu.make_async_copy(o_s.at[slot], o_ff.at[at], o_sem.at[slot]),
            pltpu.make_async_copy(n_s.at[slot], n_ff.at[at], n_sem.at[slot]),
        )

    fetch(0, 0).start()
    loads = [pltpu.make_async_copy(weights[j], to, weight_sem.at[j]) for j, to in enumerate((w1, w2, b1))]
    for load in loads:
        load.start()
    held = [pltpu.make_async_copy(prior[j], to, prior_sem.at[j]) for j, to in enumerate((acc, accb))] if prior else []
    for copy in held:
        copy.start()
    if not prior:
        acc[...] = jnp.zeros(acc.shape, F32)
        accb[...] = jnp.zeros(accb.shape, F32)
    for load in loads:
        load.wait()

    def step(k, carry):
        slot = k & 1
        fetch(0, slot).wait()
        for j in range(1, blocks):

            @pl.when(k + 1 == j)
            def _(j=j):
                fetch(j, 1 - slot).start()

        @pl.when(k >= 2)
        def _():
            for write in writes(k - 2, slot):
                write.wait()

        x = buf[slot, 0:rows]
        g = buf[slot, rows : 2 * rows]
        h = mm(x, w1[...]) + b1[...].reshape(1, -1)
        da = mm(g, w2[...], NT)
        cdf = 0.5 * (1.0 + lax.erf(h * inv_sqrt2))
        pdf = jnp.exp(-0.5 * h * h) * (1.0 / math.sqrt(2.0 * math.pi))
        act = (h * cdf).astype(BF16)
        dh = (da * (cdf + h * pdf)).astype(BF16)
        o_s[slot] = mm(act, w2[...]).astype(BF16)
        n_s[slot] = mm(dh, w1[...], NT).astype(BF16)
        for write in writes(k, slot):
            write.start()
        if prior:

            @pl.when(k == 0)
            def _():
                for copy in held:
                    copy.wait()

        accb[0:1] += jnp.sum(dh.astype(F32), axis=0, keepdims=True)
        if owned:

            @pl.when(k % 2 == 0)
            def _():
                accb[1:2] += jnp.sum(g.astype(F32), axis=0, keepdims=True)

        acc[0:width] += mm(x, dh, TN)
        acc[width:] += mm(act, g, TN)
        return carry

    lax.fori_loop(0, blocks, step, 0)
    if last:
        accb[2:3] = as_row(jnp.sum(w1[...].astype(F32) * acc[0:width], axis=1, keepdims=True))
        summed[...] = acc[...].astype(BF16)
    for k in range(blocks - 2, blocks):
        for write in writes(k, k & 1):
            write.wait()


def att_kernel(first, last, blocks, heads, size, starts, *refs):
    refs = list(refs)
    take = lambda n: [refs.pop(0) for _ in range(n)]
    length, pos, x_bit = take(3)
    parts = take(blocks)
    ff_parts = take(4)
    prior = [] if first else take(1)
    weights = take(4)
    prior_gain = [] if first else take(1)
    ff_small_in = take(1) if last else []
    keep_near, keep_far, send = take(3)
    if last:
        pieces = take(len(refs) - 34)
        (small,) = take(1)
    else:
        acc, accg = take(2)
    jt, dot_s, qs_t, qt_s, k_s, kt_s, v_s, vt_s, es, dqt, dk, dv, ot, djt = take(14)
    ff_s, ff_sem, prior_sem, out_s, out_sem, dot_bs, r_s, pack_s, pack_sem = take(9)
    wqkv, wproj, qg, kg, gain_s, small_s, weight_sem, tail_sem = take(8)
    if last:
        acc, accg = take(2)
    rows = parts[0].shape[0] // 2
    joined = wqkv.shape[0]
    total = rows * blocks
    scale = size**-0.5
    up = scale * math.log2(math.e)
    loads = [pltpu.make_async_copy(weights[j], to, weight_sem.at[j]) for j, to in enumerate((wqkv, wproj, qg, kg))]
    for load in loads[:2]:
        load.start()
    for k in range(blocks):
        pltpu.make_async_copy(parts[k], pack_s.at[k], pack_sem.at[k]).start()
    for load in loads[2:]:
        load.start()
    for load in loads[:2]:
        load.wait()

    def project(k, carry):
        pltpu.make_async_copy(parts[0], pack_s.at[k], pack_sem.at[k]).wait()
        cols = pl.ds(pl.multiple_of(k * rows, rows), rows)
        jt[:, cols] = mm(wqkv[...], pack_s[k, 0:rows], NT)
        dot_s[:, cols] = mm(wproj[...], pack_s[k, rows : 2 * rows], NT)
        return carry

    lax.fori_loop(0, blocks, project, 0)
    for load in loads[2:]:
        load.wait()
    later = [pltpu.make_async_copy(source, gain_s, tail_sem.at[0]) for source in prior_gain]
    later += [pltpu.make_async_copy(source, small_s, tail_sem.at[1]) for source in ff_small_in]
    for copy in later:
        copy.start()
    for k in range(4):
        rows_of = pl.ds(starts[k // 2], 2 * rows)
        later.append(pltpu.make_async_copy(ff_parts[k].at[rows_of], ff_s.at[k % 2, k // 2], ff_sem.at[k]))
        later[-1].start()
    if prior:
        later.append(pltpu.make_async_copy(prior[0], acc, prior_sem))
        later[-1].start()
    else:
        acc[...] = jnp.zeros(acc.shape, F32)

    def normed(u):
        c = u - jnp.mean(u, axis=0, keepdims=True)
        r = lax.rsqrt(jnp.mean(c * c, axis=0, keepdims=True) + EPS)
        return c * r, r

    ones = jnp.concatenate(
        [jnp.ones((1, rows), F32), jnp.zeros((15, rows), F32)], axis=0
    ).astype(BF16)

    def prepare(h, carry):
        base = pl.multiple_of(h * 3 * size, size)
        gh = pl.ds(pl.multiple_of(h * size, size), size)
        part = lambda c: jt[pl.ds(pl.multiple_of(base + c * size, size), size), :]
        qt = normed(part(0))[0] * qg[gh, :]
        kt = normed(part(1))[0] * kg[gh, :]
        vt = part(2)
        qs_t[h] = (qt * up).astype(BF16)
        qt_s[h] = qt.astype(BF16)
        k_s[h] = kt.T.astype(BF16)
        v_s[h] = vt.T.astype(BF16)
        for k in range(blocks):
            cols = slice(k * rows, (k + 1) * rows)
            kt_s[h, k] = kt[:, cols].astype(BF16)
            vt_s[h, k, 0:size] = vt[:, cols].astype(BF16)
            vt_s[h, k, size : size + 16] = ones
        return carry

    lax.fori_loop(0, heads, prepare, 0)

    live = length[0]
    count = (live + rows - 1) // rows

    dk[...] = jnp.zeros(dk.shape, F32)
    dv[...] = jnp.zeros(dv.shape, F32)

    def forward(j, accs):
        b = j ^ pos[0]
        start = pl.multiple_of(b * rows, rows)
        slot = lax.broadcasted_iota(jnp.int32, (rows, 1), 0) + j * rows
        out = []
        for h in range(heads):
            s = mm(k_s[h, pl.ds(start, rows), :], qs_t[h])
            e = jnp.where(slot < live, jnp.exp2(s), 0.0).astype(BF16)
            es[h, b] = e
            out.append(accs[h] + mm(vt_s[h, b], e))
        return tuple(out)

    zero = jnp.zeros((size + 16, total), F32)
    accs = lax.fori_loop(0, count, forward, (zero,) * heads)
    for h in range(heads):
        inv = 1.0 / accs[h][size : size + 1]
        o = accs[h][0:size] * inv
        hs = slice(h * size, (h + 1) * size)
        ot[hs] = o.astype(BF16)
        dot_b = (dot_s[hs] * inv).astype(BF16)
        dot_bs[hs] = dot_b
        r_s[h : h + 1] = jnp.sum(dot_b.astype(F32) * o, axis=0, keepdims=True)

    def backward(j, accs):
        b = j ^ pos[0]
        start = pl.multiple_of(b * rows, rows)
        out = []
        for h in range(heads):
            dot_b = dot_bs[h * size : (h + 1) * size]
            dp = mm(v_s[h, pl.ds(start, rows), :], dot_b)
            e = es[h, b]
            ds = (e.astype(F32) * (dp - r_s[h : h + 1])).astype(BF16)
            dv[h, b] = mm(dot_b, e, NT)
            dk[h, b] = mm(qt_s[h], ds, NT)
            out.append(accs[h] + mm(kt_s[h, b], ds))
        return tuple(out)

    zero = jnp.zeros((size, total), F32)
    accs = lax.fori_loop(0, count, backward, (zero,) * heads)
    for h in range(heads):
        dqt[h] = accs[h]

    def undo(h, carry):
        base = pl.multiple_of(h * 3 * size, size)
        gh = pl.multiple_of(h * size, size)
        for c, gain, grad in ((0, qg, dqt[h]), (1, kg, jnp.concatenate([dk[h, k] for k in range(blocks)], axis=1))):
            at = pl.ds(pl.multiple_of(base + c * size, size), size)
            n, r = normed(jt[at, :])
            grad = grad * scale
            y = grad * gain[pl.ds(gh, size), :]
            back = r * (
                y
                - jnp.mean(y, axis=0, keepdims=True)
                - n * jnp.mean(y * n, axis=0, keepdims=True)
            )
            djt[at, :] = back.astype(BF16)
            accg[pl.ds(pl.multiple_of(c * heads * size + gh, size), size), :] = jnp.sum(grad * n, axis=1, keepdims=True)
        values = jnp.concatenate([dv[h, k] for k in range(blocks)], axis=1)
        djt[pl.ds(pl.multiple_of(base + 2 * size, size), size), :] = values.astype(BF16)
        return carry

    lax.fori_loop(0, heads, undo, 0)
    for copy in later:
        copy.wait()
    if prior:
        accg[...] += gain_s[...]

    targets = [keep_near, send.at[pl.ds(0, 2 * rows)], keep_far, send.at[pl.ds(2 * rows, 2 * rows)]]
    writes = [pltpu.make_async_copy(out_s.at[k], targets[k], out_sem.at[k]) for k in range(blocks)]

    def give(k, carry):
        cols = pl.ds(pl.multiple_of(k * rows, rows), rows)
        part = pl.ds(pl.multiple_of((k & 1) * rows, rows), rows)
        n = ff_s[1, k >> 1, part, :].astype(F32) + mm(djt[:, cols], wqkv[...], TN)
        o = ff_s[0, k >> 1, part, :].astype(F32) + mm(ot[:, cols], wproj[...], TN)
        out_s[k, 0:rows] = o.astype(BF16)
        out_s[k, rows : 2 * rows] = n.astype(BF16)
        acc[0:joined] += mm(djt[:, cols], pack_s[k, 0:rows])
        acc[joined:] += mm(ot[:, cols], pack_s[k, rows : 2 * rows])
        for j in range(blocks):

            @pl.when(k == j)
            def _(j=j):
                writes[j].start()

        return carry

    lax.fori_loop(0, blocks, give, 0)
    if last:
        ln = jnp.sum(wqkv[...].astype(F32) * acc[0:joined], axis=0, keepdims=True) + small_s[2:3]
        gain_row = as_row(accg[...])
        pad = jnp.zeros((1, ln.shape[1] - gain_row.shape[1]), F32)
        lines = [jnp.concatenate([gain_row, pad], axis=1), small_s[0:2], ln, jnp.zeros((4, ln.shape[1]), F32)]
        small[...] = jnp.concatenate(lines, axis=0).astype(BF16)
        emit_halves(acc, x_bit, *pieces)
        half = pieces[0].shape[0]
        pieces[1][half : half + 8] = small[...]
    for write in writes:
        write.wait()


def final_kernel(images, *refs):
    tokens, d_out, gain, bias = refs[:4]
    ins = refs[4 : 4 + 3 * images]
    out, d_tokens = refs[-2:]
    rows = tokens.shape[1]
    for i in range(images):

        @pl.when(pl.program_id(0) == i)
        def _(i=i):
            keep, near, far = ins[3 * i : 3 * i + 3]
            both = [
                keep[at].astype(F32) + near[at].astype(F32) + far[at].astype(F32)
                for at in (slice(0, rows), slice(rows, 2 * rows))
            ]
            v = tokens[0].astype(F32)
            c = v - jnp.mean(v, axis=-1, keepdims=True)
            r = lax.rsqrt(jnp.mean(c * c, axis=-1, keepdims=True) + EPS)
            xhat = c * r
            out[0] = (v + both[0] + bias[...].reshape(1, -1)).astype(BF16)
            z = both[1] * gain[...].reshape(1, -1)
            back = r * (
                z
                - jnp.mean(z, axis=-1, keepdims=True)
                - xhat * jnp.mean(z * xhat, axis=-1, keepdims=True)
            )
            d_tokens[0] = d_out[0].astype(F32) + back


def join_kernel(n, *refs):
    pos, own, across, rest = refs[0], refs[1 : 1 + n], refs[1 + n], refs[2 + n]
    one, two, whole = refs[3 + n :]
    step = own[0].shape[0]
    half = step * n
    for k in range(n):
        z = pos[1] ^ k
        at = pl.multiple_of(pos[0] * half + z * step, step)
        whole[pl.ds(at, step), :] = own[k][...].astype(F32)
        at = pl.multiple_of((1 - pos[0]) * half + z * step, step)
        far = across[...] if k == 0 else rest[(k - 1) * step : k * step]
        whole[pl.ds(at, step), :] = far.astype(F32)
    cut = one.shape[0]
    one[...] = whole[0:cut]
    two[...] = whole[cut:]


def block(dp_size, tp_size, *args):
    (tokens, lengths, ln_gain, w_qkv, q_gain, k_gain, w_proj, w_fc1, b_fc1, w_fc2, b_fc2, d_out) = args
    images, rows, width = tokens.shape
    heads, size = q_gain.shape
    hidden = w_fc1.shape[1]
    total = rows * tp_size
    blocks = tp_size
    joined = heads * 3 * size
    inner = heads * size
    n = dp_size // 2
    t = lax.axis_index("tp").astype(jnp.int32)
    d = lax.axis_index("dp").astype(jnp.int32)
    x, z = d & 1, d >> 1

    def swap(v, axis, mask):
        count = tp_size if axis == "tp" else dp_size
        return lax.ppermute(v, axis, [(i, i ^ mask) for i in range(count)])

    def after(v, dep):
        return lax.optimization_barrier((v, dep))[0]

    def norm(begin, end):
        count = end - begin
        return call(
            functools.partial(norm_kernel, begin), [((2 * rows, width), BF16)] * count, 0,
            tokens, d_out, ln_gain, n_any=2,
            scratch=[
                pltpu.VMEM((count, rows, width), BF16),
                pltpu.SemaphoreType.DMA((count,)),
                pltpu.SemaphoreType.DMA((count,)),
            ],
        )

    own = norm(0, images)
    far = [swap(v, "tp", 2) for v in own]
    near = [swap(v, "tp", 1) for v in own]
    cross = [None] * images

    def forward(i, dep):
        cross[i] = swap(after(far[i], dep), "tp", 1)

    b1 = b_fc1
    pos = jnp.stack([x, z])

    half = (joined + inner) // 2
    qp_pieces = [((half, width), F32), ((half + 8, width), BF16)]

    def ff(first, last, packs, state):
        count = len(packs)
        outs = [((count * rows, width), BF16)] * 2
        scratch = [
            pltpu.VMEM((2, 2 * rows, width), BF16),
            pltpu.VMEM((width, hidden), BF16),
            pltpu.VMEM((hidden, width), BF16),
            pltpu.VMEM((hidden,), F32),
            pltpu.VMEM((2, rows, width), BF16),
            pltpu.VMEM((2, rows, width), BF16),
            pltpu.SemaphoreType.DMA((2,)),
            pltpu.SemaphoreType.DMA((3,)),
            pltpu.SemaphoreType.DMA((2,)),
            pltpu.SemaphoreType.DMA((2,)),
            pltpu.SemaphoreType.DMA((2,)),
        ]
        if last:
            outs += [((width + hidden, width), BF16), ((8, width), F32)]
            scratch += [pltpu.VMEM((width + hidden, width), F32)]
        else:
            outs += [((width + hidden, width), F32), ((8, width), F32)]
        res = call(
            functools.partial(ff_kernel, first, last, count, first), outs, 0,
            *packs, w_fc1, w_fc2, b1, *state, n_any=count + 3 + len(state), any_outs=2,
            scratch=scratch, flops=12 * count * rows * width * hidden,
        )
        return res[0], res[1], res[2:]

    qg = q_gain.reshape(-1, 1)
    kg = k_gain.reshape(-1, 1)
    w_t = w_qkv.T
    keeps = []

    def att(i, ff_parts, starts, state, ff_small=()):
        first, last = i == 0, i == images - 1
        outs = [((2 * rows, width), BF16)] * 2 + [((4 * rows, width), BF16)]
        scratch = [
            pltpu.VMEM((joined, total), F32),
            pltpu.VMEM((inner, total), F32),
            pltpu.VMEM((heads, size, total), BF16),
            pltpu.VMEM((heads, size, total), BF16),
            pltpu.VMEM((heads, total, size), BF16),
            pltpu.VMEM((heads, blocks, size, rows), BF16),
            pltpu.VMEM((heads, total, size), BF16),
            pltpu.VMEM((heads, blocks, size + 16, rows), BF16),
            pltpu.VMEM((heads, blocks, rows, total), BF16),
            pltpu.VMEM((heads, size, total), F32),
            pltpu.VMEM((heads, blocks, size, rows), F32),
            pltpu.VMEM((heads, blocks, size, rows), F32),
            pltpu.VMEM((inner, total), BF16),
            pltpu.VMEM((joined, total), BF16),
            pltpu.VMEM((2, 2, 2 * rows, width), BF16),
            pltpu.SemaphoreType.DMA((4,)),
            pltpu.SemaphoreType.DMA,
            pltpu.VMEM((blocks, 2 * rows, width), BF16),
            pltpu.SemaphoreType.DMA((blocks,)),
            pltpu.VMEM((inner, total), BF16),
            pltpu.VMEM((8, total), F32),
            pltpu.VMEM((blocks, 2 * rows, width), BF16),
            pltpu.SemaphoreType.DMA((blocks,)),
            pltpu.VMEM((joined, width), BF16),
            pltpu.VMEM((inner, width), BF16),
            pltpu.VMEM((inner, 1), F32),
            pltpu.VMEM((inner, 1), F32),
            pltpu.VMEM((2 * inner, 1), F32),
            pltpu.VMEM((8, width), F32),
            pltpu.SemaphoreType.DMA((4,)),
            pltpu.SemaphoreType.DMA((2,)),
        ]
        if last:
            outs += qp_pieces + [((8, width), BF16)]
            scratch += [pltpu.VMEM((joined + inner, width), F32), pltpu.VMEM((2 * inner, 1), F32)]
        else:
            outs += [((joined + inner, width), F32), ((2 * inner, 1), F32)]
        res = call(
            functools.partial(att_kernel, first, last, blocks, heads, size, starts), outs, 3,
            lengths[i : i + 1], t[None], x[None], own[i], near[i], far[i], cross[i], *ff_parts, *state[:1],
            w_t, w_proj, qg, kg, *state[1:], *ff_small, n_any=blocks + 8 + len(state) + len(ff_small), any_outs=3,
            scratch=scratch,
            flops=6 * 8 * heads * total * total * size + 8 * total * width * (joined + inner),
        )
        keep_near, keep_far, send = res[:3]
        got = swap(send, "tp", 1)
        summed = (keep_far.astype(F32) + got[2 * rows :].astype(F32)).astype(BF16)
        keeps.extend([keep_near, got, swap(summed, "tp", 2)])
        return res[3:]

    def reduce_weight(small, keep, send):
        extra = small.shape[0]
        got = swap(send, "dp", 1)
        half = keep + got[:-extra].astype(F32)
        small = (small.astype(F32) + got[-extra:].astype(F32)).astype(BF16)
        step = keep.shape[0] // n
        piece = lambda k: lax.dynamic_slice_in_dim(half, (z ^ k) * step, step, 0)
        done = piece(0)
        smalls = [small]
        for k in range(1, n):
            got = swap(jnp.concatenate([piece(k).astype(BF16), small], axis=0), "dp", 2 * k)
            done = done + got[:-extra].astype(F32)
            smalls.append(got[-extra:])
        done = done.astype(BF16)
        smalls = jnp.stack(smalls).astype(F32)
        small = sum(lax.dynamic_index_in_dim(smalls, z ^ k, 0, keepdims=False) for k in range(n))
        near = [swap(done, "dp", 2 * k) for k in range(1, n)]
        across = swap(done, "dp", 1)
        rest = swap(jnp.concatenate(near, axis=0), "dp", 1)
        return [done] + near + [across, rest], small

    def join(parts, shapes):
        return call(
            functools.partial(join_kernel, n), [(s, F32) for s in shapes], 1, pos, *parts,
            scratch=[pltpu.VMEM((joined + inner, width), F32)],
        )

    a_parts = ff(True, False, [b for i in range(images) for b in (own[i], near[i])], [])
    forward(0, a_parts[0])
    b_parts = ff(False, False, [far[0], cross[0]], a_parts[2])
    forward(1, b_parts[0])
    att_state = att(0, a_parts[:2] + b_parts[:2], (0, 0), [])
    for i in range(2, images):
        forward(i, att_state[1])
    c_parts = ff(False, True, [b for i in range(1, images) for b in (far[i], cross[i])], b_parts[2])
    state = c_parts[2]
    ff_out, ff_small = state
    fc = lax.psum(ff_out, "dp")
    for i in range(1, images):
        starts = (2 * rows * i, 2 * rows * (i - 1))
        att_state = att(i, a_parts[:2] + c_parts[:2], starts, att_state, [ff_small] if i == images - 1 else [])
    *qp_out, small = att_state
    qp_parts, late = reduce_weight(small, *qp_out)
    d_q_gain = late[0, :inner].reshape(heads, size)
    d_k_gain = late[0, inner : 2 * inner].reshape(heads, size)
    d_bias_one = late[1]
    both = late[2:4]
    both = both + swap(both, "tp", 1)
    both = both + swap(both, "tp", 2)
    d_bias_two = both[0]
    d_ln_gain = both[1] / ln_gain

    d_fc1, d_fc2 = fc[:width].astype(F32), fc[width:].astype(F32)
    d_qkv_t, d_proj = join(qp_parts, [(joined, width), (inner, width)])
    d_qkv = d_qkv_t.T

    def finish(begin, end, earlier):
        block = pl.BlockSpec((1, rows, width), lambda i: (begin + i, 0, 0))
        vector = pl.BlockSpec((width,), lambda i: (0,))
        first = pl.BlockSpec((2 * rows, width), lambda i: (0, 0))
        ins = keeps[3 * begin : 3 * end]
        return pl.pallas_call(
            functools.partial(final_kernel, end - begin),
            grid=(end - begin,),
            out_shape=[
                jax.ShapeDtypeStruct((images, rows, width), BF16),
                jax.ShapeDtypeStruct((images, rows, width), F32),
            ],
            in_specs=[block, block, vector, vector] + [first] * len(ins) + [ANY_SPEC] * len(earlier),
            out_specs=[block, block],
            input_output_aliases={4 + len(ins) + k: k for k in range(len(earlier))},
        )(tokens, d_out, ln_gain, b_fc2, *ins, *earlier)

    results = finish(0, images - 1, [])
    output, d_tokens = finish(images - 1, images, results)
    return (output, d_tokens, d_ln_gain, d_qkv, d_q_gain, d_k_gain, d_proj, d_fc1, d_bias_one, d_fc2, d_bias_two)


def solution(mesh):
    rows = P("dp", "tp", None)
    wide = P(None, "tp")
    tall = P("tp", None)
    return jax.shard_map(
        functools.partial(block, mesh.shape["dp"], mesh.shape["tp"]),
        mesh=mesh,
        in_specs=(rows, P("dp"), P(), wide, tall, tall, tall, wide, P("tp"), tall, P(), rows),
        out_specs=(rows, rows, P(), wide, tall, tall, tall, wide, P("tp"), tall, P()),
        check_vma=False,
    )
```

```python
import functools
import math

import jax
import jax.numpy as jnp
from jax import lax
from jax.experimental import pallas as pl
from jax.experimental.pallas import tpu as pltpu
from jax.sharding import PartitionSpec as P


EPS = 1e-06
F32 = jnp.float32
BF16 = jnp.bfloat16
NN = (((1,), (0,)), ((), ()))
NT = (((1,), (1,)), ((), ()))
TN = (((0,), (0,)), ((), ()))
VMEM_SPEC = pl.BlockSpec(memory_space=pltpu.VMEM)
ANY_SPEC = pl.BlockSpec(memory_space=pl.ANY)
SMEM_SPEC = pl.BlockSpec(memory_space=pltpu.SMEM)


def mm(a, b, dims=NN):
    return lax.dot_general(a, b, dims, preferred_element_type=F32)


def call(kernel, outs, n_smem, *args, n_any=0, any_outs=0, scratch=(), flops=0):
    in_specs = [SMEM_SPEC] * n_smem + [ANY_SPEC] * n_any + [VMEM_SPEC] * (len(args) - n_smem - n_any)
    moved = sum(a.size * a.dtype.itemsize for a in args)
    moved += sum(math.prod(s) * jnp.dtype(d).itemsize for s, d in outs)
    return pl.pallas_call(
        kernel,
        out_shape=[jax.ShapeDtypeStruct(s, d) for s, d in outs],
        in_specs=in_specs,
        out_specs=[ANY_SPEC] * any_outs + [VMEM_SPEC] * (len(outs) - any_outs),
        scratch_shapes=list(scratch),
        compiler_params=pltpu.CompilerParams(vmem_limit_bytes=60 * 1024 * 1024),
        cost_estimate=pl.CostEstimate(flops=flops, transcendentals=0, bytes_accessed=moved),
    )(*args)


def norm_kernel(begin, tokens, d_out, gain_ref, *refs):
    out_refs, (held, sem, sem_out) = refs[:-3], refs[-3:]
    rows = tokens.shape[1]
    reads, copies = [], []
    for i, out in enumerate(out_refs):
        reads.append(pltpu.make_async_copy(tokens.at[begin + i], held.at[i], sem.at[i]))
        reads[-1].start()
    for i, out in enumerate(out_refs):
        copies.append(pltpu.make_async_copy(d_out.at[begin + i], out.at[pl.ds(rows, rows)], sem_out.at[i]))
        copies[-1].start()
    for i, out in enumerate(out_refs):
        reads[i].wait()
        v = held[i].astype(F32)
        c = v - jnp.mean(v, axis=-1, keepdims=True)
        r = lax.rsqrt(jnp.mean(c * c, axis=-1, keepdims=True) + EPS)
        out[0:rows] = (c * r * gain_ref[...].reshape(1, -1)).astype(BF16)
    for copy in copies:
        copy.wait()


def as_row(column):
    return jnp.broadcast_to(column, (column.shape[0], 128)).T[0:1]


def emit_halves(acc, pos, keep, send):
    half = acc.shape[0] // 2
    keep[...] = acc[pl.ds(pl.multiple_of(pos[0] * half, half), half), :]
    send[0:half] = acc[pl.ds(pl.multiple_of((1 - pos[0]) * half, half), half), :].astype(BF16)


def ff_kernel(first, last, blocks, owned, *refs):
    refs = list(refs)
    take = lambda n: [refs.pop(0) for _ in range(n)]
    packs = take(blocks)
    weights = take(3)
    prior = [] if first else take(2)
    o_ff, n_ff = take(2)
    if last:
        summed, accb = take(2)
    else:
        acc, accb = take(2)
    buf, w1, w2, b1, o_s, n_s, sem, weight_sem, prior_sem, o_sem, n_sem = take(11)
    if last:
        acc, sum_s, sum_sem = take(3)
    rows = packs[0].shape[0] // 2
    width = w1.shape[0]
    inv_sqrt2 = 2.0**-0.5

    def fetch(j, slot):
        return pltpu.make_async_copy(packs[j], buf.at[slot], sem.at[slot])

    def writes(k, slot):
        at = pl.ds(pl.multiple_of(k * rows, rows), rows)
        return (
            pltpu.make_async_copy(o_s.at[slot], o_ff.at[at], o_sem.at[slot]),
            pltpu.make_async_copy(n_s.at[slot], n_ff.at[at], n_sem.at[slot]),
        )

    fetch(0, 0).start()
    loads = [pltpu.make_async_copy(weights[j], to, weight_sem.at[j]) for j, to in enumerate((w1, w2, b1))]
    for load in loads:
        load.start()
    held = [pltpu.make_async_copy(prior[j], to, prior_sem.at[j]) for j, to in enumerate((acc, accb))] if prior else []
    for copy in held:
        copy.start()
    if not prior:
        acc[...] = jnp.zeros(acc.shape, F32)
        accb[...] = jnp.zeros(accb.shape, F32)
    for load in loads:
        load.wait()

    def step(k, carry):
        slot = k & 1
        fetch(0, slot).wait()
        for j in range(1, blocks):

            @pl.when(k + 1 == j)
            def _(j=j):
                fetch(j, 1 - slot).start()

        @pl.when(k >= 2)
        def _():
            for write in writes(k - 2, slot):
                write.wait()

        x = buf[slot, 0:rows]
        g = buf[slot, rows : 2 * rows]
        h = mm(x, w1[...]) + b1[...].reshape(1, -1)
        da = mm(g, w2[...], NT)
        cdf = 0.5 * (1.0 + lax.erf(h * inv_sqrt2))
        pdf = jnp.exp(-0.5 * h * h) * (1.0 / math.sqrt(2.0 * math.pi))
        act = (h * cdf).astype(BF16)
        dh = (da * (cdf + h * pdf)).astype(BF16)
        o_s[slot] = mm(act, w2[...]).astype(BF16)
        n_s[slot] = mm(dh, w1[...], NT).astype(BF16)
        for write in writes(k, slot):
            write.start()
        if prior:

            @pl.when(k == 0)
            def _():
                for copy in held:
                    copy.wait()

        accb[0:1] += jnp.sum(dh.astype(F32), axis=0, keepdims=True)
        if owned:

            @pl.when(k % 2 == 0)
            def _():
                accb[1:2] += jnp.sum(g.astype(F32), axis=0, keepdims=True)

        acc[0:width] += mm(x, dh, TN)
        acc[width:] += mm(act, g, TN)
        return carry

    lax.fori_loop(0, blocks, step, 0)
    if last:
        sum_s[...] = acc[...].astype(BF16)
        out = pltpu.make_async_copy(sum_s, summed, sum_sem)
        out.start()
        accb[2:3] = as_row(jnp.sum(w1[...].astype(F32) * acc[0:width], axis=1, keepdims=True))
        out.wait()
    for k in range(blocks - 2, blocks):
        for write in writes(k, k & 1):
            write.wait()


def att_kernel(first, last, blocks, heads, size, starts, *refs):
    refs = list(refs)
    take = lambda n: [refs.pop(0) for _ in range(n)]
    length, pos, x_bit = take(3)
    parts = take(blocks)
    ff_parts = take(4)
    prior = [] if first else take(1)
    weights = take(4)
    prior_gain = [] if first else take(1)
    ff_small_in = take(1) if last else []
    keep_near, keep_far, send = take(3)
    if last:
        pieces = take(len(refs) - 36)
        (small,) = take(1)
    else:
        acc, accg = take(2)
    jt, dot_s, qs_t, qt_s, k_s, kt_s, v_s, vt_s, es, dqt, dk, dv, ot, djt = take(14)
    ff_s, ff_sem, prior_sem, out_s, out_sem, dot_bs, r_s, pack_s, pack_sem = take(9)
    wqkv, wproj, qg, kg, gain_s, small_s, weight_sem, tail_sem, o_acc, inv_s = take(10)
    if last:
        acc, accg = take(2)
    rows = parts[0].shape[0] // 2
    joined = wqkv.shape[0]
    scale = size**-0.5
    up = scale * math.log2(math.e)
    loads = [pltpu.make_async_copy(weights[j], to, weight_sem.at[j]) for j, to in enumerate((wqkv, wproj, qg, kg))]
    for load in loads[:2]:
        load.start()
    for k in range(blocks):
        pltpu.make_async_copy(parts[k], pack_s.at[k], pack_sem.at[k]).start()
    for load in loads[2:]:
        load.start()
    for load in loads[:2]:
        load.wait()

    def project(k, carry):
        pltpu.make_async_copy(parts[0], pack_s.at[k], pack_sem.at[k]).wait()
        cols = pl.ds(pl.multiple_of(k * rows, rows), rows)
        jt[:, cols] = mm(wqkv[...], pack_s[k, 0:rows], NT)
        dot_s[:, cols] = mm(wproj[...], pack_s[k, rows : 2 * rows], NT)
        return carry

    lax.fori_loop(0, blocks, project, 0)
    for load in loads[2:]:
        load.wait()
    later = [pltpu.make_async_copy(source, gain_s, tail_sem.at[0]) for source in prior_gain]
    later += [pltpu.make_async_copy(source, small_s, tail_sem.at[1]) for source in ff_small_in]
    for copy in later:
        copy.start()
    for k in range(4):
        rows_of = pl.ds(starts[k // 2], 2 * rows)
        later.append(pltpu.make_async_copy(ff_parts[k].at[rows_of], ff_s.at[k % 2, k // 2], ff_sem.at[k]))
        later[-1].start()
    if prior:
        later.append(pltpu.make_async_copy(prior[0], acc, prior_sem))
        later[-1].start()
    else:
        acc[...] = jnp.zeros(acc.shape, F32)

    def normed(u):
        c = u - jnp.mean(u, axis=0, keepdims=True)
        r = lax.rsqrt(jnp.mean(c * c, axis=0, keepdims=True) + EPS)
        return c * r, r

    ones = jnp.concatenate(
        [jnp.ones((1, rows), F32), jnp.zeros((15, rows), F32)], axis=0
    ).astype(BF16)

    def prepare(h, carry):
        base = pl.multiple_of(h * 3 * size, size)
        gh = pl.ds(pl.multiple_of(h * size, size), size)
        at = lambda c: pl.ds(pl.multiple_of(base + c * size, size), size)
        scaled = []
        for c, gain in ((0, qg), (1, kg)):
            unit, r = normed(jt[at(c), :])
            jt[at(c), :] = unit
            inv_s[pl.ds(2 * h + c, 1), :] = r
            scaled.append(unit * gain[gh, :])
        qt, kt = scaled
        vt = jt[at(2), :]
        qs_t[h] = (qt * up).astype(BF16)
        qt_s[h] = qt.astype(BF16)
        k_s[h] = kt.T.astype(BF16)
        v_s[h] = vt.T.astype(BF16)
        for k in range(blocks):
            cols = slice(k * rows, (k + 1) * rows)
            kt_s[h, k] = kt[:, cols].astype(BF16)
            vt_s[h, k, 0:size] = vt[:, cols].astype(BF16)
            vt_s[h, k, size : size + 16] = ones
        return carry

    lax.fori_loop(0, heads, prepare, 0)

    live = length[0]
    count = (live + rows - 1) // rows

    dk[...] = jnp.zeros(dk.shape, F32)
    dv[...] = jnp.zeros(dv.shape, F32)

    def forward(j, carry):
        b = j ^ pos[0]
        start = pl.multiple_of(b * rows, rows)
        slot = lax.broadcasted_iota(jnp.int32, (rows, 1), 0) + j * rows
        for h in range(heads):
            s = mm(k_s[h, pl.ds(start, rows), :], qs_t[h])
            e = jnp.where(slot < live, jnp.exp2(s), 0.0).astype(BF16)
            es[h, b] = e
            o_acc[h] += mm(vt_s[h, b], e)
        return carry

    o_acc[...] = jnp.zeros(o_acc.shape, F32)
    dqt[...] = jnp.zeros(dqt.shape, F32)
    lax.fori_loop(0, count, forward, 0)
    for h in range(heads):
        inv = 1.0 / o_acc[h, size : size + 1]
        o = o_acc[h, 0:size] * inv
        hs = slice(h * size, (h + 1) * size)
        ot[hs] = o.astype(BF16)
        dot_b = (dot_s[hs] * inv).astype(BF16)
        dot_bs[hs] = dot_b
        r_s[h : h + 1] = jnp.sum(dot_b.astype(F32) * o, axis=0, keepdims=True)

    def backward(j, carry):
        b = j ^ pos[0]
        start = pl.multiple_of(b * rows, rows)
        for h in range(heads):
            dot_b = dot_bs[h * size : (h + 1) * size]
            dp = mm(v_s[h, pl.ds(start, rows), :], dot_b)
            e = es[h, b]
            ds = (e.astype(F32) * (dp - r_s[h : h + 1])).astype(BF16)
            dv[h, b] = mm(dot_b, e, NT)
            dk[h, b] = mm(qt_s[h], ds, NT)
            dqt[h] += mm(kt_s[h, b], ds)
        return carry

    lax.fori_loop(0, count, backward, 0)

    def undo(h, carry):
        base = pl.multiple_of(h * 3 * size, size)
        gh = pl.multiple_of(h * size, size)
        for c, gain, grad in ((0, qg, dqt[h]), (1, kg, jnp.concatenate([dk[h, k] for k in range(blocks)], axis=1))):
            at = pl.ds(pl.multiple_of(base + c * size, size), size)
            n, r = jt[at, :], inv_s[pl.ds(2 * h + c, 1), :]
            grad = grad * scale
            y = grad * gain[pl.ds(gh, size), :]
            back = r * (
                y
                - jnp.mean(y, axis=0, keepdims=True)
                - n * jnp.mean(y * n, axis=0, keepdims=True)
            )
            djt[at, :] = back.astype(BF16)
            accg[pl.ds(pl.multiple_of(c * heads * size + gh, size), size), :] = jnp.sum(grad * n, axis=1, keepdims=True)
        values = jnp.concatenate([dv[h, k] for k in range(blocks)], axis=1)
        djt[pl.ds(pl.multiple_of(base + 2 * size, size), size), :] = values.astype(BF16)
        return carry

    lax.fori_loop(0, heads, undo, 0)
    for copy in later:
        copy.wait()
    if prior:
        accg[...] += gain_s[...]

    targets = [keep_near, send.at[pl.ds(0, 2 * rows)], keep_far, send.at[pl.ds(2 * rows, 2 * rows)]]
    writes = [pltpu.make_async_copy(out_s.at[k], targets[k], out_sem.at[k]) for k in range(blocks)]

    def give(k, carry):
        cols = pl.ds(pl.multiple_of(k * rows, rows), rows)
        part = pl.ds(pl.multiple_of((k & 1) * rows, rows), rows)
        n = ff_s[1, k >> 1, part, :].astype(F32) + mm(djt[:, cols], wqkv[...], TN)
        o = ff_s[0, k >> 1, part, :].astype(F32) + mm(ot[:, cols], wproj[...], TN)
        out_s[k, 0:rows] = o.astype(BF16)
        out_s[k, rows : 2 * rows] = n.astype(BF16)
        acc[0:joined] += mm(djt[:, cols], pack_s[k, 0:rows])
        acc[joined:] += mm(ot[:, cols], pack_s[k, rows : 2 * rows])
        for j in range(blocks):

            @pl.when(k == j)
            def _(j=j):
                writes[j].start()

        return carry

    lax.fori_loop(0, blocks, give, 0)
    if last:
        ln = jnp.sum(wqkv[...].astype(F32) * acc[0:joined], axis=0, keepdims=True) + small_s[2:3]
        gain_row = as_row(accg[...])
        pad = jnp.zeros((1, ln.shape[1] - gain_row.shape[1]), F32)
        lines = [jnp.concatenate([gain_row, pad], axis=1), small_s[0:2], ln, jnp.zeros((4, ln.shape[1]), F32)]
        small[...] = jnp.concatenate(lines, axis=0).astype(BF16)
        emit_halves(acc, x_bit, *pieces)
        half = pieces[0].shape[0]
        pieces[1][half : half + 8] = small[...]
    for write in writes:
        write.wait()


def final_kernel(images, *refs):
    tokens, d_out, gain, bias = refs[:4]
    ins = refs[4 : 4 + 3 * images]
    out, d_tokens = refs[-2:]
    rows = tokens.shape[1]
    for i in range(images):

        @pl.when(pl.program_id(0) == i)
        def _(i=i):
            keep, near, far = ins[3 * i : 3 * i + 3]
            both = [
                keep[at].astype(F32) + near[at].astype(F32) + far[at].astype(F32)
                for at in (slice(0, rows), slice(rows, 2 * rows))
            ]
            v = tokens[0].astype(F32)
            c = v - jnp.mean(v, axis=-1, keepdims=True)
            r = lax.rsqrt(jnp.mean(c * c, axis=-1, keepdims=True) + EPS)
            xhat = c * r
            out[0] = (v + both[0] + bias[...].reshape(1, -1)).astype(BF16)
            z = both[1] * gain[...].reshape(1, -1)
            back = r * (
                z
                - jnp.mean(z, axis=-1, keepdims=True)
                - xhat * jnp.mean(z * xhat, axis=-1, keepdims=True)
            )
            d_tokens[0] = d_out[0].astype(F32) + back


def join_kernel(n, *refs):
    pos, own, across, rest = refs[0], refs[1 : 1 + n], refs[1 + n], refs[2 + n]
    one, two, whole = refs[3 + n :]
    step = own[0].shape[0]
    half = step * n
    for k in range(n):
        z = pos[1] ^ k
        at = pl.multiple_of(pos[0] * half + z * step, step)
        whole[pl.ds(at, step), :] = own[k][...].astype(F32)
        at = pl.multiple_of((1 - pos[0]) * half + z * step, step)
        far = across[...] if k == 0 else rest[(k - 1) * step : k * step]
        whole[pl.ds(at, step), :] = far.astype(F32)
    cut = one.shape[0]
    one[...] = whole[0:cut]
    two[...] = whole[cut:]


def block(dp_size, tp_size, *args):
    (tokens, lengths, ln_gain, w_qkv, q_gain, k_gain, w_proj, w_fc1, b_fc1, w_fc2, b_fc2, d_out) = args
    images, rows, width = tokens.shape
    heads, size = q_gain.shape
    hidden = w_fc1.shape[1]
    total = rows * tp_size
    blocks = tp_size
    joined = heads * 3 * size
    inner = heads * size
    n = dp_size // 2
    t = lax.axis_index("tp").astype(jnp.int32)
    d = lax.axis_index("dp").astype(jnp.int32)
    x, z = d & 1, d >> 1

    def swap(v, axis, mask):
        count = tp_size if axis == "tp" else dp_size
        return lax.ppermute(v, axis, [(i, i ^ mask) for i in range(count)])

    def after(v, dep):
        return lax.optimization_barrier((v, dep))[0]

    def norm(begin, end):
        count = end - begin
        return call(
            functools.partial(norm_kernel, begin), [((2 * rows, width), BF16)] * count, 0,
            tokens, d_out, ln_gain, n_any=2,
            scratch=[
                pltpu.VMEM((count, rows, width), BF16),
                pltpu.SemaphoreType.DMA((count,)),
                pltpu.SemaphoreType.DMA((count,)),
            ],
        )

    own = norm(0, images)
    far = [swap(v, "tp", 2) for v in own]
    near = [swap(v, "tp", 1) for v in own]
    cross = [None] * images

    def forward(i, dep):
        cross[i] = swap(after(far[i], dep), "tp", 1)

    b1 = b_fc1
    pos = jnp.stack([x, z])

    half = (joined + inner) // 2
    qp_pieces = [((half, width), F32), ((half + 8, width), BF16)]

    def ff(first, last, packs, state):
        count = len(packs)
        outs = [((count * rows, width), BF16)] * 2
        scratch = [
            pltpu.VMEM((2, 2 * rows, width), BF16),
            pltpu.VMEM((width, hidden), BF16),
            pltpu.VMEM((hidden, width), BF16),
            pltpu.VMEM((hidden,), F32),
            pltpu.VMEM((2, rows, width), BF16),
            pltpu.VMEM((2, rows, width), BF16),
            pltpu.SemaphoreType.DMA((2,)),
            pltpu.SemaphoreType.DMA((3,)),
            pltpu.SemaphoreType.DMA((2,)),
            pltpu.SemaphoreType.DMA((2,)),
            pltpu.SemaphoreType.DMA((2,)),
        ]
        if last:
            outs += [((width + hidden, width), BF16), ((8, width), F32)]
            scratch += [
                pltpu.VMEM((width + hidden, width), F32),
                pltpu.VMEM((width + hidden, width), BF16),
                pltpu.SemaphoreType.DMA,
            ]
        else:
            outs += [((width + hidden, width), F32), ((8, width), F32)]
        res = call(
            functools.partial(ff_kernel, first, last, count, first), outs, 0,
            *packs, w_fc1, w_fc2, b1, *state, n_any=count + 3 + len(state), any_outs=3 if last else 2,
            scratch=scratch, flops=12 * count * rows * width * hidden,
        )
        return res[0], res[1], res[2:]

    qg = q_gain.reshape(-1, 1)
    kg = k_gain.reshape(-1, 1)
    w_t = w_qkv.T
    keeps = []

    def att(i, ff_parts, starts, state, ff_small=()):
        first, last = i == 0, i == images - 1
        outs = [((2 * rows, width), BF16)] * 2 + [((4 * rows, width), BF16)]
        scratch = [
            pltpu.VMEM((joined, total), F32),
            pltpu.VMEM((inner, total), F32),
            pltpu.VMEM((heads, size, total), BF16),
            pltpu.VMEM((heads, size, total), BF16),
            pltpu.VMEM((heads, total, size), BF16),
            pltpu.VMEM((heads, blocks, size, rows), BF16),
            pltpu.VMEM((heads, total, size), BF16),
            pltpu.VMEM((heads, blocks, size + 16, rows), BF16),
            pltpu.VMEM((heads, blocks, rows, total), BF16),
            pltpu.VMEM((heads, size, total), F32),
            pltpu.VMEM((heads, blocks, size, rows), F32),
            pltpu.VMEM((heads, blocks, size, rows), F32),
            pltpu.VMEM((inner, total), BF16),
            pltpu.VMEM((joined, total), BF16),
            pltpu.VMEM((2, 2, 2 * rows, width), BF16),
            pltpu.SemaphoreType.DMA((4,)),
            pltpu.SemaphoreType.DMA,
            pltpu.VMEM((blocks, 2 * rows, width), BF16),
            pltpu.SemaphoreType.DMA((blocks,)),
            pltpu.VMEM((inner, total), BF16),
            pltpu.VMEM((8, total), F32),
            pltpu.VMEM((blocks, 2 * rows, width), BF16),
            pltpu.SemaphoreType.DMA((blocks,)),
            pltpu.VMEM((joined, width), BF16),
            pltpu.VMEM((inner, width), BF16),
            pltpu.VMEM((inner, 1), F32),
            pltpu.VMEM((inner, 1), F32),
            pltpu.VMEM((2 * inner, 1), F32),
            pltpu.VMEM((8, width), F32),
            pltpu.SemaphoreType.DMA((4,)),
            pltpu.SemaphoreType.DMA((2,)),
            pltpu.VMEM((heads, size + 16, total), F32),
            pltpu.VMEM((8, total), F32),
        ]
        if last:
            outs += qp_pieces + [((8, width), BF16)]
            scratch += [pltpu.VMEM((joined + inner, width), F32), pltpu.VMEM((2 * inner, 1), F32)]
        else:
            outs += [((joined + inner, width), F32), ((2 * inner, 1), F32)]
        res = call(
            functools.partial(att_kernel, first, last, blocks, heads, size, starts), outs, 3,
            lengths[i : i + 1], t[None], x[None], own[i], near[i], far[i], cross[i], *ff_parts, *state[:1],
            w_t, w_proj, qg, kg, *state[1:], *ff_small, n_any=blocks + 8 + len(state) + len(ff_small), any_outs=3,
            scratch=scratch,
            flops=6 * 8 * heads * total * total * size + 8 * total * width * (joined + inner),
        )
        keep_near, keep_far, send = res[:3]
        got = swap(send, "tp", 1)
        summed = (keep_far.astype(F32) + got[2 * rows :].astype(F32)).astype(BF16)
        keeps.extend([keep_near, got, swap(summed, "tp", 2)])
        return res[3:]

    def reduce_weight(small, keep, send):
        extra = small.shape[0]
        got = swap(send, "dp", 1)
        half = keep + got[:-extra].astype(F32)
        small = (small.astype(F32) + got[-extra:].astype(F32)).astype(BF16)
        step = keep.shape[0] // n
        piece = lambda k: lax.dynamic_slice_in_dim(half, (z ^ k) * step, step, 0)
        done = piece(0)
        smalls = [small]
        for k in range(1, n):
            got = swap(jnp.concatenate([piece(k).astype(BF16), small], axis=0), "dp", 2 * k)
            done = done + got[:-extra].astype(F32)
            smalls.append(got[-extra:])
        done = done.astype(BF16)
        smalls = jnp.stack(smalls).astype(F32)
        small = sum(lax.dynamic_index_in_dim(smalls, z ^ k, 0, keepdims=False) for k in range(n))
        near = [swap(done, "dp", 2 * k) for k in range(1, n)]
        across = swap(done, "dp", 1)
        rest = swap(jnp.concatenate(near, axis=0), "dp", 1)
        return [done] + near + [across, rest], small

    def join(parts, shapes):
        return call(
            functools.partial(join_kernel, n), [(s, F32) for s in shapes], 1, pos, *parts,
            scratch=[pltpu.VMEM((joined + inner, width), F32)],
        )

    a_parts = ff(True, False, [b for i in range(images) for b in (own[i], near[i])], [])
    forward(0, a_parts[0])
    b_parts = ff(False, False, [far[0], cross[0]], a_parts[2])
    forward(1, b_parts[0])
    att_state = att(0, a_parts[:2] + b_parts[:2], (0, 0), [])
    for i in range(2, images):
        forward(i, att_state[1])
    c_parts = ff(False, True, [b for i in range(1, images) for b in (far[i], cross[i])], b_parts[2])
    state = c_parts[2]
    ff_out, ff_small = state
    fc = lax.psum(ff_out, "dp")
    for i in range(1, images):
        starts = (2 * rows * i, 2 * rows * (i - 1))
        att_state = att(i, a_parts[:2] + c_parts[:2], starts, att_state, [ff_small] if i == images - 1 else [])
    *qp_out, small = att_state
    qp_parts, late = reduce_weight(small, *qp_out)
    d_q_gain = late[0, :inner].reshape(heads, size)
    d_k_gain = late[0, inner : 2 * inner].reshape(heads, size)
    d_bias_one = late[1]
    both = late[2:4]
    both = both + swap(both, "tp", 1)
    both = both + swap(both, "tp", 2)
    d_bias_two = both[0]
    d_ln_gain = both[1] / ln_gain

    d_fc1, d_fc2 = fc[:width].astype(F32), fc[width:].astype(F32)
    d_qkv_t, d_proj = join(qp_parts, [(joined, width), (inner, width)])
    d_qkv = d_qkv_t.T

    def finish(begin, end, earlier):
        block = pl.BlockSpec((1, rows, width), lambda i: (begin + i, 0, 0))
        vector = pl.BlockSpec((width,), lambda i: (0,))
        first = pl.BlockSpec((2 * rows, width), lambda i: (0, 0))
        ins = keeps[3 * begin : 3 * end]
        return pl.pallas_call(
            functools.partial(final_kernel, end - begin),
            grid=(end - begin,),
            out_shape=[
                jax.ShapeDtypeStruct((images, rows, width), BF16),
                jax.ShapeDtypeStruct((images, rows, width), F32),
            ],
            in_specs=[block, block, vector, vector] + [first] * len(ins) + [ANY_SPEC] * len(earlier),
            out_specs=[block, block],
            input_output_aliases={4 + len(ins) + k: k for k in range(len(earlier))},
        )(tokens, d_out, ln_gain, b_fc2, *ins, *earlier)

    results = finish(0, images - 1, [])
    output, d_tokens = finish(images - 1, images, results)
    return (output, d_tokens, d_ln_gain, d_qkv, d_q_gain, d_k_gain, d_proj, d_fc1, d_bias_one, d_fc2, d_bias_two)


def solution(mesh):
    rows = P("dp", "tp", None)
    wide = P(None, "tp")
    tall = P("tp", None)
    return jax.shard_map(
        functools.partial(block, mesh.shape["dp"], mesh.shape["tp"]),
        mesh=mesh,
        in_specs=(rows, P("dp"), P(), wide, tall, tall, tall, wide, P("tp"), tall, P(), rows),
        out_specs=(rows, rows, P(), wide, tall, tall, tall, wide, P("tp"), tall, P()),
        check_vma=False,
    )
```

```python
import functools
import math

import jax
import jax.numpy as jnp
from jax import lax
from jax.experimental import pallas as pl
from jax.experimental.pallas import tpu as pltpu
from jax.sharding import PartitionSpec as P


EPS = 1e-06
F32 = jnp.float32
BF16 = jnp.bfloat16
NN = (((1,), (0,)), ((), ()))
NT = (((1,), (1,)), ((), ()))
TN = (((0,), (0,)), ((), ()))
VMEM_SPEC = pl.BlockSpec(memory_space=pltpu.VMEM)
ANY_SPEC = pl.BlockSpec(memory_space=pl.ANY)
SMEM_SPEC = pl.BlockSpec(memory_space=pltpu.SMEM)


def mm(a, b, dims=NN):
    return lax.dot_general(a, b, dims, preferred_element_type=F32)


def call(kernel, outs, n_smem, *args, n_any=0, any_outs=0, scratch=(), flops=0):
    in_specs = [SMEM_SPEC] * n_smem + [ANY_SPEC] * n_any + [VMEM_SPEC] * (len(args) - n_smem - n_any)
    moved = sum(a.size * a.dtype.itemsize for a in args)
    moved += sum(math.prod(s) * jnp.dtype(d).itemsize for s, d in outs)
    return pl.pallas_call(
        kernel,
        out_shape=[jax.ShapeDtypeStruct(s, d) for s, d in outs],
        in_specs=in_specs,
        out_specs=[ANY_SPEC] * any_outs + [VMEM_SPEC] * (len(outs) - any_outs),
        scratch_shapes=list(scratch),
        compiler_params=pltpu.CompilerParams(vmem_limit_bytes=60 * 1024 * 1024),
        cost_estimate=pl.CostEstimate(flops=flops, transcendentals=0, bytes_accessed=moved),
    )(*args)


def norm_kernel(begin, tokens, d_out, gain_ref, *refs):
    out_refs, (held, sem, sem_out) = refs[:-3], refs[-3:]
    rows = tokens.shape[1]
    reads, copies = [], []
    for i, out in enumerate(out_refs):
        reads.append(pltpu.make_async_copy(tokens.at[begin + i], held.at[i], sem.at[i]))
        reads[-1].start()
    for i, out in enumerate(out_refs):
        copies.append(pltpu.make_async_copy(d_out.at[begin + i], out.at[pl.ds(rows, rows)], sem_out.at[i]))
        copies[-1].start()
    for i, out in enumerate(out_refs):
        reads[i].wait()
        v = held[i].astype(F32)
        c = v - jnp.mean(v, axis=-1, keepdims=True)
        r = lax.rsqrt(jnp.mean(c * c, axis=-1, keepdims=True) + EPS)
        out[0:rows] = (c * r * gain_ref[...].reshape(1, -1)).astype(BF16)
    for copy in copies:
        copy.wait()


def as_row(column):
    return jnp.broadcast_to(column, (column.shape[0], 128)).T[0:1]


def emit_halves(acc, pos, keep, send):
    half = acc.shape[0] // 2
    keep[...] = acc[pl.ds(pl.multiple_of(pos[0] * half, half), half), :]
    send[0:half] = acc[pl.ds(pl.multiple_of((1 - pos[0]) * half, half), half), :].astype(BF16)


def ff_kernel(first, last, blocks, owned, *refs):
    refs = list(refs)
    take = lambda n: [refs.pop(0) for _ in range(n)]
    packs = take(blocks)
    weights = take(3)
    prior = [] if first else take(2)
    o_ff, n_ff = take(2)
    if last:
        summed, accb = take(2)
    else:
        acc, accb = take(2)
    buf, w1, w2, b1, o_s, n_s, sem, weight_sem, prior_sem, o_sem, n_sem = take(11)
    if last:
        (acc,) = take(1)
    rows = packs[0].shape[0] // 2
    width = w1.shape[0]
    inv_sqrt2 = 2.0**-0.5

    def fetch(j, slot):
        return pltpu.make_async_copy(packs[j], buf.at[slot], sem.at[slot])

    def writes(k, slot):
        at = pl.ds(pl.multiple_of(k * rows, rows), rows)
        return (
            pltpu.make_async_copy(o_s.at[slot], o_ff.at[at], o_sem.at[slot]),
            pltpu.make_async_copy(n_s.at[slot], n_ff.at[at], n_sem.at[slot]),
        )

    fetch(0, 0).start()
    loads = [pltpu.make_async_copy(weights[j], to, weight_sem.at[j]) for j, to in enumerate((w1, w2, b1))]
    for load in loads:
        load.start()
    held = [pltpu.make_async_copy(prior[j], to, prior_sem.at[j]) for j, to in enumerate((acc, accb))] if prior else []
    if not prior:
        acc[...] = jnp.zeros(acc.shape, F32)
        accb[...] = jnp.zeros(accb.shape, F32)
    for load in loads:
        load.wait()
    for copy in held:
        copy.start()

    def step(k, carry):
        slot = k & 1
        fetch(0, slot).wait()
        for j in range(1, blocks):

            @pl.when(k + 1 == j)
            def _(j=j):
                fetch(j, 1 - slot).start()

        @pl.when(k >= 2)
        def _():
            for write in writes(k - 2, slot):
                write.wait()

        x = buf[slot, 0:rows]
        g = buf[slot, rows : 2 * rows]
        h = mm(x, w1[...]) + b1[...].reshape(1, -1)
        da = mm(g, w2[...], NT)
        cdf = 0.5 * (1.0 + lax.erf(h * inv_sqrt2))
        pdf = jnp.exp(-0.5 * h * h) * (1.0 / math.sqrt(2.0 * math.pi))
        act = (h * cdf).astype(BF16)
        dh = (da * (cdf + h * pdf)).astype(BF16)
        o_s[slot] = mm(act, w2[...]).astype(BF16)
        n_s[slot] = mm(dh, w1[...], NT).astype(BF16)
        for write in writes(k, slot):
            write.start()
        if prior:

            @pl.when(k == 0)
            def _():
                for copy in held:
                    copy.wait()

        accb[0:1] += jnp.sum(dh.astype(F32), axis=0, keepdims=True)
        if owned:

            @pl.when(k % 2 == 0)
            def _():
                accb[1:2] += jnp.sum(g.astype(F32), axis=0, keepdims=True)

        acc[0:width] += mm(x, dh, TN)
        acc[width:] += mm(act, g, TN)
        return carry

    lax.fori_loop(0, blocks, step, 0)
    if last:
        accb[2:3] = as_row(jnp.sum(w1[...].astype(F32) * acc[0:width], axis=1, keepdims=True))
        summed[...] = acc[...].astype(BF16)
    for k in range(blocks - 2, blocks):
        for write in writes(k, k & 1):
            write.wait()


def att_kernel(first, last, blocks, heads, size, starts, *refs):
    refs = list(refs)
    take = lambda n: [refs.pop(0) for _ in range(n)]
    length, pos, x_bit = take(3)
    parts = take(blocks)
    ff_parts = take(4)
    prior = [] if first else take(1)
    weights = take(4)
    prior_gain = [] if first else take(1)
    ff_small_in = take(1) if last else []
    keep_near, keep_far, send = take(3)
    if last:
        pieces = take(len(refs) - 36)
        (small,) = take(1)
    else:
        acc, accg = take(2)
    jt, dot_s, qs_t, qt_s, k_s, kt_s, v_s, vt_s, es, dqt, dk, dv, ot, djt = take(14)
    ff_s, ff_sem, prior_sem, out_s, out_sem, dot_bs, r_s, pack_s, pack_sem = take(9)
    wqkv, wproj, qg, kg, gain_s, small_s, weight_sem, tail_sem, o_acc, inv_s = take(10)
    if last:
        acc, accg = take(2)
    rows = parts[0].shape[0] // 2
    joined = wqkv.shape[0]
    scale = size**-0.5
    up = scale * math.log2(math.e)
    loads = [pltpu.make_async_copy(weights[j], to, weight_sem.at[j]) for j, to in enumerate((wqkv, wproj, qg, kg))]
    for load in loads[:2]:
        load.start()
    for k in range(blocks):
        pltpu.make_async_copy(parts[k], pack_s.at[k], pack_sem.at[k]).start()
    for load in loads[2:]:
        load.start()
    for load in loads[:2]:
        load.wait()

    def project(k, carry):
        pltpu.make_async_copy(parts[0], pack_s.at[k], pack_sem.at[k]).wait()
        cols = pl.ds(pl.multiple_of(k * rows, rows), rows)
        jt[:, cols] = mm(wqkv[...], pack_s[k, 0:rows], NT)
        dot_s[:, cols] = mm(wproj[...], pack_s[k, rows : 2 * rows], NT)
        return carry

    lax.fori_loop(0, blocks, project, 0)
    for load in loads[2:]:
        load.wait()
    later = [pltpu.make_async_copy(source, gain_s, tail_sem.at[0]) for source in prior_gain]
    later += [pltpu.make_async_copy(source, small_s, tail_sem.at[1]) for source in ff_small_in]
    for copy in later:
        copy.start()
    for k in range(4):
        rows_of = pl.ds(starts[k // 2], 2 * rows)
        later.append(pltpu.make_async_copy(ff_parts[k].at[rows_of], ff_s.at[k % 2, k // 2], ff_sem.at[k]))
        later[-1].start()
    if prior:
        later.append(pltpu.make_async_copy(prior[0], acc, prior_sem))
        later[-1].start()
    else:
        acc[...] = jnp.zeros(acc.shape, F32)

    def normed(u):
        c = u - jnp.mean(u, axis=0, keepdims=True)
        r = lax.rsqrt(jnp.mean(c * c, axis=0, keepdims=True) + EPS)
        return c * r, r

    ones = jnp.concatenate(
        [jnp.ones((1, rows), F32), jnp.zeros((15, rows), F32)], axis=0
    ).astype(BF16)

    def prepare(h, carry):
        base = pl.multiple_of(h * 3 * size, size)
        gh = pl.ds(pl.multiple_of(h * size, size), size)
        at = lambda c: pl.ds(pl.multiple_of(base + c * size, size), size)
        scaled = []
        for c, gain in ((0, qg), (1, kg)):
            unit, r = normed(jt[at(c), :])
            jt[at(c), :] = unit
            inv_s[pl.ds(2 * h + c, 1), :] = r
            scaled.append(unit * gain[gh, :])
        qt, kt = scaled
        vt = jt[at(2), :]
        qs_t[h] = (qt * up).astype(BF16)
        qt_s[h] = qt.astype(BF16)
        k_s[h] = kt.T.astype(BF16)
        v_s[h] = vt.T.astype(BF16)
        for k in range(blocks):
            cols = slice(k * rows, (k + 1) * rows)
            kt_s[h, k] = kt[:, cols].astype(BF16)
            vt_s[h, k, 0:size] = vt[:, cols].astype(BF16)
            vt_s[h, k, size : size + 16] = ones
        return carry

    lax.fori_loop(0, heads, prepare, 0)

    live = length[0]
    count = (live + rows - 1) // rows

    dk[...] = jnp.zeros(dk.shape, F32)
    dv[...] = jnp.zeros(dv.shape, F32)

    def forward(j, carry):
        b = j ^ pos[0]
        start = pl.multiple_of(b * rows, rows)
        slot = lax.broadcasted_iota(jnp.int32, (rows, 1), 0) + j * rows
        for h in range(heads):
            s = mm(k_s[h, pl.ds(start, rows), :], qs_t[h])
            e = jnp.where(slot < live, jnp.exp2(s), 0.0).astype(BF16)
            es[h, b] = e
            o_acc[h] += mm(vt_s[h, b], e)
        return carry

    o_acc[...] = jnp.zeros(o_acc.shape, F32)
    dqt[...] = jnp.zeros(dqt.shape, F32)
    lax.fori_loop(0, count, forward, 0)
    for h in range(heads):
        inv = 1.0 / o_acc[h, size : size + 1]
        o = o_acc[h, 0:size] * inv
        hs = slice(h * size, (h + 1) * size)
        ot[hs] = o.astype(BF16)
        dot_b = (dot_s[hs] * inv).astype(BF16)
        dot_bs[hs] = dot_b
        r_s[h : h + 1] = jnp.sum(dot_b.astype(F32) * o, axis=0, keepdims=True)

    def backward(j, carry):
        b = j ^ pos[0]
        start = pl.multiple_of(b * rows, rows)
        for h in range(heads):
            dot_b = dot_bs[h * size : (h + 1) * size]
            dp = mm(v_s[h, pl.ds(start, rows), :], dot_b)
            e = es[h, b]
            ds = (e.astype(F32) * (dp - r_s[h : h + 1])).astype(BF16)
            dv[h, b] = mm(dot_b, e, NT)
            dk[h, b] = mm(qt_s[h], ds, NT)
            dqt[h] += mm(kt_s[h, b], ds)
        return carry

    lax.fori_loop(0, count, backward, 0)

    def undo(h, carry):
        base = pl.multiple_of(h * 3 * size, size)
        gh = pl.multiple_of(h * size, size)
        for c, gain, grad in ((0, qg, dqt[h]), (1, kg, jnp.concatenate([dk[h, k] for k in range(blocks)], axis=1))):
            at = pl.ds(pl.multiple_of(base + c * size, size), size)
            n, r = jt[at, :], inv_s[pl.ds(2 * h + c, 1), :]
            grad = grad * scale
            y = grad * gain[pl.ds(gh, size), :]
            back = r * (
                y
                - jnp.mean(y, axis=0, keepdims=True)
                - n * jnp.mean(y * n, axis=0, keepdims=True)
            )
            djt[at, :] = back.astype(BF16)
            accg[pl.ds(pl.multiple_of(c * heads * size + gh, size), size), :] = jnp.sum(grad * n, axis=1, keepdims=True)
        values = jnp.concatenate([dv[h, k] for k in range(blocks)], axis=1)
        djt[pl.ds(pl.multiple_of(base + 2 * size, size), size), :] = values.astype(BF16)
        return carry

    lax.fori_loop(0, heads, undo, 0)
    for copy in later:
        copy.wait()
    if prior:
        accg[...] += gain_s[...]

    targets = [keep_near, send.at[pl.ds(0, 2 * rows)], keep_far, send.at[pl.ds(2 * rows, 2 * rows)]]
    writes = [pltpu.make_async_copy(out_s.at[k], targets[k], out_sem.at[k]) for k in range(blocks)]

    def give(k, carry):
        cols = pl.ds(pl.multiple_of(k * rows, rows), rows)
        part = pl.ds(pl.multiple_of((k & 1) * rows, rows), rows)
        n = ff_s[1, k >> 1, part, :].astype(F32) + mm(djt[:, cols], wqkv[...], TN)
        o = ff_s[0, k >> 1, part, :].astype(F32) + mm(ot[:, cols], wproj[...], TN)
        out_s[k, 0:rows] = o.astype(BF16)
        out_s[k, rows : 2 * rows] = n.astype(BF16)
        acc[0:joined] += mm(djt[:, cols], pack_s[k, 0:rows])
        acc[joined:] += mm(ot[:, cols], pack_s[k, rows : 2 * rows])
        for j in range(blocks):

            @pl.when(k == j)
            def _(j=j):
                writes[j].start()

        return carry

    lax.fori_loop(0, blocks, give, 0)
    if last:
        ln = jnp.sum(wqkv[...].astype(F32) * acc[0:joined], axis=0, keepdims=True) + small_s[2:3]
        gain_row = as_row(accg[...])
        pad = jnp.zeros((1, ln.shape[1] - gain_row.shape[1]), F32)
        lines = [jnp.concatenate([gain_row, pad], axis=1), small_s[0:2], ln, jnp.zeros((4, ln.shape[1]), F32)]
        small[...] = jnp.concatenate(lines, axis=0).astype(BF16)
        emit_halves(acc, x_bit, *pieces)
        half = pieces[0].shape[0]
        pieces[1][half : half + 8] = small[...]
    for write in writes:
        write.wait()


def final_kernel(images, *refs):
    tokens, d_out, gain, bias = refs[:4]
    ins = refs[4 : 4 + 3 * images]
    out, d_tokens = refs[-2:]
    rows = tokens.shape[1]
    for i in range(images):

        @pl.when(pl.program_id(0) == i)
        def _(i=i):
            keep, near, far = ins[3 * i : 3 * i + 3]
            both = [
                keep[at].astype(F32) + near[at].astype(F32) + far[at].astype(F32)
                for at in (slice(0, rows), slice(rows, 2 * rows))
            ]
            v = tokens[0].astype(F32)
            c = v - jnp.mean(v, axis=-1, keepdims=True)
            r = lax.rsqrt(jnp.mean(c * c, axis=-1, keepdims=True) + EPS)
            xhat = c * r
            out[0] = (v + both[0] + bias[...].reshape(1, -1)).astype(BF16)
            z = both[1] * gain[...].reshape(1, -1)
            back = r * (
                z
                - jnp.mean(z, axis=-1, keepdims=True)
                - xhat * jnp.mean(z * xhat, axis=-1, keepdims=True)
            )
            d_tokens[0] = d_out[0].astype(F32) + back


def join_kernel(n, *refs):
    pos, own, across, rest = refs[0], refs[1 : 1 + n], refs[1 + n], refs[2 + n]
    one, two, whole = refs[3 + n :]
    step = own[0].shape[0]
    half = step * n
    for k in range(n):
        z = pos[1] ^ k
        at = pl.multiple_of(pos[0] * half + z * step, step)
        whole[pl.ds(at, step), :] = own[k][...].astype(F32)
        at = pl.multiple_of((1 - pos[0]) * half + z * step, step)
        far = across[...] if k == 0 else rest[(k - 1) * step : k * step]
        whole[pl.ds(at, step), :] = far.astype(F32)
    cut = one.shape[0]
    one[...] = whole[0:cut]
    two[...] = whole[cut:]


def block(dp_size, tp_size, *args):
    (tokens, lengths, ln_gain, w_qkv, q_gain, k_gain, w_proj, w_fc1, b_fc1, w_fc2, b_fc2, d_out) = args
    images, rows, width = tokens.shape
    heads, size = q_gain.shape
    hidden = w_fc1.shape[1]
    total = rows * tp_size
    blocks = tp_size
    joined = heads * 3 * size
    inner = heads * size
    n = dp_size // 2
    t = lax.axis_index("tp").astype(jnp.int32)
    d = lax.axis_index("dp").astype(jnp.int32)
    x, z = d & 1, d >> 1

    def swap(v, axis, mask):
        count = tp_size if axis == "tp" else dp_size
        return lax.ppermute(v, axis, [(i, i ^ mask) for i in range(count)])

    def after(v, dep):
        return lax.optimization_barrier((v, dep))[0]

    def norm(begin, end):
        count = end - begin
        return call(
            functools.partial(norm_kernel, begin), [((2 * rows, width), BF16)] * count, 0,
            tokens, d_out, ln_gain, n_any=2,
            scratch=[
                pltpu.VMEM((count, rows, width), BF16),
                pltpu.SemaphoreType.DMA((count,)),
                pltpu.SemaphoreType.DMA((count,)),
            ],
        )

    own = norm(0, images)
    far = [swap(v, "tp", 2) for v in own]
    near = [swap(v, "tp", 1) for v in own]
    cross = [None] * images

    def forward(i, dep):
        cross[i] = swap(after(far[i], dep), "tp", 1)

    b1 = b_fc1
    pos = jnp.stack([x, z])

    half = (joined + inner) // 2
    qp_pieces = [((half, width), F32), ((half + 8, width), BF16)]

    def ff(first, last, packs, state):
        count = len(packs)
        outs = [((count * rows, width), BF16)] * 2
        scratch = [
            pltpu.VMEM((2, 2 * rows, width), BF16),
            pltpu.VMEM((width, hidden), BF16),
            pltpu.VMEM((hidden, width), BF16),
            pltpu.VMEM((hidden,), F32),
            pltpu.VMEM((2, rows, width), BF16),
            pltpu.VMEM((2, rows, width), BF16),
            pltpu.SemaphoreType.DMA((2,)),
            pltpu.SemaphoreType.DMA((3,)),
            pltpu.SemaphoreType.DMA((2,)),
            pltpu.SemaphoreType.DMA((2,)),
            pltpu.SemaphoreType.DMA((2,)),
        ]
        if last:
            outs += [((width + hidden, width), BF16), ((8, width), F32)]
            scratch += [pltpu.VMEM((width + hidden, width), F32)]
        else:
            outs += [((width + hidden, width), F32), ((8, width), F32)]
        res = call(
            functools.partial(ff_kernel, first, last, count, first), outs, 0,
            *packs, w_fc1, w_fc2, b1, *state, n_any=count + 3 + len(state), any_outs=2,
            scratch=scratch, flops=12 * count * rows * width * hidden,
        )
        return res[0], res[1], res[2:]

    qg = q_gain.reshape(-1, 1)
    kg = k_gain.reshape(-1, 1)
    w_t = w_qkv.T
    keeps = []

    def att(i, ff_parts, starts, state, ff_small=()):
        first, last = i == 0, i == images - 1
        outs = [((2 * rows, width), BF16)] * 2 + [((4 * rows, width), BF16)]
        scratch = [
            pltpu.VMEM((joined, total), F32),
            pltpu.VMEM((inner, total), F32),
            pltpu.VMEM((heads, size, total), BF16),
            pltpu.VMEM((heads, size, total), BF16),
            pltpu.VMEM((heads, total, size), BF16),
            pltpu.VMEM((heads, blocks, size, rows), BF16),
            pltpu.VMEM((heads, total, size), BF16),
            pltpu.VMEM((heads, blocks, size + 16, rows), BF16),
            pltpu.VMEM((heads, blocks, rows, total), BF16),
            pltpu.VMEM((heads, size, total), F32),
            pltpu.VMEM((heads, blocks, size, rows), F32),
            pltpu.VMEM((heads, blocks, size, rows), F32),
            pltpu.VMEM((inner, total), BF16),
            pltpu.VMEM((joined, total), BF16),
            pltpu.VMEM((2, 2, 2 * rows, width), BF16),
            pltpu.SemaphoreType.DMA((4,)),
            pltpu.SemaphoreType.DMA,
            pltpu.VMEM((blocks, 2 * rows, width), BF16),
            pltpu.SemaphoreType.DMA((blocks,)),
            pltpu.VMEM((inner, total), BF16),
            pltpu.VMEM((8, total), F32),
            pltpu.VMEM((blocks, 2 * rows, width), BF16),
            pltpu.SemaphoreType.DMA((blocks,)),
            pltpu.VMEM((joined, width), BF16),
            pltpu.VMEM((inner, width), BF16),
            pltpu.VMEM((inner, 1), F32),
            pltpu.VMEM((inner, 1), F32),
            pltpu.VMEM((2 * inner, 1), F32),
            pltpu.VMEM((8, width), F32),
            pltpu.SemaphoreType.DMA((4,)),
            pltpu.SemaphoreType.DMA((2,)),
            pltpu.VMEM((heads, size + 16, total), F32),
            pltpu.VMEM((8, total), F32),
        ]
        if last:
            outs += qp_pieces + [((8, width), BF16)]
            scratch += [pltpu.VMEM((joined + inner, width), F32), pltpu.VMEM((2 * inner, 1), F32)]
        else:
            outs += [((joined + inner, width), F32), ((2 * inner, 1), F32)]
        res = call(
            functools.partial(att_kernel, first, last, blocks, heads, size, starts), outs, 3,
            lengths[i : i + 1], t[None], x[None], own[i], near[i], far[i], cross[i], *ff_parts, *state[:1],
            w_t, w_proj, qg, kg, *state[1:], *ff_small, n_any=blocks + 8 + len(state) + len(ff_small), any_outs=3,
            scratch=scratch,
            flops=6 * 8 * heads * total * total * size + 8 * total * width * (joined + inner),
        )
        keep_near, keep_far, send = res[:3]
        got = swap(send, "tp", 1)
        summed = (keep_far.astype(F32) + got[2 * rows :].astype(F32)).astype(BF16)
        keeps.extend([keep_near, got, swap(summed, "tp", 2)])
        return res[3:]

    def reduce_weight(small, keep, send):
        extra = small.shape[0]
        got = swap(send, "dp", 1)
        half = keep + got[:-extra].astype(F32)
        small = (small.astype(F32) + got[-extra:].astype(F32)).astype(BF16)
        step = keep.shape[0] // n
        piece = lambda k: lax.dynamic_slice_in_dim(half, (z ^ k) * step, step, 0)
        done = piece(0)
        smalls = [small]
        for k in range(1, n):
            got = swap(jnp.concatenate([piece(k).astype(BF16), small], axis=0), "dp", 2 * k)
            done = done + got[:-extra].astype(F32)
            smalls.append(got[-extra:])
        done = done.astype(BF16)
        smalls = jnp.stack(smalls).astype(F32)
        small = sum(lax.dynamic_index_in_dim(smalls, z ^ k, 0, keepdims=False) for k in range(n))
        near = [swap(done, "dp", 2 * k) for k in range(1, n)]
        across = swap(done, "dp", 1)
        rest = swap(jnp.concatenate(near, axis=0), "dp", 1)
        return [done] + near + [across, rest], small

    def join(parts, shapes):
        return call(
            functools.partial(join_kernel, n), [(s, F32) for s in shapes], 1, pos, *parts,
            scratch=[pltpu.VMEM((joined + inner, width), F32)],
        )

    a_parts = ff(True, False, [b for i in range(images) for b in (own[i], near[i])], [])
    forward(0, a_parts[0])
    b_parts = ff(False, False, [far[0], cross[0]], a_parts[2])
    forward(1, b_parts[0])
    att_state = att(0, a_parts[:2] + b_parts[:2], (0, 0), [])
    for i in range(2, images):
        forward(i, att_state[1])
    c_parts = ff(False, True, [b for i in range(1, images) for b in (far[i], cross[i])], b_parts[2])
    state = c_parts[2]
    ff_out, ff_small = state
    fc = lax.psum(ff_out, "dp")
    for i in range(1, images):
        starts = (2 * rows * i, 2 * rows * (i - 1))
        att_state = att(i, a_parts[:2] + c_parts[:2], starts, att_state, [ff_small] if i == images - 1 else [])
    *qp_out, small = att_state
    qp_parts, late = reduce_weight(small, *qp_out)
    d_q_gain = late[0, :inner].reshape(heads, size)
    d_k_gain = late[0, inner : 2 * inner].reshape(heads, size)
    d_bias_one = late[1]
    both = late[2:4]
    both = both + swap(both, "tp", 1)
    both = both + swap(both, "tp", 2)
    d_bias_two = both[0]
    d_ln_gain = both[1] / ln_gain

    d_fc1, d_fc2 = fc[:width].astype(F32), fc[width:].astype(F32)
    d_qkv_t, d_proj = join(qp_parts, [(joined, width), (inner, width)])
    d_qkv = d_qkv_t.T

    def finish(begin, end, earlier):
        block = pl.BlockSpec((1, rows, width), lambda i: (begin + i, 0, 0))
        vector = pl.BlockSpec((width,), lambda i: (0,))
        first = pl.BlockSpec((2 * rows, width), lambda i: (0, 0))
        ins = keeps[3 * begin : 3 * end]
        return pl.pallas_call(
            functools.partial(final_kernel, end - begin),
            grid=(end - begin,),
            out_shape=[
                jax.ShapeDtypeStruct((images, rows, width), BF16),
                jax.ShapeDtypeStruct((images, rows, width), F32),
            ],
            in_specs=[block, block, vector, vector] + [first] * len(ins) + [ANY_SPEC] * len(earlier),
            out_specs=[block, block],
            input_output_aliases={4 + len(ins) + k: k for k in range(len(earlier))},
        )(tokens, d_out, ln_gain, b_fc2, *ins, *earlier)

    results = finish(0, images - 1, [])
    output, d_tokens = finish(images - 1, images, results)
    return (output, d_tokens, d_ln_gain, d_qkv, d_q_gain, d_k_gain, d_proj, d_fc1, d_bias_one, d_fc2, d_bias_two)


def solution(mesh):
    rows = P("dp", "tp", None)
    wide = P(None, "tp")
    tall = P("tp", None)
    return jax.shard_map(
        functools.partial(block, mesh.shape["dp"], mesh.shape["tp"]),
        mesh=mesh,
        in_specs=(rows, P("dp"), P(), wide, tall, tall, tall, wide, P("tp"), tall, P(), rows),
        out_specs=(rows, rows, P(), wide, tall, tall, tall, wide, P("tp"), tall, P()),
        check_vma=False,
    )
```
